32 devices in a mesh: dp: 8 (over z, core), mp: 4 (over y, x).
Axes of the slice: x: 2, y: 2, z: 4, core: 2. Of those that a mesh axis runs over, the one named last changes fastest.
Arguments:
- inputs: bfloat16 [1024, 32768], P('dp', 'mp'), may hold values from -6 to 6
- cotangent: bfloat16 [1024, 32768], P('dp', 'mp'), may hold values from -6 to 6
- first_weight: bfloat16 [128, 2, 256, 256], P('mp', None, 'dp'), may hold values from -0.25 to 0.25
- second_weight: bfloat16 [128, 2, 256, 256], P('mp', None, 'dp'), may hold values from -0.25 to 0.25
- orders: int32 [2, 256], replicated, may hold values from 0 to 255, each once within a row
Outputs:
- input_grad: bfloat16 [1024, 32768], P('dp', 'mp')
- first_grad: float32 [128, 2, 256, 256], P('mp', None, 'dp')
- second_grad: float32 [128, 2, 256, 256], P('mp', None, 'dp')
The draws below stay inside these ranges and needn't reach their ends.
Inputs may be any that keep to these rules, and one draw needn't show every extreme that they name: Each of the two rows of orders is a permutation of 0 to 255.
All inputs are finite; a program needn't handle non-finite values.
Results may differ from the reference program's by a relative error of at most 0.018.
Values may be sent and summed in bfloat16 or wider, within the bound.
A program may use at most 128 MiB of HBM per device.

```python
import math
import jax
import jax.numpy as jnp
import numpy as np
from jax import lax

H = 32768
B = 256
TOK_DEV = 128
TOKENS = 1024


def levels(rng, shape, shards, low, largest):
    loudness, own = 1.0, jax.random.fold_in(rng, 6)
    for dim, parts in shards:
        steps = jnp.exp(jax.random.uniform(jax.random.fold_in(own, dim), (parts,), jnp.float32, low / len(shards), largest / len(shards)))
        loudness = loudness * jnp.repeat(steps, shape[dim] // parts).reshape([-1 if axis == dim else 1 for axis in range(len(shape))])
    return loudness


def normal_values(key, shape, deviation, reach, pieces=(), held_as=jnp.bfloat16):
    array = deviation * jax.random.normal(key, shape, jnp.float32)
    if pieces:
        array = array * levels(key, shape, pieces, -0.22, 0.18)
    return jnp.clip(array, -reach, reach).astype(held_as)


def setup_inputs(seed: int = 0) -> dict:
    key_of = jax.random.split(jax.random.key(seed), 6)
    return {
        "inputs": normal_values(key_of[0], (TOKENS, H), 1.0, 6.0, ((0, 8), (1, 4))),
        "cotangent": normal_values(key_of[1], (TOKENS, H), 1.0, 6.0, ((0, 8), (1, 4))),
        "first_weight": normal_values(key_of[2], (H // B, 2, B, B), (2 * B) ** -0.5, 0.25, ((0, 4), (2, 8))),
        "second_weight": normal_values(key_of[3], (H // B, 2, B, B), (2 * B) ** -0.5, 0.25, ((0, 4), (2, 8))),
        "orders": jax.vmap(lambda own: jax.random.permutation(own, B))(jax.random.split(key_of[4], 2)).reshape((2, B)).astype(jnp.int32),
    }


def gelu_tanh(argument):
    return jax.nn.gelu(argument, approximate=True)

def rounded(argument):
    return lax.optimization_barrier(argument.astype(jnp.bfloat16)).astype(jnp.float32)

def inverse_order(order):
    length = order.shape[0]
    positions = jnp.arange(length, dtype=jnp.int32)
    matches = order[None, :] == positions[:, None]
    return lax.optimization_barrier(jnp.sum(jnp.where(matches, positions[None, :], 0), axis=1)).astype(jnp.int32)

def contract(left, right):
    return jnp.einsum('tnk,nkj->tnj', left, right)

def contract_back(left, right):
    return jnp.einsum('tnj,nkj->tnk', left, right)

def outer_sum(left, right):
    return jnp.einsum('tnk,tnj->nkj', left, right)

def reference(inputs, cotangent, first_weight, second_weight, orders):
    block_count = H // B
    block_index = np.arange(block_count)
    first_partner = (block_index + block_count // 2) % block_count
    quarter = block_count // 4
    second_partner = np.where(block_index // quarter % 2 == 0, block_index + quarter, block_index - quarter)
    order_first = orders[0]
    order_second = orders[1]
    inverse_first = inverse_order(order_first)
    inverse_second = inverse_order(order_second)
    first_float = first_weight.astype(jnp.float32)
    second_float = second_weight.astype(jnp.float32)
    grad_scale = 1.0 / math.sqrt(TOKENS)
    group_count = TOKENS // TOK_DEV
    group_inputs = inputs.reshape(group_count, TOK_DEV, block_count, B)
    group_cot = cotangent.reshape(group_count, TOK_DEV, block_count, B)

    def group_step(carry, group_pair):
        first_acc, second_acc = carry
        tokens_in = group_pair[0].astype(jnp.float32)
        tokens_cot = group_pair[1].astype(jnp.float32)
        partner_in = tokens_in[:, first_partner]
        pre_act = contract(tokens_in, first_float[:, 0]) + contract(partner_in[:, :, order_first], first_float[:, 1])
        saved_pre = rounded(pre_act)
        activated = rounded(gelu_tanh(pre_act))
        cross_two = rounded(contract_back(tokens_cot, second_float[:, 1])[:, second_partner][:, :, inverse_second])
        act_grad = contract_back(tokens_cot, second_float[:, 0]) + cross_two
        pullback = jax.vjp(gelu_tanh, saved_pre)[1]
        pre_grad = rounded(pullback(act_grad)[0])
        cross_one = rounded(contract_back(pre_grad, first_float[:, 1])[:, first_partner][:, :, inverse_first])
        input_grad = (contract_back(pre_grad, first_float[:, 0]) + cross_one).astype(jnp.bfloat16)
        first_part = jnp.stack([outer_sum(tokens_in, pre_grad), outer_sum(partner_in, pre_grad)[:, order_first, :]], axis=1)
        second_part = jnp.stack([outer_sum(activated, tokens_cot), outer_sum(activated[:, second_partner], tokens_cot)[:, order_second, :]], axis=1)
        first_acc = first_acc + rounded(first_part * grad_scale)
        second_acc = second_acc + rounded(second_part * grad_scale)
        return ((first_acc, second_acc), input_grad)
    zeros_grad = jnp.zeros((block_count, 2, B, B), jnp.float32)
    sums, grads_in = lax.scan(group_step, (zeros_grad, zeros_grad), (group_inputs, group_cot))
    input_grad = grads_in.reshape(TOKENS, H)
    return (input_grad, sums[0], sums[1])
```

```python
import functools
import math

import jax
import jax.numpy as jnp
from jax import lax
from jax.experimental import pallas as pl
from jax.experimental.pallas import tpu as pltpu
from jax.sharding import PartitionSpec as P

B = 256
MESH = pl.DeviceIdType.MESH
ANY = pl.BlockSpec(memory_space=pl.ANY)
NT = (((1,), (1,)), ((), ()))
TN = (((0,), (0,)), ((), ()))


class Plan:
    def __init__(self, dp, mp, local_blocks):
        self.dp, self.mp, self.nb = dp, mp, local_blocks
        self.low = mp // 4
        g = max(1, dp // 2)
        while local_blocks % (4 * g):
            g //= 2
        self.g, self.groups = g, dp // g
        self.nq = local_blocks // (4 * g)

    def here(self):
        d, m = lax.axis_index("dp"), lax.axis_index("mp")
        return d, d // self.g, d % self.g, m // self.low, m % self.low


def greet(plan, d, h, lo):
    barrier = pltpu.get_barrier_semaphore()
    others = 4 * plan.dp
    me = d * 4 + h
    for k in range(1, others):
        t = (me + k) % others
        pl.semaphore_signal(
            barrier, inc=1, device_id=(t // 4, (t % 4) * plan.low + lo), device_id_type=MESH
        )
    pl.semaphore_wait(barrier, others - 1)


def sweep(first, last, body):
    lax.fori_loop(first, last, lambda k, _: (body(k), None)[1], None)


def whole(plan, scale, order, x, c, w1, w2, igo, gfo, gso, xb, cb, w1b, w2b, ig, gf, gs, w1p, w2p, act, pre,
          ts, tr, ws, wr, ls, os, orr, gsem, gr, ol):
    d, gi, r, h, lo = plan.here()
    tok, rows, nq = x.shape[0], w1.shape[2], plan.nq
    n_t, n_w = 4 * plan.g, 4 * plan.dp
    me_o, me_w = r * 4 + h, d * 4 + h
    greet(plan, d, h, lo)

    def peer_of_group(t):
        return (gi * plan.g + t // 4, (t % 4) * plan.low + lo)

    def peer_of_all(t):
        return (t // 4, (t % 4) * plan.low + lo)

    def tokens_in(i, a, k):
        t = (me_o + 5 * k) % n_t
        src, dst = ((x, xb), (c, cb))[a]
        s = src.at[:, pl.ds(pl.multiple_of((t * nq + i) * B, B), B)]
        e = dst.at[i, h, pl.ds(pl.multiple_of(r * tok, tok), tok)]
        if isinstance(k, int) and k == 0:
            return pltpu.make_async_copy(s, e, ls.at[i, a])
        return pltpu.make_async_remote_copy(
            s, e, ts.at[i, a, k], tr.at[i, a, k], device_id=peer_of_group(t), device_id_type=MESH
        )

    def weights_in(i, a, k):
        t = (me_w + 11 * k) % n_w
        src, dst = ((w1, w1b), (w2, w2b))[a]
        o = ((t // 4) % plan.g) * 4 + t % 4
        s = src.at[o * nq + i]
        e = dst.at[i, h, :, pl.ds(pl.multiple_of(d * rows, rows), rows)]
        if isinstance(k, int) and k == 0:
            return pltpu.make_async_copy(s, e, ls.at[i, 2 + a])
        return pltpu.make_async_remote_copy(
            s, e, ws.at[i, a, k], wr.at[i, a, k], device_id=peer_of_all(t), device_id_type=MESH
        )

    def tokens_out(i, k):
        t = (me_o + 5 * k) % n_t
        s = ig.at[i, t % 4, pl.ds(pl.multiple_of((t // 4) * tok, tok), tok)]
        e = igo.at[:, pl.ds(pl.multiple_of((me_o * nq + i) * B, B), B)]
        if isinstance(k, int) and k == 0:
            return pltpu.make_async_copy(s, e, ol.at[i, 0])
        return pltpu.make_async_remote_copy(
            s, e, os.at[i, k], orr.at[i, k], device_id=peer_of_group(t), device_id_type=MESH
        )

    def grads_out(i, a, k):
        t = (me_w + 11 * k) % n_w
        src, dst = ((gf, gfo), (gs, gso))[a]
        s = src.at[i, t % 4, :, pl.ds(pl.multiple_of((t // 4) * rows, rows), rows)]
        e = dst.at[gi, me_o * nq + i]
        if isinstance(k, int) and k == 0:
            return pltpu.make_async_copy(s, e, ol.at[i, 1 + a])
        return pltpu.make_async_remote_copy(
            s, e, gsem.at[i, a, k], gr.at[i, a, k], device_id=peer_of_all(t), device_id_type=MESH
        )

    def all_in(i, act_on):
        def some_weights(k, first):
            for j in range(first, plan.groups):
                for a in (0, 1):
                    act_on(weights_in(i, a, plan.groups * k + j))

        def both(k):
            act_on(tokens_in(i, 0, k))
            some_weights(k, 0)
            act_on(tokens_in(i, 1, k))

        some_weights(0, 1)
        sweep(1, n_t, both)

    def all_out(i, act_on):
        def some_grads(k, first):
            for j in range(first, plan.groups):
                for a in (0, 1):
                    act_on(grads_out(i, a, plan.groups * k + j))

        def both(k):
            act_on(tokens_out(i, k))
            some_grads(k, 0)

        some_grads(0, 1)
        sweep(1, n_t, both)

    def own_in(i):
        return [f(i, a, 0) for f in (tokens_in, weights_in) for a in (0, 1)]

    def own_out(i):
        return [tokens_out(i, 0), grads_out(i, 0, 0), grads_out(i, 1, 0)]

    for i in range(nq):
        all_in(i, lambda copy: copy.start())
        for copy in own_in(i):
            copy.start()
    for i in range(nq):
        for copy in own_in(i):
            copy.wait()
        all_in(i, lambda copy: copy.wait_recv())
        factors(scale, order, xb.at[i], cb.at[i], w1b.at[i], w2b.at[i], ig.at[i], gf.at[i], gs.at[i], w1p, w2p, act, pre)
        all_out(i, lambda copy: copy.start())
        for copy in own_out(i):
            copy.start()
    for i in range(nq):
        all_in(i, lambda copy: copy.wait_send())
        for copy in own_out(i):
            copy.wait()
        all_out(i, lambda copy: copy.wait())


class Lanes:
    def __init__(self, dp, mp, local_blocks):
        self.nc = nc = dp // 4
        self.low = mp // 4
        self.ng = local_blocks // (4 * nc) if nc else 0
        self.fits = dp % 4 == 0 and mp % 4 == 0 and self.ng > 0 and local_blocks % (4 * nc) == 0


def lanes(plan, scale, order, x, c, w1, w2, igo, gfo, gso, xb, cb, w1b, w2b, ig, gf, gs, gif, gis, w1p, w2p, act, pre,
          tin, win, wout, wrel, gin, done, st, sw, sd, sr, so, su, si, sg, sf):
    nc, low, ng = plan.nc, plan.low, plan.ng
    tok, rows = x.shape[0], w1.shape[2]
    d, m = lax.axis_index("dp"), lax.axis_index("mp")
    h, lo = m // low, m % low
    quarter, side, core, slot = d // nc, d // (2 * nc), d % nc, d % (2 * nc)
    inner = jnp.logical_or(quarter == 1, quarter == 2)
    outer = jnp.logical_not(inner)
    base, other, far = nc + side * nc, 2 * nc - side * nc, 3 * nc * side
    first, me, us = 2 * nc * side, core * 4 + h, slot * 4 + h
    n_s, n_o = 4 * nc, 8 * nc
    X, W, G, GI, GO = (x, c), (w1, w2), (gf, gs), (gif, gis), (gfo, gso)
    XB, WB = (xb, cb), (w1b, w2b)

    def mp_of(hh):
        return hh * low + lo

    def span(start, size):
        return pl.ds(pl.multiple_of(start * size, size), size)

    def put(src, dst, ssem, rsem, dev):
        return pltpu.make_async_remote_copy(src, dst, ssem, rsem, device_id=dev, device_id_type=MESH)

    def arrived(ref, sem):
        pltpu.make_async_copy(ref, ref, sem).wait()

    barrier = pltpu.get_barrier_semaphore()

    def hello(dev):
        pl.semaphore_signal(barrier, inc=1, device_id=dev, device_id_type=MESH)

    @pl.when(inner)
    def _():
        for k in range(1, n_o):
            u = (us + k) % n_o
            hello((first + u // 4, mp_of(u % 4)))
        for cs in range(nc):
            hello((other + cs, m))
        pl.semaphore_wait(barrier, n_o - 1 + nc)

    @pl.when(outer)
    def _():
        for k in range(n_s):
            t = (me + k) % n_s
            hello((base + t // 4, mp_of(t % 4)))
        for kh in range(1, 4):
            hello((d, mp_of((h + kh) % 4)))
        pl.semaphore_wait(barrier, n_s + 3)

    def block_of(a, t, i):
        return W[a].at[t * ng + i]

    def columns_of(a, t, i):
        return X[a].at[:, span(t * ng + i, B)]

    def own_w(i, a, k):
        t = (me + k) % n_s
        e = WB[a].at[i, h, :, span(d, rows)]
        if isinstance(k, int) and k == 0:
            return pltpu.make_async_copy(block_of(a, t, i), e, win.at[i, a, h])
        return put(block_of(a, t, i), e, sw.at[i, a, k], win.at[i, a, h], (base + t // 4, mp_of(t % 4)))

    def cross_w(i, a, cs):
        e = WB[a].at[i, h, :, span(d, rows)]
        return put(block_of(a, cs * 4 + h, i), e, sd.at[i, a, cs], wrel.at[i, a], (other + cs, m))

    def own_t(i, a, k):
        t = (me + k) % n_s
        e = XB[a].at[i, h, span(slot, tok)]
        if isinstance(k, int) and k == 0:
            return pltpu.make_async_copy(columns_of(a, t, i), e, tin.at[i, a])
        return put(columns_of(a, t, i), e, st.at[i, a, k], tin.at[i, a], (base + t // 4, mp_of(t % 4)))

    def plane_w(i, a, cs, kh):
        hh = (h + kh) % 4
        s, e = block_of(a, cs * 4 + hh, i), WB[a].at[i, h, :, span(cs, rows)]
        if kh == 0:
            return pltpu.make_async_copy(s, e, wout.at[i, a])
        return put(s, e, sw.at[i, a, cs * 4 + kh], wout.at[i, a], (d, mp_of(hh)))

    def plane_t(i, a, cs, kh):
        hh = (h + kh) % 4
        s, e = columns_of(a, cs * 4 + hh, i), XB[a].at[i, h, span(cs, tok)]
        if kh == 0:
            return pltpu.make_async_copy(s, e, tin.at[i, a])
        return put(s, e, st.at[i, a, cs * 4 + kh], tin.at[i, a], (d, mp_of(hh)))

    def up_w(i, a, cs):
        s, e = WB[a].at[i, :, :, span(cs, rows)], WB[a].at[i, :, :, span(d, rows)]
        return put(s, e, su.at[i, a, cs], wout.at[i, a], (base + cs, m))

    def up_t(i, a, cs):
        s, e = XB[a].at[i, :, span(cs, tok)], XB[a].at[i, :, span(slot, tok)]
        return put(s, e, su.at[i, 2 + a, cs], tin.at[i, a], (base + cs, m))

    def relay_in(i, a, kh):
        s = WB[a].at[i, (h + kh) % 4, :, span(base // nc, nc * rows)]
        return put(s, s, sr.at[i, a, kh], wrel.at[i, a], (other + core, m))

    def relay_out(i, a):
        s = WB[a].at[i, :, :, span(far // nc, nc * rows)]
        return put(s, s, so.at[i, a], wrel.at[i, a], (other + core, m))

    def tokens_out(i, k):
        u = (us + k) % n_o
        s, e = ig.at[i, u % 4, span(u // 4, tok)], igo.at[:, span(me * ng + i, B)]
        if isinstance(k, int) and k == 0:
            return pltpu.make_async_copy(s, e, done.at[0])
        return put(s, e, si.at[i, k], done.at[0], (first + u // 4, mp_of(u % 4)))

    def partial(i, a, kh):
        hh = (h + kh) % 4
        s = G[a].at[i, hh, :, span(1 - side, 2 * nc * rows)]
        return put(s, GI[a].at[i, hh], sg.at[i, a, kh], gin.at[i, a, kh], (other + core, m))

    def grads_out(i, a, kh, k):
        hh, r = (h + kh) % 4, (slot + k) % (2 * nc)
        s, e = GI[a].at[i, hh, :, span(r, rows)], GO[a].at[me * ng + i]
        if kh == 0 and k == 0:
            return pltpu.make_async_copy(s, e, done.at[1 + a])
        return put(s, e, sf.at[i, a, kh, k], done.at[1 + a], (first + r, mp_of(hh)))

    def both(f, *at):
        return [f(at[0], a, *at[1:]) for a in (0, 1)]

    def begin(copies):
        for copy in copies:
            copy.start()

    def combine(i):
        for kh in range(4):
            hh = (h + kh) % 4
            for a in (0, 1):
                arrived(GI[a].at[i, hh], gin.at[i, a, kh])
                mine = G[a][i, hh, :, span(side, 2 * nc * rows)].astype(jnp.float32)
                GI[a][i, hh] = (mine + GI[a][i, hh].astype(jnp.float32)).astype(jnp.bfloat16)
                begin([grads_out(i, a, kh, k) for k in range(2 * nc)])

    @pl.when(inner)
    def _():
        for i in range(ng):
            for cs in range(nc):
                begin(both(cross_w, i, cs))
        for i in range(ng):
            sweep(1, n_s, lambda k: begin(both(own_w, i, k)))
            begin(both(own_w, i, 0))
        for i in range(ng):
            sweep(1, n_s, lambda k: begin(both(own_t, i, k)))
            begin(both(own_t, i, 0))
        for i in range(ng):
            for kh in range(4):
                for a in (0, 1):
                    hh = (h + kh) % 4
                    arrived(WB[a].at[i, hh, :, span(base // nc, nc * rows)], win.at[i, a, hh])
                    if kh:
                        relay_in(i, a, kh).start()
        for i in range(ng):
            for a in (0, 1):
                arrived(WB[a].at[i, :, :, span(far // nc, nc * rows)], wout.at[i, a])
                relay_out(i, a).start()
        for i in range(ng):
            for a in (0, 1):
                arrived(WB[a].at[i, :, :, span(1 - side, 2 * nc * rows)], wrel.at[i, a])
                arrived(XB[a].at[i], tin.at[i, a])
            factors(scale, order, xb.at[i], cb.at[i], w1b.at[i], w2b.at[i], ig.at[i], gf.at[i], gs.at[i], w1p, w2p, act, pre)
            for kh in range(4):
                begin(both(partial, i, kh))
            sweep(1, n_o, lambda k: tokens_out(i, k).start())
            tokens_out(i, 0).start()
            if i >= 2:
                combine(i - 2)
        for i in range(max(0, ng - 2), ng):
            combine(i)
        for i in range(ng):
            for a in (0, 1):
                sweep(1, n_s, lambda k: own_w(i, a, k).wait_send())
                sweep(1, n_s, lambda k: own_t(i, a, k).wait_send())
                for cs in range(nc):
                    cross_w(i, a, cs).wait_send()
                for kh in range(1, 4):
                    relay_in(i, a, kh).wait_send()
                relay_out(i, a).wait_send()
                for kh in range(4):
                    partial(i, a, kh).wait_send()
                    for k in range(2 * nc):
                        if kh or k:
                            grads_out(i, a, kh, k).wait_send()
            sweep(1, n_o, lambda k: tokens_out(i, k).wait_send())

    @pl.when(outer)
    def _():
        for i in range(ng):
            for kh in (1, 2, 3, 0):
                for cs in range(nc):
                    begin(both(plane_w, i, cs, kh))
        for i in range(ng):
            for kh in (1, 2, 3, 0):
                for cs in range(nc):
                    begin(both(plane_t, i, cs, kh))
        for i in range(ng):
            for a in (0, 1):
                arrived(WB[a].at[i, :, :, span(0, nc * rows)], wout.at[i, a])
                begin([up_w(i, a, cs) for cs in range(nc)])
        for i in range(ng):
            for a in (0, 1):
                arrived(XB[a].at[i, :, span(0, nc * tok)], tin.at[i, a])
                begin([up_t(i, a, cs) for cs in range(nc)])
        for i in range(ng):
            for a in (0, 1):
                for cs in range(nc):
                    for kh in range(1, 4):
                        plane_w(i, a, cs, kh).wait_send()
                        plane_t(i, a, cs, kh).wait_send()
                    up_w(i, a, cs).wait_send()
                    up_t(i, a, cs).wait_send()

    arrived(igo, done.at[0])
    arrived(gfo, done.at[1])
    arrived(gso, done.at[2])


def by_lanes(plan, inputs, cotangent, first_weight, second_weight, orders):
    tok, width = inputs.shape
    rows = first_weight.shape[2]
    nc, ng, bf = plan.nc, plan.ng, jnp.bfloat16
    scale = 1.0 / math.sqrt(tok * 4 * nc)
    dma = pltpu.SemaphoreType.DMA
    toks = pltpu.VMEM((ng, 4, 2 * nc * tok, B), bf)
    mats = pltpu.VMEM((ng, 4, 2, B, B), bf)
    half = pltpu.VMEM((ng, 4, 2, 2 * nc * rows, B), bf)
    part = jax.ShapeDtypeStruct(first_weight.shape, bf)
    input_grad, first, second = pl.pallas_call(
        functools.partial(lanes, plan, scale),
        out_shape=(jax.ShapeDtypeStruct((tok, width), bf), part, part),
        in_specs=[pl.BlockSpec(memory_space=pltpu.VMEM)] + [ANY] * 4,
        out_specs=(ANY,) * 3,
        scratch_shapes=[toks, toks, mats, mats, toks, mats, mats, half, half]
        + [pltpu.VMEM((4, B, B), bf)] * 2
        + [pltpu.VMEM((4, 2 * nc * tok, B), bf)] * 2
        + [dma((ng, 2)), dma((ng, 2, 4)), dma((ng, 2)), dma((ng, 2)), dma((ng, 2, 4)), dma((3,))]
        + [dma((ng, 2, 4 * nc)), dma((ng, 2, 4 * nc)), dma((ng, 2, nc)), dma((ng, 2, 4)), dma((ng, 2)), dma((ng, 4, nc))]
        + [dma((ng, 8 * nc)), dma((ng, 2, 4)), dma((ng, 2, 4, 2 * nc))],
        compiler_params=pltpu.CompilerParams(
            collective_id=0, has_side_effects=True, vmem_limit_bytes=58 * 2**20
        ),
        name="lanes",
    )(orders, inputs, cotangent, first_weight, second_weight)
    return input_grad, first.astype(jnp.float32), second.astype(jnp.float32)


def dot(left, right, dims=(((1,), (0,)), ((), ()))):
    return lax.dot_general(left, right, dims, preferred_element_type=jnp.float32)


def factors(scale, order, x, c, w1, w2, ig, gf, gs, w1p, w2p, act, pre):
    bf = jnp.bfloat16
    place = lax.broadcasted_iota(jnp.int32, (B, B), 0)
    spread_one = (place == order[0:1, :]).astype(jnp.float32).astype(bf)
    spread_two = (place == order[1:2, :]).astype(jnp.float32).astype(bf)
    root = math.sqrt(2.0 / math.pi)
    for h in range(4):
        w1p[h] = dot(spread_one, w1[h, 1]).astype(bf)
        w2p[h] = dot(spread_two, w2[h, 1]).astype(bf)
    for h in range(4):
        p, q = h ^ 2, h ^ 1
        v = dot(x[h], w1[h, 0]) + dot(x[p], w1p[h])
        up = dot(c[h], w2[h, 0], NT) + dot(c[q], w2p[q], NT)
        v2 = v * v
        t = jnp.tanh(root * v * (1.0 + 0.044715 * v2))
        half = 0.5 + 0.5 * t
        act[h] = (v * half).astype(bf)
        slope = half + (0.5 * root) * v * (1.0 - t * t) * (1.0 + (3 * 0.044715) * v2)
        pre[h] = (up * slope).astype(bf)
    for h in range(4):
        p, q = h ^ 2, h ^ 1
        ig[h] = (dot(pre[h], w1[h, 0], NT) + dot(pre[p], w1p[p], NT)).astype(bf)
        gf[h, 0] = (dot(x[h], pre[h], TN) * scale).astype(bf)
        cross = (dot(x[p], pre[h], TN) * scale).astype(bf)
        gf[h, 1] = dot(spread_one, cross, TN).astype(bf)
        gs[h, 0] = (dot(act[h], c[h], TN) * scale).astype(bf)
        cross = (dot(act[q], c[h], TN) * scale).astype(bf)
        gs[h, 1] = dot(spread_two, cross, TN).astype(bf)


def shards(plan, inputs, cotangent, first_weight, second_weight, orders):
    tok, width = inputs.shape
    rows = first_weight.shape[2]
    bf = jnp.bfloat16
    all_tok = plan.g * tok
    nq = plan.nq
    scale = 1.0 / math.sqrt(tok * plan.dp)
    dma = pltpu.SemaphoreType.DMA
    n_t, n_w = 4 * plan.g, 4 * plan.dp
    toks = pltpu.VMEM((nq, 4, all_tok, B), bf)
    mats = pltpu.VMEM((nq, 4, 2, B, B), bf)
    part = jax.ShapeDtypeStruct((plan.groups, plan.nb, 2, rows, B), bf)
    input_grad, first, second = pl.pallas_call(
        functools.partial(whole, plan, scale),
        out_shape=(jax.ShapeDtypeStruct((tok, width), bf), part, part),
        in_specs=[pl.BlockSpec(memory_space=pltpu.VMEM)] + [ANY] * 4,
        out_specs=(ANY,) * 3,
        scratch_shapes=[toks, toks, mats, mats, toks, mats, mats]
        + [pltpu.VMEM((4, B, B), bf)] * 2
        + [pltpu.VMEM((4, all_tok, B), bf)] * 2
        + [dma((nq, 2, n_t)), dma((nq, 2, n_t)), dma((nq, 2, n_w)), dma((nq, 2, n_w)), dma((nq, 4))]
        + [dma((nq, n_t)), dma((nq, n_t)), dma((nq, 2, n_w)), dma((nq, 2, n_w)), dma((nq, 3))],
        compiler_params=pltpu.CompilerParams(
            collective_id=0, has_side_effects=True, vmem_limit_bytes=56 * 2**20
        ),
        name="whole",
    )(orders, inputs, cotangent, first_weight, second_weight)
    total = lambda parts: jnp.sum(parts.astype(jnp.float32), axis=0)
    return input_grad, total(first), total(second)


def solution(mesh):
    in_specs = (
        P("dp", "mp"),
        P("dp", "mp"),
        P("mp", None, "dp", None),
        P("mp", None, "dp", None),
        P(),
    )
    out_specs = (P("dp", "mp"), P("mp", None, "dp", None), P("mp", None, "dp", None))

    def body(inputs, *rest):
        sizes = mesh.shape["dp"], mesh.shape["mp"], inputs.shape[1] // B
        plan = Lanes(*sizes)
        if plan.fits:
            return by_lanes(plan, inputs, *rest)
        plan = Plan(*sizes)
        return shards(plan, inputs, *rest)

    return jax.shard_map(body, mesh=mesh, in_specs=in_specs, out_specs=out_specs, check_vma=False)
```

```python
import functools
import math

import jax
import jax.numpy as jnp
from jax import lax
from jax.experimental import pallas as pl
from jax.experimental.pallas import tpu as pltpu
from jax.sharding import PartitionSpec as P

B = 256
MESH = pl.DeviceIdType.MESH
ANY = pl.BlockSpec(memory_space=pl.ANY)
NT = (((1,), (1,)), ((), ()))
TN = (((0,), (0,)), ((), ()))


class Plan:
    def __init__(self, dp, mp, local_blocks):
        self.dp, self.mp, self.nb = dp, mp, local_blocks
        self.low = mp // 4
        g = max(1, dp // 2)
        while local_blocks % (4 * g):
            g //= 2
        self.g, self.groups = g, dp // g
        self.nq = local_blocks // (4 * g)

    def here(self):
        d, m = lax.axis_index("dp"), lax.axis_index("mp")
        return d, d // self.g, d % self.g, m // self.low, m % self.low


def greet(plan, d, h, lo):
    barrier = pltpu.get_barrier_semaphore()
    others = 4 * plan.dp
    me = d * 4 + h
    for k in range(1, others):
        t = (me + k) % others
        pl.semaphore_signal(
            barrier, inc=1, device_id=(t // 4, (t % 4) * plan.low + lo), device_id_type=MESH
        )
    pl.semaphore_wait(barrier, others - 1)


def sweep(first, last, body):
    lax.fori_loop(first, last, lambda k, _: (body(k), None)[1], None)


def whole(plan, scale, order, x, c, w1, w2, igo, gfo, gso, xb, cb, w1b, w2b, ig, gf, gs, w1p, w2p, act, pre,
          ts, tr, ws, wr, ls, os, orr, gsem, gr, ol):
    d, gi, r, h, lo = plan.here()
    tok, rows, nq = x.shape[0], w1.shape[2], plan.nq
    n_t, n_w = 4 * plan.g, 4 * plan.dp
    me_o, me_w = r * 4 + h, d * 4 + h
    greet(plan, d, h, lo)

    def peer_of_group(t):
        return (gi * plan.g + t // 4, (t % 4) * plan.low + lo)

    def peer_of_all(t):
        return (t // 4, (t % 4) * plan.low + lo)

    def tokens_in(i, a, k):
        t = (me_o + 5 * k) % n_t
        src, dst = ((x, xb), (c, cb))[a]
        s = src.at[:, pl.ds(pl.multiple_of((t * nq + i) * B, B), B)]
        e = dst.at[i, h, pl.ds(pl.multiple_of(r * tok, tok), tok)]
        if isinstance(k, int) and k == 0:
            return pltpu.make_async_copy(s, e, ls.at[i, a])
        return pltpu.make_async_remote_copy(
            s, e, ts.at[i, a, k], tr.at[i, a, k], device_id=peer_of_group(t), device_id_type=MESH
        )

    def weights_in(i, a, k):
        t = (me_w + 11 * k) % n_w
        src, dst = ((w1, w1b), (w2, w2b))[a]
        o = ((t // 4) % plan.g) * 4 + t % 4
        s = src.at[o * nq + i]
        e = dst.at[i, h, :, pl.ds(pl.multiple_of(d * rows, rows), rows)]
        if isinstance(k, int) and k == 0:
            return pltpu.make_async_copy(s, e, ls.at[i, 2 + a])
        return pltpu.make_async_remote_copy(
            s, e, ws.at[i, a, k], wr.at[i, a, k], device_id=peer_of_all(t), device_id_type=MESH
        )

    def tokens_out(i, k):
        t = (me_o + 5 * k) % n_t
        s = ig.at[i, t % 4, pl.ds(pl.multiple_of((t // 4) * tok, tok), tok)]
        e = igo.at[:, pl.ds(pl.multiple_of((me_o * nq + i) * B, B), B)]
        if isinstance(k, int) and k == 0:
            return pltpu.make_async_copy(s, e, ol.at[i, 0])
        return pltpu.make_async_remote_copy(
            s, e, os.at[i, k], orr.at[i, k], device_id=peer_of_group(t), device_id_type=MESH
        )

    def grads_out(i, a, k):
        t = (me_w + 11 * k) % n_w
        src, dst = ((gf, gfo), (gs, gso))[a]
        s = src.at[i, t % 4, :, pl.ds(pl.multiple_of((t // 4) * rows, rows), rows)]
        e = dst.at[gi, me_o * nq + i]
        if isinstance(k, int) and k == 0:
            return pltpu.make_async_copy(s, e, ol.at[i, 1 + a])
        return pltpu.make_async_remote_copy(
            s, e, gsem.at[i, a, k], gr.at[i, a, k], device_id=peer_of_all(t), device_id_type=MESH
        )

    def all_in(i, act_on):
        def some_weights(k, first):
            for j in range(first, plan.groups):
                for a in (0, 1):
                    act_on(weights_in(i, a, plan.groups * k + j))

        def both(k):
            act_on(tokens_in(i, 0, k))
            some_weights(k, 0)
            act_on(tokens_in(i, 1, k))

        some_weights(0, 1)
        sweep(1, n_t, both)

    def all_out(i, act_on):
        def some_grads(k, first):
            for j in range(first, plan.groups):
                for a in (0, 1):
                    act_on(grads_out(i, a, plan.groups * k + j))

        def both(k):
            act_on(tokens_out(i, k))
            some_grads(k, 0)

        some_grads(0, 1)
        sweep(1, n_t, both)

    def own_in(i):
        return [f(i, a, 0) for f in (tokens_in, weights_in) for a in (0, 1)]

    def own_out(i):
        return [tokens_out(i, 0), grads_out(i, 0, 0), grads_out(i, 1, 0)]

    for i in range(nq):
        all_in(i, lambda copy: copy.start())
        for copy in own_in(i):
            copy.start()
    for i in range(nq):
        for copy in own_in(i):
            copy.wait()
        all_in(i, lambda copy: copy.wait_recv())
        factors(scale, order, xb.at[i], cb.at[i], w1b.at[i], w2b.at[i], ig.at[i], gf.at[i], gs.at[i], w1p, w2p, act, pre)
        all_out(i, lambda copy: copy.start())
        for copy in own_out(i):
            copy.start()
    for i in range(nq):
        all_in(i, lambda copy: copy.wait_send())
        for copy in own_out(i):
            copy.wait()
        all_out(i, lambda copy: copy.wait())


class Lanes:
    def __init__(self, dp, mp, local_blocks):
        self.nc = nc = dp // 4
        self.low = mp // 4
        self.ng = local_blocks // (4 * nc) if nc else 0
        self.fits = dp % 4 == 0 and mp % 4 == 0 and self.ng > 0 and local_blocks % (4 * nc) == 0


def lanes(plan, scale, order, x, c, w1, w2, igo, gfo, gso, xb, cb, w1b, w2b, ig, gf, gs, gif, gis, w1p, w2p, act, pre,
          tin, win, wout, wrel, gin, done, st, sw, sd, sr, so, su, si, sg, sf):
    nc, low, ng = plan.nc, plan.low, plan.ng
    tok, rows = x.shape[0], w1.shape[2]
    d, m = lax.axis_index("dp"), lax.axis_index("mp")
    h, lo = m // low, m % low
    quarter, side, core, slot = d // nc, d // (2 * nc), d % nc, d % (2 * nc)
    inner = jnp.logical_or(quarter == 1, quarter == 2)
    outer = jnp.logical_not(inner)
    base, other, far = nc + side * nc, 2 * nc - side * nc, 3 * nc * side
    first, me, us = 2 * nc * side, core * 4 + h, slot * 4 + h
    n_s, n_o = 4 * nc, 8 * nc
    X, W, G, GI, GO = (x, c), (w1, w2), (gf, gs), (gif, gis), (gfo, gso)
    XB, WB = (xb, cb), (w1b, w2b)

    def mp_of(hh):
        return hh * low + lo

    def span(start, size):
        return pl.ds(pl.multiple_of(start * size, size), size)

    def put(src, dst, ssem, rsem, dev):
        return pltpu.make_async_remote_copy(src, dst, ssem, rsem, device_id=dev, device_id_type=MESH)

    def arrived(ref, sem):
        pltpu.make_async_copy(ref, ref, sem).wait()

    barrier = pltpu.get_barrier_semaphore()

    def hello(dev):
        pl.semaphore_signal(barrier, inc=1, device_id=dev, device_id_type=MESH)

    @pl.when(inner)
    def _():
        for k in range(1, n_o):
            u = (us + k) % n_o
            hello((first + u // 4, mp_of(u % 4)))
        for cs in range(nc):
            hello((other + cs, m))
        pl.semaphore_wait(barrier, n_o - 1 + nc)

    @pl.when(outer)
    def _():
        for k in range(n_s):
            t = (me + k) % n_s
            hello((base + t // 4, mp_of(t % 4)))
        for kh in range(1, 4):
            hello((d, mp_of((h + kh) % 4)))
        pl.semaphore_wait(barrier, n_s + 3)

    def block_of(a, t, i):
        return W[a].at[t * ng + i]

    def columns_of(a, t, i):
        return X[a].at[:, span(t * ng + i, B)]

    def own_w(i, a, k):
        t = (me + k) % n_s
        e = WB[a].at[i, h, :, span(d, rows)]
        if isinstance(k, int) and k == 0:
            return pltpu.make_async_copy(block_of(a, t, i), e, win.at[i, a, h])
        return put(block_of(a, t, i), e, sw.at[i, a, k], win.at[i, a, h], (base + t // 4, mp_of(t % 4)))

    def cross_w(i, a, cs):
        e = WB[a].at[i, h, :, span(d, rows)]
        return put(block_of(a, cs * 4 + h, i), e, sd.at[i, a, cs], wrel.at[i, a], (other + cs, m))

    def own_t(i, a, k):
        t = (me + k) % n_s
        e = XB[a].at[i, h, span(slot, tok)]
        if isinstance(k, int) and k == 0:
            return pltpu.make_async_copy(columns_of(a, t, i), e, tin.at[i, a])
        return put(columns_of(a, t, i), e, st.at[i, a, k], tin.at[i, a], (base + t // 4, mp_of(t % 4)))

    def plane_w(i, a, cs, kh):
        hh = (h + kh) % 4
        s, e = block_of(a, cs * 4 + hh, i), WB[a].at[i, h, :, span(cs, rows)]
        if kh == 0:
            return pltpu.make_async_copy(s, e, wout.at[i, a])
        return put(s, e, sw.at[i, a, cs * 4 + kh], wout.at[i, a], (d, mp_of(hh)))

    def plane_t(i, a, cs, kh):
        hh = (h + kh) % 4
        s, e = columns_of(a, cs * 4 + hh, i), XB[a].at[i, h, span(cs, tok)]
        if kh == 0:
            return pltpu.make_async_copy(s, e, tin.at[i, a])
        return put(s, e, st.at[i, a, cs * 4 + kh], tin.at[i, a], (d, mp_of(hh)))

    def up_w(i, a, cs):
        s, e = WB[a].at[i, :, :, span(cs, rows)], WB[a].at[i, :, :, span(d, rows)]
        return put(s, e, su.at[i, a, cs], wout.at[i, a], (base + cs, m))

    def up_t(i, a, cs):
        s, e = XB[a].at[i, :, span(cs, tok)], XB[a].at[i, :, span(slot, tok)]
        return put(s, e, su.at[i, 2 + a, cs], tin.at[i, a], (base + cs, m))

    def relay_in(i, a, kh):
        s = WB[a].at[i, (h + kh) % 4, :, span(base // nc, nc * rows)]
        return put(s, s, sr.at[i, a, kh], wrel.at[i, a], (other + core, m))

    def relay_out(i, a):
        s = WB[a].at[i, :, :, span(far // nc, nc * rows)]
        return put(s, s, so.at[i, a], wrel.at[i, a], (other + core, m))

    def tokens_out(i, k):
        u = (us + k) % n_o
        s, e = ig.at[i, u % 4, span(u // 4, tok)], igo.at[:, span(me * ng + i, B)]
        if isinstance(k, int) and k == 0:
            return pltpu.make_async_copy(s, e, done.at[0])
        return put(s, e, si.at[i, k], done.at[0], (first + u // 4, mp_of(u % 4)))

    def partial(i, a, kh, near):
        hh, theirs = (h + kh) % 4, other // nc if near else 3 - far // nc
        s = G[a].at[i, hh, :, span(theirs, nc * rows)]
        return put(s, GI[a].at[i, hh, near], sg.at[i, a, kh, near], gin.at[i, a, kh, near], (other + core, m))

    def grads_out(i, a, kh, near, k):
        hh, cs = (h + kh) % 4, (core + k) % nc
        s, e = GI[a].at[i, hh, near, :, span(cs, rows)], GO[a].at[me * ng + i]
        if near and kh == 0 and k == 0:
            return pltpu.make_async_copy(s, e, done.at[1 + a])
        return put(s, e, sf.at[i, a, kh, near, k], done.at[1 + a], ((base if near else far) + cs, mp_of(hh)))

    parts = [(a, kh, near) for near in (0, 1) for kh in (1, 2, 3, 0) for a in (0, 1)]

    def both(f, *at):
        return [f(at[0], a, *at[1:]) for a in (0, 1)]

    def begin(copies):
        for copy in copies:
            copy.start()

    def combine(i):
        for a, kh, near in parts:
            hh = (h + kh) % 4
            arrived(GI[a].at[i, hh, near], gin.at[i, a, kh, near])
            ours = base // nc if near else far // nc
            mine = G[a][i, hh, :, span(ours, nc * rows)].astype(jnp.float32)
            GI[a][i, hh, near] = (mine + GI[a][i, hh, near].astype(jnp.float32)).astype(jnp.bfloat16)
            begin([grads_out(i, a, kh, near, k) for k in range(nc)])

    @pl.when(inner)
    def _():
        for i in range(ng):
            for cs in range(nc):
                begin(both(cross_w, i, cs))
        for i in range(ng):
            sweep(1, n_s, lambda k: begin(both(own_w, i, k)))
            begin(both(own_w, i, 0))
        for i in range(ng):
            sweep(1, n_s, lambda k: begin(both(own_t, i, k)))
            begin(both(own_t, i, 0))
        for i in range(ng):
            for kh in range(4):
                for a in (0, 1):
                    hh = (h + kh) % 4
                    arrived(WB[a].at[i, hh, :, span(base // nc, nc * rows)], win.at[i, a, hh])
                    if kh:
                        relay_in(i, a, kh).start()
        for i in range(ng):
            for a in (0, 1):
                arrived(WB[a].at[i, :, :, span(far // nc, nc * rows)], wout.at[i, a])
                relay_out(i, a).start()
        for i in range(ng):
            for a in (0, 1):
                arrived(WB[a].at[i, :, :, span(1 - side, 2 * nc * rows)], wrel.at[i, a])
                arrived(XB[a].at[i], tin.at[i, a])
            factors(scale, order, xb.at[i], cb.at[i], w1b.at[i], w2b.at[i], ig.at[i], gf.at[i], gs.at[i], w1p, w2p, act, pre)
            begin([partial(i, *at) for at in parts])
            sweep(1, n_o, lambda k: tokens_out(i, k).start())
            tokens_out(i, 0).start()
            if i >= 1:
                combine(i - 1)
        combine(ng - 1)
        for i in range(ng):
            for a in (0, 1):
                sweep(1, n_s, lambda k: own_w(i, a, k).wait_send())
                sweep(1, n_s, lambda k: own_t(i, a, k).wait_send())
                for cs in range(nc):
                    cross_w(i, a, cs).wait_send()
                for kh in range(1, 4):
                    relay_in(i, a, kh).wait_send()
                relay_out(i, a).wait_send()
            sweep(1, n_o, lambda k: tokens_out(i, k).wait_send())
            for a, kh, near in parts:
                partial(i, a, kh, near).wait_send()
                for k in range(nc):
                    if not near or kh or k:
                        grads_out(i, a, kh, near, k).wait_send()

    @pl.when(outer)
    def _():
        for i in range(ng):
            for kh in (1, 2, 3, 0):
                for cs in range(nc):
                    begin(both(plane_w, i, cs, kh))
        for i in range(ng):
            for kh in (1, 2, 3, 0):
                for cs in range(nc):
                    begin(both(plane_t, i, cs, kh))
        for i in range(ng):
            for a in (0, 1):
                arrived(WB[a].at[i, :, :, span(0, nc * rows)], wout.at[i, a])
                begin([up_w(i, a, cs) for cs in range(nc)])
        for i in range(ng):
            for a in (0, 1):
                arrived(XB[a].at[i, :, span(0, nc * tok)], tin.at[i, a])
                begin([up_t(i, a, cs) for cs in range(nc)])
        for i in range(ng):
            for a in (0, 1):
                for cs in range(nc):
                    for kh in range(1, 4):
                        plane_w(i, a, cs, kh).wait_send()
                        plane_t(i, a, cs, kh).wait_send()
                    up_w(i, a, cs).wait_send()
                    up_t(i, a, cs).wait_send()

    arrived(igo, done.at[0])
    arrived(gfo, done.at[1])
    arrived(gso, done.at[2])


def by_lanes(plan, inputs, cotangent, first_weight, second_weight, orders):
    tok, width = inputs.shape
    rows = first_weight.shape[2]
    nc, ng, bf = plan.nc, plan.ng, jnp.bfloat16
    scale = 1.0 / math.sqrt(tok * 4 * nc)
    dma = pltpu.SemaphoreType.DMA
    toks = pltpu.VMEM((ng, 4, 2 * nc * tok, B), bf)
    mats = pltpu.VMEM((ng, 4, 2, B, B), bf)
    half = pltpu.VMEM((ng, 4, 2, 2, nc * rows, B), bf)
    part = jax.ShapeDtypeStruct(first_weight.shape, bf)
    input_grad, first, second = pl.pallas_call(
        functools.partial(lanes, plan, scale),
        out_shape=(jax.ShapeDtypeStruct((tok, width), bf), part, part),
        in_specs=[pl.BlockSpec(memory_space=pltpu.VMEM)] + [ANY] * 4,
        out_specs=(ANY,) * 3,
        scratch_shapes=[toks, toks, mats, mats, toks, mats, mats, half, half]
        + [pltpu.VMEM((4, B, B), bf)] * 2
        + [pltpu.VMEM((4, 2 * nc * tok, B), bf)] * 2
        + [dma((ng, 2)), dma((ng, 2, 4)), dma((ng, 2)), dma((ng, 2)), dma((ng, 2, 4, 2)), dma((3,))]
        + [dma((ng, 2, 4 * nc)), dma((ng, 2, 4 * nc)), dma((ng, 2, nc)), dma((ng, 2, 4)), dma((ng, 2)), dma((ng, 4, nc))]
        + [dma((ng, 8 * nc)), dma((ng, 2, 4, 2)), dma((ng, 2, 4, 2, nc))],
        compiler_params=pltpu.CompilerParams(
            collective_id=0, has_side_effects=True, vmem_limit_bytes=58 * 2**20
        ),
        name="lanes",
    )(orders, inputs, cotangent, first_weight, second_weight)
    return input_grad, first.astype(jnp.float32), second.astype(jnp.float32)


def dot(left, right, dims=(((1,), (0,)), ((), ()))):
    return lax.dot_general(left, right, dims, preferred_element_type=jnp.float32)


def factors(scale, order, x, c, w1, w2, ig, gf, gs, w1p, w2p, act, pre):
    bf = jnp.bfloat16
    place = lax.broadcasted_iota(jnp.int32, (B, B), 0)
    spread_one = (place == order[0:1, :]).astype(jnp.float32).astype(bf)
    spread_two = (place == order[1:2, :]).astype(jnp.float32).astype(bf)
    root = math.sqrt(2.0 / math.pi)
    for h in range(4):
        w1p[h] = dot(spread_one, w1[h, 1]).astype(bf)
        w2p[h] = dot(spread_two, w2[h, 1]).astype(bf)
    for h in range(4):
        p, q = h ^ 2, h ^ 1
        v = dot(x[h], w1[h, 0]) + dot(x[p], w1p[h])
        up = dot(c[h], w2[h, 0], NT) + dot(c[q], w2p[q], NT)
        v2 = v * v
        t = jnp.tanh(root * v * (1.0 + 0.044715 * v2))
        half = 0.5 + 0.5 * t
        act[h] = (v * half).astype(bf)
        slope = half + (0.5 * root) * v * (1.0 - t * t) * (1.0 + (3 * 0.044715) * v2)
        pre[h] = (up * slope).astype(bf)
    for h in range(4):
        p, q = h ^ 2, h ^ 1
        ig[h] = (dot(pre[h], w1[h, 0], NT) + dot(pre[p], w1p[p], NT)).astype(bf)
        gf[h, 0] = (dot(x[h], pre[h], TN) * scale).astype(bf)
        cross = (dot(x[p], pre[h], TN) * scale).astype(bf)
        gf[h, 1] = dot(spread_one, cross, TN).astype(bf)
        gs[h, 0] = (dot(act[h], c[h], TN) * scale).astype(bf)
        cross = (dot(act[q], c[h], TN) * scale).astype(bf)
        gs[h, 1] = dot(spread_two, cross, TN).astype(bf)


def shards(plan, inputs, cotangent, first_weight, second_weight, orders):
    tok, width = inputs.shape
    rows = first_weight.shape[2]
    bf = jnp.bfloat16
    all_tok = plan.g * tok
    nq = plan.nq
    scale = 1.0 / math.sqrt(tok * plan.dp)
    dma = pltpu.SemaphoreType.DMA
    n_t, n_w = 4 * plan.g, 4 * plan.dp
    toks = pltpu.VMEM((nq, 4, all_tok, B), bf)
    mats = pltpu.VMEM((nq, 4, 2, B, B), bf)
    part = jax.ShapeDtypeStruct((plan.groups, plan.nb, 2, rows, B), bf)
    input_grad, first, second = pl.pallas_call(
        functools.partial(whole, plan, scale),
        out_shape=(jax.ShapeDtypeStruct((tok, width), bf), part, part),
        in_specs=[pl.BlockSpec(memory_space=pltpu.VMEM)] + [ANY] * 4,
        out_specs=(ANY,) * 3,
        scratch_shapes=[toks, toks, mats, mats, toks, mats, mats]
        + [pltpu.VMEM((4, B, B), bf)] * 2
        + [pltpu.VMEM((4, all_tok, B), bf)] * 2
        + [dma((nq, 2, n_t)), dma((nq, 2, n_t)), dma((nq, 2, n_w)), dma((nq, 2, n_w)), dma((nq, 4))]
        + [dma((nq, n_t)), dma((nq, n_t)), dma((nq, 2, n_w)), dma((nq, 2, n_w)), dma((nq, 3))],
        compiler_params=pltpu.CompilerParams(
            collective_id=0, has_side_effects=True, vmem_limit_bytes=56 * 2**20
        ),
        name="whole",
    )(orders, inputs, cotangent, first_weight, second_weight)
    total = lambda parts: jnp.sum(parts.astype(jnp.float32), axis=0)
    return input_grad, total(first), total(second)


def solution(mesh):
    in_specs = (
        P("dp", "mp"),
        P("dp", "mp"),
        P("mp", None, "dp", None),
        P("mp", None, "dp", None),
        P(),
    )
    out_specs = (P("dp", "mp"), P("mp", None, "dp", None), P("mp", None, "dp", None))

    def body(inputs, *rest):
        sizes = mesh.shape["dp"], mesh.shape["mp"], inputs.shape[1] // B
        plan = Lanes(*sizes)
        if plan.fits:
            return by_lanes(plan, inputs, *rest)
        plan = Plan(*sizes)
        return shards(plan, inputs, *rest)

    return jax.shard_map(body, mesh=mesh, in_specs=in_specs, out_specs=out_specs, check_vma=False)
```

```python
import functools
import math

import jax
import jax.numpy as jnp
from jax import lax
from jax.experimental import pallas as pl
from jax.experimental.pallas import tpu as pltpu
from jax.sharding import PartitionSpec as P

B = 256
MESH = pl.DeviceIdType.MESH
ANY = pl.BlockSpec(memory_space=pl.ANY)
NT = (((1,), (1,)), ((), ()))
TN = (((0,), (0,)), ((), ()))


class Plan:
    def __init__(self, dp, mp, local_blocks):
        self.dp, self.mp, self.nb = dp, mp, local_blocks
        self.low = mp // 4
        g = max(1, dp // 2)
        while local_blocks % (4 * g):
            g //= 2
        self.g, self.groups = g, dp // g
        self.nq = local_blocks // (4 * g)

    def here(self):
        d, m = lax.axis_index("dp"), lax.axis_index("mp")
        return d, d // self.g, d % self.g, m // self.low, m % self.low


def greet(plan, d, h, lo):
    barrier = pltpu.get_barrier_semaphore()
    others = 4 * plan.dp
    me = d * 4 + h
    for k in range(1, others):
        t = (me + k) % others
        pl.semaphore_signal(
            barrier, inc=1, device_id=(t // 4, (t % 4) * plan.low + lo), device_id_type=MESH
        )
    pl.semaphore_wait(barrier, others - 1)


def sweep(first, last, body):
    lax.fori_loop(first, last, lambda k, _: (body(k), None)[1], None)


def whole(plan, scale, order, x, c, w1, w2, igo, gfo, gso, xb, cb, w1b, w2b, ig, gf, gs, w1p, w2p, act, pre,
          ts, tr, ws, wr, ls, os, orr, gsem, gr, ol):
    d, gi, r, h, lo = plan.here()
    tok, rows, nq = x.shape[0], w1.shape[2], plan.nq
    n_t, n_w = 4 * plan.g, 4 * plan.dp
    me_o, me_w = r * 4 + h, d * 4 + h
    greet(plan, d, h, lo)

    def peer_of_group(t):
        return (gi * plan.g + t // 4, (t % 4) * plan.low + lo)

    def peer_of_all(t):
        return (t // 4, (t % 4) * plan.low + lo)

    def tokens_in(i, a, k):
        t = (me_o + 5 * k) % n_t
        src, dst = ((x, xb), (c, cb))[a]
        s = src.at[:, pl.ds(pl.multiple_of((t * nq + i) * B, B), B)]
        e = dst.at[i, h, pl.ds(pl.multiple_of(r * tok, tok), tok)]
        if isinstance(k, int) and k == 0:
            return pltpu.make_async_copy(s, e, ls.at[i, a])
        return pltpu.make_async_remote_copy(
            s, e, ts.at[i, a, k], tr.at[i, a, k], device_id=peer_of_group(t), device_id_type=MESH
        )

    def weights_in(i, a, k):
        t = (me_w + 11 * k) % n_w
        src, dst = ((w1, w1b), (w2, w2b))[a]
        o = ((t // 4) % plan.g) * 4 + t % 4
        s = src.at[o * nq + i]
        e = dst.at[i, h, :, pl.ds(pl.multiple_of(d * rows, rows), rows)]
        if isinstance(k, int) and k == 0:
            return pltpu.make_async_copy(s, e, ls.at[i, 2 + a])
        return pltpu.make_async_remote_copy(
            s, e, ws.at[i, a, k], wr.at[i, a, k], device_id=peer_of_all(t), device_id_type=MESH
        )

    def tokens_out(i, k):
        t = (me_o + 5 * k) % n_t
        s = ig.at[i, t % 4, pl.ds(pl.multiple_of((t // 4) * tok, tok), tok)]
        e = igo.at[:, pl.ds(pl.multiple_of((me_o * nq + i) * B, B), B)]
        if isinstance(k, int) and k == 0:
            return pltpu.make_async_copy(s, e, ol.at[i, 0])
        return pltpu.make_async_remote_copy(
            s, e, os.at[i, k], orr.at[i, k], device_id=peer_of_group(t), device_id_type=MESH
        )

    def grads_out(i, a, k):
        t = (me_w + 11 * k) % n_w
        src, dst = ((gf, gfo), (gs, gso))[a]
        s = src.at[i, t % 4, :, pl.ds(pl.multiple_of((t // 4) * rows, rows), rows)]
        e = dst.at[gi, me_o * nq + i]
        if isinstance(k, int) and k == 0:
            return pltpu.make_async_copy(s, e, ol.at[i, 1 + a])
        return pltpu.make_async_remote_copy(
            s, e, gsem.at[i, a, k], gr.at[i, a, k], device_id=peer_of_all(t), device_id_type=MESH
        )

    def all_in(i, act_on):
        def some_weights(k, first):
            for j in range(first, plan.groups):
                for a in (0, 1):
                    act_on(weights_in(i, a, plan.groups * k + j))

        def both(k):
            act_on(tokens_in(i, 0, k))
            some_weights(k, 0)
            act_on(tokens_in(i, 1, k))

        some_weights(0, 1)
        sweep(1, n_t, both)

    def all_out(i, act_on):
        def some_grads(k, first):
            for j in range(first, plan.groups):
                for a in (0, 1):
                    act_on(grads_out(i, a, plan.groups * k + j))

        def both(k):
            act_on(tokens_out(i, k))
            some_grads(k, 0)

        some_grads(0, 1)
        sweep(1, n_t, both)

    def own_in(i):
        return [f(i, a, 0) for f in (tokens_in, weights_in) for a in (0, 1)]

    def own_out(i):
        return [tokens_out(i, 0), grads_out(i, 0, 0), grads_out(i, 1, 0)]

    for i in range(nq):
        all_in(i, lambda copy: copy.start())
        for copy in own_in(i):
            copy.start()
    for i in range(nq):
        for copy in own_in(i):
            copy.wait()
        all_in(i, lambda copy: copy.wait_recv())
        factors(scale, order, xb.at[i], cb.at[i], w1b.at[i], w2b.at[i], ig.at[i], gf.at[i], gs.at[i], w1p, w2p, act, pre)
        all_out(i, lambda copy: copy.start())
        for copy in own_out(i):
            copy.start()
    for i in range(nq):
        all_in(i, lambda copy: copy.wait_send())
        for copy in own_out(i):
            copy.wait()
        all_out(i, lambda copy: copy.wait())


class Lanes:
    def __init__(self, dp, mp, local_blocks):
        self.nc = nc = dp // 4
        self.low = mp // 4
        self.ng = local_blocks // (4 * nc) if nc else 0
        self.fits = dp % 4 == 0 and mp % 4 == 0 and self.ng > 0 and local_blocks % (4 * nc) == 0


def lanes(plan, scale, orders, x, c, w1, w2, igo, gfo, gso, order, ordered, xb, cb, w1b, w2b, ig, gf, gs, gif, gis, w1p, w2p, act, pre,
          tin, win, wout, wrel, gin, done, st, sw, sd, sr, so, su, si, sg, sf):
    nc, low, ng = plan.nc, plan.low, plan.ng
    tok, rows = x.shape[0], w1.shape[2]
    d, m = lax.axis_index("dp"), lax.axis_index("mp")
    h, lo = m // low, m % low
    quarter, side, core, slot = d // nc, d // (2 * nc), d % nc, d % (2 * nc)
    inner = jnp.logical_or(quarter == 1, quarter == 2)
    outer = jnp.logical_not(inner)
    base, other, far = nc + side * nc, 2 * nc - side * nc, 3 * nc * side
    first, me, us = 2 * nc * side, core * 4 + h, slot * 4 + h
    n_s, n_o = 4 * nc, 8 * nc
    X, W, G, GI, GO = (x, c), (w1, w2), (gf, gs), (gif, gis), (gfo, gso)
    XB, WB = (xb, cb), (w1b, w2b)

    def mp_of(hh):
        return hh * low + lo

    def span(start, size):
        return pl.ds(pl.multiple_of(start * size, size), size)

    def put(src, dst, ssem, rsem, dev):
        return pltpu.make_async_remote_copy(src, dst, ssem, rsem, device_id=dev, device_id_type=MESH)

    def arrived(ref, sem):
        pltpu.make_async_copy(ref, ref, sem).wait()

    barrier = pltpu.get_barrier_semaphore()

    def hello(dev):
        pl.semaphore_signal(barrier, inc=1, device_id=dev, device_id_type=MESH)

    @pl.when(inner)
    def _():
        for k in range(1, n_o):
            u = (us + k) % n_o
            hello((first + u // 4, mp_of(u % 4)))
        for cs in range(nc):
            hello((other + cs, m))
        pl.semaphore_wait(barrier, n_o - 1 + nc)

    @pl.when(outer)
    def _():
        for k in range(n_s):
            t = (me + k) % n_s
            hello((base + t // 4, mp_of(t % 4)))
        for kh in range(1, 4):
            hello((d, mp_of((h + kh) % 4)))
        pl.semaphore_wait(barrier, n_s + 3)

    def block_of(a, t, i):
        return W[a].at[t * ng + i]

    def columns_of(a, t, i):
        return X[a].at[:, span(t * ng + i, B)]

    def own_w(i, a, k):
        t = (me + k) % n_s
        e = WB[a].at[i, h, :, span(d, rows)]
        if isinstance(k, int) and k == 0:
            return pltpu.make_async_copy(block_of(a, t, i), e, win.at[i, a, h])
        return put(block_of(a, t, i), e, sw.at[i, a, k], win.at[i, a, h], (base + t // 4, mp_of(t % 4)))

    def cross_w(i, a, cs):
        e = WB[a].at[i, h, :, span(d, rows)]
        return put(block_of(a, cs * 4 + h, i), e, sd.at[i, a, cs], wrel.at[i, a], (other + cs, m))

    def own_t(i, a, k):
        t = (me + k) % n_s
        e = XB[a].at[i, h, span(slot, tok)]
        if isinstance(k, int) and k == 0:
            return pltpu.make_async_copy(columns_of(a, t, i), e, tin.at[i, a])
        return put(columns_of(a, t, i), e, st.at[i, a, k], tin.at[i, a], (base + t // 4, mp_of(t % 4)))

    def plane_w(i, a, cs, kh):
        hh = (h + kh) % 4
        s, e = block_of(a, cs * 4 + hh, i), WB[a].at[i, h, :, span(cs, rows)]
        if kh == 0:
            return pltpu.make_async_copy(s, e, wout.at[i, a])
        return put(s, e, sw.at[i, a, cs * 4 + kh], wout.at[i, a], (d, mp_of(hh)))

    def plane_t(i, a, cs, kh):
        hh = (h + kh) % 4
        s, e = columns_of(a, cs * 4 + hh, i), XB[a].at[i, h, span(cs, tok)]
        if kh == 0:
            return pltpu.make_async_copy(s, e, tin.at[i, a])
        return put(s, e, st.at[i, a, cs * 4 + kh], tin.at[i, a], (d, mp_of(hh)))

    def up_w(i, a, cs):
        s, e = WB[a].at[i, :, :, span(cs, rows)], WB[a].at[i, :, :, span(d, rows)]
        return put(s, e, su.at[i, a, cs], wout.at[i, a], (base + cs, m))

    def up_t(i, a, cs):
        s, e = XB[a].at[i, :, span(cs, tok)], XB[a].at[i, :, span(slot, tok)]
        return put(s, e, su.at[i, 2 + a, cs], tin.at[i, a], (base + cs, m))

    def relay_in(i, a, kh):
        s = WB[a].at[i, (h + kh) % 4, :, span(base // nc, nc * rows)]
        return put(s, s, sr.at[i, a, kh], wrel.at[i, a], (other + core, m))

    def relay_out(i, a):
        s = WB[a].at[i, :, :, span(far // nc, nc * rows)]
        return put(s, s, so.at[i, a], wrel.at[i, a], (other + core, m))

    def tokens_out(i, k):
        u = (us + k) % n_o
        s, e = ig.at[i, u % 4, span(u // 4, tok)], igo.at[:, span(me * ng + i, B)]
        if isinstance(k, int) and k == 0:
            return pltpu.make_async_copy(s, e, done.at[0])
        return put(s, e, si.at[i, k], done.at[0], (first + u // 4, mp_of(u % 4)))

    def partial(i, a, kh, near):
        hh, theirs = (h + kh) % 4, other // nc if near else 3 - far // nc
        s = G[a].at[i, hh, :, span(theirs, nc * rows)]
        return put(s, GI[a].at[i, hh, near], sg.at[i, a, kh, near], gin.at[i, a, kh, near], (other + core, m))

    def grads_out(i, a, kh, near, k):
        hh, cs = (h + kh) % 4, (core + k) % nc
        s, e = GI[a].at[i, hh, near, :, span(cs, rows)], GO[a].at[me * ng + i]
        if near and kh == 0 and k == 0:
            return pltpu.make_async_copy(s, e, done.at[1 + a])
        return put(s, e, sf.at[i, a, kh, near, k], done.at[1 + a], ((base if near else far) + cs, mp_of(hh)))

    parts = [(a, kh, near) for near in (0, 1) for kh in (1, 2, 3, 0) for a in (0, 1)]

    def both(f, *at):
        return [f(at[0], a, *at[1:]) for a in (0, 1)]

    def begin(copies):
        for copy in copies:
            copy.start()

    def combine(i):
        for a, kh, near in parts:
            hh = (h + kh) % 4
            arrived(GI[a].at[i, hh, near], gin.at[i, a, kh, near])
            ours = base // nc if near else far // nc
            mine = G[a][i, hh, :, span(ours, nc * rows)].astype(jnp.float32)
            GI[a][i, hh, near] = (mine + GI[a][i, hh, near].astype(jnp.float32)).astype(jnp.bfloat16)
            begin([grads_out(i, a, kh, near, k) for k in range(nc)])

    @pl.when(inner)
    def _():
        for i in range(ng):
            for cs in range(nc):
                begin(both(cross_w, i, cs))
        pltpu.make_async_copy(orders, order, ordered).start()
        for i in range(ng):
            sweep(1, n_s, lambda k: begin(both(own_w, i, k)))
            begin(both(own_w, i, 0))
        for i in range(ng):
            sweep(1, n_s, lambda k: begin(both(own_t, i, k)))
            begin(both(own_t, i, 0))
        for i in range(ng):
            for kh in range(4):
                for a in (0, 1):
                    hh = (h + kh) % 4
                    arrived(WB[a].at[i, hh, :, span(base // nc, nc * rows)], win.at[i, a, hh])
                    if kh:
                        relay_in(i, a, kh).start()
        for i in range(ng):
            for a in (0, 1):
                arrived(WB[a].at[i, :, :, span(far // nc, nc * rows)], wout.at[i, a])
                relay_out(i, a).start()
        arrived(order, ordered)
        for i in range(ng):
            for a in (0, 1):
                arrived(WB[a].at[i, :, :, span(1 - side, 2 * nc * rows)], wrel.at[i, a])
                arrived(XB[a].at[i], tin.at[i, a])
            factors(scale, order, xb.at[i], cb.at[i], w1b.at[i], w2b.at[i], ig.at[i], gf.at[i], gs.at[i], w1p, w2p, act, pre)
            begin([partial(i, *at) for at in parts])
            sweep(1, n_o, lambda k: tokens_out(i, k).start())
            tokens_out(i, 0).start()
            if i >= 1:
                combine(i - 1)
        combine(ng - 1)
        for i in range(ng):
            for a in (0, 1):
                sweep(1, n_s, lambda k: own_w(i, a, k).wait_send())
                sweep(1, n_s, lambda k: own_t(i, a, k).wait_send())
                for cs in range(nc):
                    cross_w(i, a, cs).wait_send()
                for kh in range(1, 4):
                    relay_in(i, a, kh).wait_send()
                relay_out(i, a).wait_send()
            sweep(1, n_o, lambda k: tokens_out(i, k).wait_send())
            for a, kh, near in parts:
                partial(i, a, kh, near).wait_send()
                for k in range(nc):
                    if not near or kh or k:
                        grads_out(i, a, kh, near, k).wait_send()

    @pl.when(outer)
    def _():
        for i in range(ng):
            for kh in (1, 2, 3, 0):
                for cs in range(nc):
                    begin(both(plane_w, i, cs, kh))
        for i in range(ng):
            for kh in (1, 2, 3, 0):
                for cs in range(nc):
                    begin(both(plane_t, i, cs, kh))
        for i in range(ng):
            for a in (0, 1):
                arrived(WB[a].at[i, :, :, span(0, nc * rows)], wout.at[i, a])
                begin([up_w(i, a, cs) for cs in range(nc)])
        for i in range(ng):
            for a in (0, 1):
                arrived(XB[a].at[i, :, span(0, nc * tok)], tin.at[i, a])
                begin([up_t(i, a, cs) for cs in range(nc)])
        for i in range(ng):
            for a in (0, 1):
                for cs in range(nc):
                    for kh in range(1, 4):
                        plane_w(i, a, cs, kh).wait_send()
                        plane_t(i, a, cs, kh).wait_send()
                    up_w(i, a, cs).wait_send()
                    up_t(i, a, cs).wait_send()

    arrived(igo, done.at[0])
    arrived(gfo, done.at[1])
    arrived(gso, done.at[2])


def by_lanes(plan, inputs, cotangent, first_weight, second_weight, orders):
    tok, width = inputs.shape
    rows = first_weight.shape[2]
    nc, ng, bf = plan.nc, plan.ng, jnp.bfloat16
    scale = 1.0 / math.sqrt(tok * 4 * nc)
    dma = pltpu.SemaphoreType.DMA
    toks = pltpu.VMEM((ng, 4, 2 * nc * tok, B), bf)
    mats = pltpu.VMEM((ng, 4, 2, B, B), bf)
    half = pltpu.VMEM((ng, 4, 2, 2, nc * rows, B), bf)
    part = pltpu.VMEM(first_weight.shape, bf)
    input_grad, first, second = pl.pallas_call(
        functools.partial(lanes, plan, scale),
        out_shape=(pltpu.VMEM((tok, width), bf), part, part),
        in_specs=[ANY] * 5,
        out_specs=(ANY,) * 3,
        scratch_shapes=[pltpu.VMEM(orders.shape, orders.dtype), dma]
        + [toks, toks, mats, mats, toks, mats, mats, half, half]
        + [pltpu.VMEM((4, B, B), bf)] * 2
        + [pltpu.VMEM((4, 2 * nc * tok, B), bf)] * 2
        + [dma((ng, 2)), dma((ng, 2, 4)), dma((ng, 2)), dma((ng, 2)), dma((ng, 2, 4, 2)), dma((3,))]
        + [dma((ng, 2, 4 * nc)), dma((ng, 2, 4 * nc)), dma((ng, 2, nc)), dma((ng, 2, 4)), dma((ng, 2)), dma((ng, 4, nc))]
        + [dma((ng, 8 * nc)), dma((ng, 2, 4, 2)), dma((ng, 2, 4, 2, nc))],
        compiler_params=pltpu.CompilerParams(
            collective_id=0, has_side_effects=True, vmem_limit_bytes=58 * 2**20
        ),
        name="lanes",
    )(orders, inputs, cotangent, first_weight, second_weight)
    return input_grad, first.astype(jnp.float32), second.astype(jnp.float32)


def dot(left, right, dims=(((1,), (0,)), ((), ()))):
    return lax.dot_general(left, right, dims, preferred_element_type=jnp.float32)


def factors(scale, order, x, c, w1, w2, ig, gf, gs, w1p, w2p, act, pre):
    bf = jnp.bfloat16
    place = lax.broadcasted_iota(jnp.int32, (B, B), 0)
    spread_one = (place == order[0:1, :]).astype(jnp.float32).astype(bf)
    spread_two = (place == order[1:2, :]).astype(jnp.float32).astype(bf)
    root = math.sqrt(2.0 / math.pi)
    for h in range(4):
        w1p[h] = dot(spread_one, w1[h, 1]).astype(bf)
        w2p[h] = dot(spread_two, w2[h, 1]).astype(bf)
    for h in range(4):
        p, q = h ^ 2, h ^ 1
        v = dot(x[h], w1[h, 0]) + dot(x[p], w1p[h])
        up = dot(c[h], w2[h, 0], NT) + dot(c[q], w2p[q], NT)
        v2 = v * v
        t = jnp.tanh(root * v * (1.0 + 0.044715 * v2))
        half = 0.5 + 0.5 * t
        act[h] = (v * half).astype(bf)
        slope = half + (0.5 * root) * v * (1.0 - t * t) * (1.0 + (3 * 0.044715) * v2)
        pre[h] = (up * slope).astype(bf)
    for h in range(4):
        p, q = h ^ 2, h ^ 1
        ig[h] = (dot(pre[h], w1[h, 0], NT) + dot(pre[p], w1p[p], NT)).astype(bf)
        gf[h, 0] = (dot(x[h], pre[h], TN) * scale).astype(bf)
        cross = (dot(x[p], pre[h], TN) * scale).astype(bf)
        gf[h, 1] = dot(spread_one, cross, TN).astype(bf)
        gs[h, 0] = (dot(act[h], c[h], TN) * scale).astype(bf)
        cross = (dot(act[q], c[h], TN) * scale).astype(bf)
        gs[h, 1] = dot(spread_two, cross, TN).astype(bf)


def shards(plan, inputs, cotangent, first_weight, second_weight, orders):
    tok, width = inputs.shape
    rows = first_weight.shape[2]
    bf = jnp.bfloat16
    all_tok = plan.g * tok
    nq = plan.nq
    scale = 1.0 / math.sqrt(tok * plan.dp)
    dma = pltpu.SemaphoreType.DMA
    n_t, n_w = 4 * plan.g, 4 * plan.dp
    toks = pltpu.VMEM((nq, 4, all_tok, B), bf)
    mats = pltpu.VMEM((nq, 4, 2, B, B), bf)
    part = jax.ShapeDtypeStruct((plan.groups, plan.nb, 2, rows, B), bf)
    input_grad, first, second = pl.pallas_call(
        functools.partial(whole, plan, scale),
        out_shape=(jax.ShapeDtypeStruct((tok, width), bf), part, part),
        in_specs=[pl.BlockSpec(memory_space=pltpu.VMEM)] + [ANY] * 4,
        out_specs=(ANY,) * 3,
        scratch_shapes=[toks, toks, mats, mats, toks, mats, mats]
        + [pltpu.VMEM((4, B, B), bf)] * 2
        + [pltpu.VMEM((4, all_tok, B), bf)] * 2
        + [dma((nq, 2, n_t)), dma((nq, 2, n_t)), dma((nq, 2, n_w)), dma((nq, 2, n_w)), dma((nq, 4))]
        + [dma((nq, n_t)), dma((nq, n_t)), dma((nq, 2, n_w)), dma((nq, 2, n_w)), dma((nq, 3))],
        compiler_params=pltpu.CompilerParams(
            collective_id=0, has_side_effects=True, vmem_limit_bytes=56 * 2**20
        ),
        name="whole",
    )(orders, inputs, cotangent, first_weight, second_weight)
    total = lambda parts: jnp.sum(parts.astype(jnp.float32), axis=0)
    return input_grad, total(first), total(second)


def solution(mesh):
    in_specs = (
        P("dp", "mp"),
        P("dp", "mp"),
        P("mp", None, "dp", None),
        P("mp", None, "dp", None),
        P(),
    )
    out_specs = (P("dp", "mp"), P("mp", None, "dp", None), P("mp", None, "dp", None))

    def body(inputs, *rest):
        sizes = mesh.shape["dp"], mesh.shape["mp"], inputs.shape[1] // B
        plan = Lanes(*sizes)
        if plan.fits:
            return by_lanes(plan, inputs, *rest)
        plan = Plan(*sizes)
        return shards(plan, inputs, *rest)

    return jax.shard_map(body, mesh=mesh, in_specs=in_specs, out_specs=out_specs, check_vma=False)
```

```python
import functools
import math

import jax
import jax.numpy as jnp
from jax import lax
from jax.experimental import pallas as pl
from jax.experimental.pallas import tpu as pltpu
from jax.sharding import PartitionSpec as P

B = 256
CHUNKS = 4
MESH = pl.DeviceIdType.MESH
ANY = pl.BlockSpec(memory_space=pl.ANY)
NT = (((1,), (1,)), ((), ()))
TN = (((0,), (0,)), ((), ()))


class Plan:
    def __init__(self, dp, mp, local_blocks):
        self.dp, self.mp, self.nb = dp, mp, local_blocks
        self.low = mp // 4
        g = max(1, dp // 2)
        while local_blocks % (4 * g):
            g //= 2
        self.g, self.groups = g, dp // g
        self.nq = local_blocks // (4 * g)

    def here(self):
        d, m = lax.axis_index("dp"), lax.axis_index("mp")
        return d, d // self.g, d % self.g, m // self.low, m % self.low


def greet(plan, d, h, lo):
    barrier = pltpu.get_barrier_semaphore()
    others = 4 * plan.dp
    me = d * 4 + h
    for k in range(1, others):
        t = (me + k) % others
        pl.semaphore_signal(
            barrier, inc=1, device_id=(t // 4, (t % 4) * plan.low + lo), device_id_type=MESH
        )
    pl.semaphore_wait(barrier, others - 1)


def sweep(first, last, body):
    lax.fori_loop(first, last, lambda k, _: (body(k), None)[1], None)


def whole(plan, scale, order, x, c, w1, w2, igo, gfo, gso, xb, cb, w1b, w2b, ig, gf, gs, w1p, w2p, act, pre,
          ts, tr, ws, wr, ls, os, orr, gsem, gr, ol):
    d, gi, r, h, lo = plan.here()
    tok, rows, nq = x.shape[0], w1.shape[2], plan.nq
    n_t, n_w = 4 * plan.g, 4 * plan.dp
    me_o, me_w = r * 4 + h, d * 4 + h
    greet(plan, d, h, lo)

    def peer_of_group(t):
        return (gi * plan.g + t // 4, (t % 4) * plan.low + lo)

    def peer_of_all(t):
        return (t // 4, (t % 4) * plan.low + lo)

    def tokens_in(i, a, k):
        t = (me_o + 5 * k) % n_t
        src, dst = ((x, xb), (c, cb))[a]
        s = src.at[:, pl.ds(pl.multiple_of((t * nq + i) * B, B), B)]
        e = dst.at[i, h, pl.ds(pl.multiple_of(r * tok, tok), tok)]
        if isinstance(k, int) and k == 0:
            return pltpu.make_async_copy(s, e, ls.at[i, a])
        return pltpu.make_async_remote_copy(
            s, e, ts.at[i, a, k], tr.at[i, a, k], device_id=peer_of_group(t), device_id_type=MESH
        )

    def weights_in(i, a, k):
        t = (me_w + 11 * k) % n_w
        src, dst = ((w1, w1b), (w2, w2b))[a]
        o = ((t // 4) % plan.g) * 4 + t % 4
        s = src.at[o * nq + i]
        e = dst.at[i, h, :, pl.ds(pl.multiple_of(d * rows, rows), rows)]
        if isinstance(k, int) and k == 0:
            return pltpu.make_async_copy(s, e, ls.at[i, 2 + a])
        return pltpu.make_async_remote_copy(
            s, e, ws.at[i, a, k], wr.at[i, a, k], device_id=peer_of_all(t), device_id_type=MESH
        )

    def tokens_out(i, k):
        t = (me_o + 5 * k) % n_t
        s = ig.at[i, t % 4, pl.ds(pl.multiple_of((t // 4) * tok, tok), tok)]
        e = igo.at[:, pl.ds(pl.multiple_of((me_o * nq + i) * B, B), B)]
        if isinstance(k, int) and k == 0:
            return pltpu.make_async_copy(s, e, ol.at[i, 0])
        return pltpu.make_async_remote_copy(
            s, e, os.at[i, k], orr.at[i, k], device_id=peer_of_group(t), device_id_type=MESH
        )

    def grads_out(i, a, k):
        t = (me_w + 11 * k) % n_w
        src, dst = ((gf, gfo), (gs, gso))[a]
        s = src.at[i, t % 4, :, pl.ds(pl.multiple_of((t // 4) * rows, rows), rows)]
        e = dst.at[gi, me_o * nq + i]
        if isinstance(k, int) and k == 0:
            return pltpu.make_async_copy(s, e, ol.at[i, 1 + a])
        return pltpu.make_async_remote_copy(
            s, e, gsem.at[i, a, k], gr.at[i, a, k], device_id=peer_of_all(t), device_id_type=MESH
        )

    def all_in(i, act_on):
        def some_weights(k, first):
            for j in range(first, plan.groups):
                for a in (0, 1):
                    act_on(weights_in(i, a, plan.groups * k + j))

        def both(k):
            act_on(tokens_in(i, 0, k))
            some_weights(k, 0)
            act_on(tokens_in(i, 1, k))

        some_weights(0, 1)
        sweep(1, n_t, both)

    def all_out(i, act_on):
        def some_grads(k, first):
            for j in range(first, plan.groups):
                for a in (0, 1):
                    act_on(grads_out(i, a, plan.groups * k + j))

        def both(k):
            act_on(tokens_out(i, k))
            some_grads(k, 0)

        some_grads(0, 1)
        sweep(1, n_t, both)

    def own_in(i):
        return [f(i, a, 0) for f in (tokens_in, weights_in) for a in (0, 1)]

    def own_out(i):
        return [tokens_out(i, 0), grads_out(i, 0, 0), grads_out(i, 1, 0)]

    for i in range(nq):
        all_in(i, lambda copy: copy.start())
        for copy in own_in(i):
            copy.start()
    for i in range(nq):
        for copy in own_in(i):
            copy.wait()
        all_in(i, lambda copy: copy.wait_recv())
        factors(scale, order, xb.at[i], cb.at[i], w1b.at[i], w2b.at[i], ig.at[i], gf.at[i], gs.at[i], w1p, w2p, act, pre)
        all_out(i, lambda copy: copy.start())
        for copy in own_out(i):
            copy.start()
    for i in range(nq):
        all_in(i, lambda copy: copy.wait_send())
        for copy in own_out(i):
            copy.wait()
        all_out(i, lambda copy: copy.wait())


class Lanes:
    def __init__(self, dp, mp, local_blocks):
        self.nc = nc = dp // 4
        self.low = mp // 4
        self.ng = local_blocks // (4 * nc) if nc else 0
        self.fits = dp % 4 == 0 and mp % 4 == 0 and self.ng > 0 and local_blocks % (4 * nc) == 0


def lanes(plan, scale, orders, x, c, w1, w2, igo, gfo, gso, order, ordered, xb, cb, w1b, w2b, ig, gf, gs, gif, gis, w1p, w2p, act, pre,
          tin, win, wout, wrel, gin, done, st, sw, sd, sr, so, su, si, sg, sf):
    nc, low, ng = plan.nc, plan.low, plan.ng
    tok, rows = x.shape[0], w1.shape[2]
    d, m = lax.axis_index("dp"), lax.axis_index("mp")
    h, lo = m // low, m % low
    quarter, side, core, slot = d // nc, d // (2 * nc), d % nc, d % (2 * nc)
    inner = jnp.logical_or(quarter == 1, quarter == 2)
    outer = jnp.logical_not(inner)
    base, other, far = nc + side * nc, 2 * nc - side * nc, 3 * nc * side
    first, me, us = 2 * nc * side, core * 4 + h, slot * 4 + h
    n_s, n_o = 4 * nc, 8 * nc
    X, W, G, GI, GO = (x, c), (w1, w2), (gf, gs), (gif, gis), (gfo, gso)
    XB, WB = (xb, cb), (w1b, w2b)

    def mp_of(hh):
        return hh * low + lo

    def span(start, size):
        return pl.ds(pl.multiple_of(start * size, size), size)

    def put(src, dst, ssem, rsem, dev):
        return pltpu.make_async_remote_copy(src, dst, ssem, rsem, device_id=dev, device_id_type=MESH)

    def arrived(ref, sem):
        pltpu.make_async_copy(ref, ref, sem).wait()

    barrier = pltpu.get_barrier_semaphore()

    def hello(dev):
        pl.semaphore_signal(barrier, inc=1, device_id=dev, device_id_type=MESH)

    @pl.when(inner)
    def _():
        for cs in range(nc):
            hello((other + cs, m))
        for k in range(1, n_s):
            t = (me + k) % n_s
            hello((base + t // 4, mp_of(t % 4)))
        for cs in range(nc):
            hello((far + cs, m))
        pl.semaphore_wait(barrier, n_s - 1 + nc)

    @pl.when(outer)
    def _():
        for kh in range(1, 4):
            hello((d, mp_of((h + kh) % 4)))
        pl.semaphore_wait(barrier, nc + 3)

    def block_of(a, t, i):
        return W[a].at[t * ng + i]

    def columns_of(a, t, i):
        return X[a].at[:, span(t * ng + i, B)]

    def own_w(i, a, k):
        t = (me + k) % n_s
        e = WB[a].at[i, h, :, span(d, rows)]
        if isinstance(k, int) and k == 0:
            return pltpu.make_async_copy(block_of(a, t, i), e, win.at[i, a, h])
        return put(block_of(a, t, i), e, sw.at[i, a, k], win.at[i, a, h], (base + t // 4, mp_of(t % 4)))

    def cross_w(i, a, cs):
        e = WB[a].at[i, h, :, span(d, rows)]
        return put(block_of(a, cs * 4 + h, i), e, sd.at[i, a, cs], wrel.at[i, a], (other + cs, m))

    def own_t(i, a, k):
        t = (me + k) % n_s
        e = XB[a].at[i, h, span(slot, tok)]
        if isinstance(k, int) and k == 0:
            return pltpu.make_async_copy(columns_of(a, t, i), e, tin.at[i, a])
        return put(columns_of(a, t, i), e, st.at[i, a, k], tin.at[i, a], (base + t // 4, mp_of(t % 4)))

    def plane_w(i, a, cs, kh):
        hh = (h + kh) % 4
        s, e = block_of(a, cs * 4 + hh, i), WB[a].at[i, h, :, span(cs, rows)]
        if kh == 0:
            return pltpu.make_async_copy(s, e, wout.at[i, a])
        return put(s, e, sw.at[i, a, cs * 4 + kh], wout.at[i, a], (d, mp_of(hh)))

    def plane_t(i, a, cs, kh):
        hh = (h + kh) % 4
        s, e = columns_of(a, cs * 4 + hh, i), XB[a].at[i, h, span(cs, tok)]
        if kh == 0:
            return pltpu.make_async_copy(s, e, tin.at[i, a])
        return put(s, e, st.at[i, a, cs * 4 + kh], tin.at[i, a], (d, mp_of(hh)))

    def up_w(i, a, cs):
        s, e = WB[a].at[i, :, :, span(cs, rows)], WB[a].at[i, :, :, span(d, rows)]
        return put(s, e, su.at[i, a, cs], wout.at[i, a], (base + cs, m))

    def up_t(i, a, cs):
        s, e = XB[a].at[i, :, span(cs, tok)], XB[a].at[i, :, span(slot, tok)]
        return put(s, e, su.at[i, 2 + a, cs], tin.at[i, a], (base + cs, m))

    def relay_in(i, a, kh):
        s = WB[a].at[i, (h + kh) % 4, :, span(base // nc, nc * rows)]
        return put(s, s, sr.at[i, a, kh], wrel.at[i, a], (other + core, m))

    def relay_out(i, a):
        s = WB[a].at[i, :, :, span(far // nc, nc * rows)]
        return put(s, s, so.at[i, a], wrel.at[i, a], (other + core, m))

    def tokens_out(i, k):
        u = (us + k) % n_o
        s, e = ig.at[i, u % 4, span(u // 4, tok)], igo.at[:, span(me * ng + i, B)]
        if isinstance(k, int) and k == 0:
            return pltpu.make_async_copy(s, e, done.at[0])
        return put(s, e, si.at[i, k], done.at[0], (first + u // 4, mp_of(u % 4)))

    def partial(i, a, kh, near):
        hh, theirs = (h + kh) % 4, other // nc if near else 3 - far // nc
        s = G[a].at[i, hh, :, span(theirs, nc * rows)]
        return put(s, GI[a].at[i, hh, near], sg.at[i, a, kh, near], gin.at[i, a, kh, near], (other + core, m))

    def grads_out(i, a, kh, near, k):
        hh, cs = (h + kh) % 4, (core + k) % nc
        s, e = GI[a].at[i, hh, near, :, span(cs, rows)], GO[a].at[me * ng + i]
        if near and kh == 0 and k == 0:
            return pltpu.make_async_copy(s, e, done.at[1 + a])
        return put(s, e, sf.at[i, a, kh, near, k], done.at[1 + a], ((base if near else far) + cs, mp_of(hh)))

    parts = [(a, kh, near) for near in (0, 1) for kh in (1, 2, 3, 0) for a in (0, 1)]

    def both(f, *at):
        return [f(at[0], a, *at[1:]) for a in (0, 1)]

    def begin(copies):
        for copy in copies:
            copy.start()

    def combine(i):
        for a, kh, near in parts:
            hh = (h + kh) % 4
            arrived(GI[a].at[i, hh, near], gin.at[i, a, kh, near])
            ours = base // nc if near else far // nc
            mine = G[a][i, hh, :, span(ours, nc * rows)].astype(jnp.float32)
            GI[a][i, hh, near] = (mine + GI[a][i, hh, near].astype(jnp.float32)).astype(jnp.bfloat16)
            begin([grads_out(i, a, kh, near, k) for k in range(nc)])

    @pl.when(inner)
    def _():
        for i in range(ng):
            for cs in range(nc):
                begin(both(cross_w, i, cs))
        pltpu.make_async_copy(orders, order, ordered).start()
        for i in range(ng):
            sweep(1, n_s, lambda k: begin(both(own_w, i, k)))
            begin(both(own_w, i, 0))
        for i in range(ng):
            sweep(1, n_s, lambda k: begin(both(own_t, i, k)))
            begin(both(own_t, i, 0))
        for i in range(ng):
            for kh in range(4):
                for a in (0, 1):
                    hh = (h + kh) % 4
                    arrived(WB[a].at[i, hh, :, span(base // nc, nc * rows)], win.at[i, a, hh])
                    if kh:
                        relay_in(i, a, kh).start()
        for i in range(ng):
            for a in (0, 1):
                arrived(WB[a].at[i, :, :, span(far // nc, nc * rows)], wout.at[i, a])
                relay_out(i, a).start()
        arrived(order, ordered)
        for i in range(ng):
            for a in (0, 1):
                arrived(WB[a].at[i, :, :, span(1 - side, 2 * nc * rows)], wrel.at[i, a])
                arrived(XB[a].at[i], tin.at[i, a])
            factors(scale, order, xb.at[i], cb.at[i], w1b.at[i], w2b.at[i], ig.at[i], gf.at[i], gs.at[i], w1p, w2p, act, pre)
            begin([partial(i, *at) for at in parts])
            sweep(1, n_o, lambda k: tokens_out(i, k).start())
            tokens_out(i, 0).start()
            if i >= 1:
                combine(i - 1)
        combine(ng - 1)
        for i in range(ng):
            for a in (0, 1):
                sweep(1, n_s, lambda k: own_w(i, a, k).wait_send())
                sweep(1, n_s, lambda k: own_t(i, a, k).wait_send())
                for cs in range(nc):
                    cross_w(i, a, cs).wait_send()
                for kh in range(1, 4):
                    relay_in(i, a, kh).wait_send()
                relay_out(i, a).wait_send()
            sweep(1, n_o, lambda k: tokens_out(i, k).wait_send())
            for a, kh, near in parts:
                partial(i, a, kh, near).wait_send()
                for k in range(nc):
                    if not near or kh or k:
                        grads_out(i, a, kh, near, k).wait_send()

    @pl.when(outer)
    def _():
        for i in range(ng):
            for kh in (1, 2, 3, 0):
                for cs in range(nc):
                    begin(both(plane_w, i, cs, kh))
        for i in range(ng):
            for kh in (1, 2, 3, 0):
                for cs in range(nc):
                    begin(both(plane_t, i, cs, kh))
        for i in range(ng):
            for a in (0, 1):
                arrived(WB[a].at[i, :, :, span(0, nc * rows)], wout.at[i, a])
                begin([up_w(i, a, cs) for cs in range(nc)])
        for i in range(ng):
            for a in (0, 1):
                arrived(XB[a].at[i, :, span(0, nc * tok)], tin.at[i, a])
                begin([up_t(i, a, cs) for cs in range(nc)])
        for i in range(ng):
            for a in (0, 1):
                for cs in range(nc):
                    for kh in range(1, 4):
                        plane_w(i, a, cs, kh).wait_send()
                        plane_t(i, a, cs, kh).wait_send()
                    up_w(i, a, cs).wait_send()
                    up_t(i, a, cs).wait_send()

    arrived(igo, done.at[0])
    arrived(gfo, done.at[1])
    arrived(gso, done.at[2])


def by_lanes(plan, inputs, cotangent, first_weight, second_weight, orders):
    tok, width = inputs.shape
    rows = first_weight.shape[2]
    nc, ng, bf = plan.nc, plan.ng, jnp.bfloat16
    scale = 1.0 / math.sqrt(tok * 4 * nc)
    dma = pltpu.SemaphoreType.DMA
    toks = pltpu.VMEM((ng, 4, 2 * nc * tok, B), bf)
    mats = pltpu.VMEM((ng, 4, 2, B, B), bf)
    half = pltpu.VMEM((ng, 4, 2, 2, nc * rows, B), bf)
    part = pltpu.VMEM(first_weight.shape, bf)
    input_grad, first, second = pl.pallas_call(
        functools.partial(lanes, plan, scale),
        out_shape=(pltpu.VMEM((tok, width), bf), part, part),
        in_specs=[ANY] * 5,
        out_specs=(ANY,) * 3,
        scratch_shapes=[pltpu.VMEM(orders.shape, orders.dtype), dma]
        + [toks, toks, mats, mats, toks, mats, mats, half, half]
        + [pltpu.VMEM((4, B, B), bf)] * 2
        + [pltpu.VMEM((4, 2 * nc * tok, B), bf)] * 2
        + [dma((ng, 2)), dma((ng, 2, 4)), dma((ng, 2)), dma((ng, 2)), dma((ng, 2, 4, 2)), dma((3,))]
        + [dma((ng, 2, 4 * nc)), dma((ng, 2, 4 * nc)), dma((ng, 2, nc)), dma((ng, 2, 4)), dma((ng, 2)), dma((ng, 4, nc))]
        + [dma((ng, 8 * nc)), dma((ng, 2, 4, 2)), dma((ng, 2, 4, 2, nc))],
        compiler_params=pltpu.CompilerParams(
            collective_id=0, has_side_effects=True, vmem_limit_bytes=58 * 2**20
        ),
        name="lanes",
    )(orders, inputs, cotangent, first_weight, second_weight)
    return finish(input_grad, first, second)


def store(ig, first, second, igo, fo, so, fw, sw, sems):
    copies = [pltpu.make_async_copy(ig, igo, sems.at[0, 0])]
    copies[0].start()
    size = max(1, first.shape[0] // CHUNKS)
    for n, at in enumerate(range(0, first.shape[0], size)):
        for a, (src, wide, dst) in enumerate(((first, fw, fo), (second, sw, so))):
            rows = pl.ds(at, size)
            wide[rows] = src[rows].astype(jnp.float32)
            copies.append(pltpu.make_async_copy(wide.at[rows], dst.at[rows], sems.at[1 + a, n]))
            copies[-1].start()
    for copy in copies:
        copy.wait()


def finish(input_grad, first, second):
    wide = jax.ShapeDtypeStruct(first.shape, jnp.float32)
    return pl.pallas_call(
        store,
        out_shape=(jax.ShapeDtypeStruct(input_grad.shape, input_grad.dtype), wide, wide),
        in_specs=[pl.BlockSpec(memory_space=pltpu.VMEM)] * 3,
        out_specs=(ANY,) * 3,
        scratch_shapes=[pltpu.VMEM(first.shape, jnp.float32)] * 2 + [pltpu.SemaphoreType.DMA((3, CHUNKS))],
        compiler_params=pltpu.CompilerParams(vmem_limit_bytes=48 * 2**20),
        name="store",
    )(input_grad, first, second)


def dot(left, right, dims=(((1,), (0,)), ((), ()))):
    return lax.dot_general(left, right, dims, preferred_element_type=jnp.float32)


def factors(scale, order, x, c, w1, w2, ig, gf, gs, w1p, w2p, act, pre):
    bf = jnp.bfloat16
    place = lax.broadcasted_iota(jnp.int32, (B, B), 0)
    spread_one = (place == order[0:1, :]).astype(jnp.float32).astype(bf)
    spread_two = (place == order[1:2, :]).astype(jnp.float32).astype(bf)
    root = math.sqrt(2.0 / math.pi)
    for h in range(4):
        w1p[h] = dot(spread_one, w1[h, 1]).astype(bf)
        w2p[h] = dot(spread_two, w2[h, 1]).astype(bf)
    for h in range(4):
        p, q = h ^ 2, h ^ 1
        v = dot(x[h], w1[h, 0]) + dot(x[p], w1p[h])
        up = dot(c[h], w2[h, 0], NT) + dot(c[q], w2p[q], NT)
        v2 = v * v
        t = jnp.tanh(root * v * (1.0 + 0.044715 * v2))
        half = 0.5 + 0.5 * t
        act[h] = (v * half).astype(bf)
        slope = half + (0.5 * root) * v * (1.0 - t * t) * (1.0 + (3 * 0.044715) * v2)
        pre[h] = (up * slope).astype(bf)
    for h in range(4):
        p, q = h ^ 2, h ^ 1
        ig[h] = (dot(pre[h], w1[h, 0], NT) + dot(pre[p], w1p[p], NT)).astype(bf)
        gf[h, 0] = (dot(x[h], pre[h], TN) * scale).astype(bf)
        cross = (dot(x[p], pre[h], TN) * scale).astype(bf)
        gf[h, 1] = dot(spread_one, cross, TN).astype(bf)
        gs[h, 0] = (dot(act[h], c[h], TN) * scale).astype(bf)
        cross = (dot(act[q], c[h], TN) * scale).astype(bf)
        gs[h, 1] = dot(spread_two, cross, TN).astype(bf)


def shards(plan, inputs, cotangent, first_weight, second_weight, orders):
    tok, width = inputs.shape
    rows = first_weight.shape[2]
    bf = jnp.bfloat16
    all_tok = plan.g * tok
    nq = plan.nq
    scale = 1.0 / math.sqrt(tok * plan.dp)
    dma = pltpu.SemaphoreType.DMA
    n_t, n_w = 4 * plan.g, 4 * plan.dp
    toks = pltpu.VMEM((nq, 4, all_tok, B), bf)
    mats = pltpu.VMEM((nq, 4, 2, B, B), bf)
    part = jax.ShapeDtypeStruct((plan.groups, plan.nb, 2, rows, B), bf)
    input_grad, first, second = pl.pallas_call(
        functools.partial(whole, plan, scale),
        out_shape=(jax.ShapeDtypeStruct((tok, width), bf), part, part),
        in_specs=[pl.BlockSpec(memory_space=pltpu.VMEM)] + [ANY] * 4,
        out_specs=(ANY,) * 3,
        scratch_shapes=[toks, toks, mats, mats, toks, mats, mats]
        + [pltpu.VMEM((4, B, B), bf)] * 2
        + [pltpu.VMEM((4, all_tok, B), bf)] * 2
        + [dma((nq, 2, n_t)), dma((nq, 2, n_t)), dma((nq, 2, n_w)), dma((nq, 2, n_w)), dma((nq, 4))]
        + [dma((nq, n_t)), dma((nq, n_t)), dma((nq, 2, n_w)), dma((nq, 2, n_w)), dma((nq, 3))],
        compiler_params=pltpu.CompilerParams(
            collective_id=0, has_side_effects=True, vmem_limit_bytes=56 * 2**20
        ),
        name="whole",
    )(orders, inputs, cotangent, first_weight, second_weight)
    total = lambda parts: jnp.sum(parts.astype(jnp.float32), axis=0)
    return input_grad, total(first), total(second)


def solution(mesh):
    in_specs = (
        P("dp", "mp"),
        P("dp", "mp"),
        P("mp", None, "dp", None),
        P("mp", None, "dp", None),
        P(),
    )
    out_specs = (P("dp", "mp"), P("mp", None, "dp", None), P("mp", None, "dp", None))

    def body(inputs, *rest):
        sizes = mesh.shape["dp"], mesh.shape["mp"], inputs.shape[1] // B
        plan = Lanes(*sizes)
        if plan.fits:
            return by_lanes(plan, inputs, *rest)
        plan = Plan(*sizes)
        return shards(plan, inputs, *rest)

    return jax.shard_map(body, mesh=mesh, in_specs=in_specs, out_specs=out_specs, check_vma=False)
```

```python
import functools
import math

import jax
import jax.numpy as jnp
from jax import lax
from jax.experimental import pallas as pl
from jax.experimental.pallas import tpu as pltpu
from jax.sharding import PartitionSpec as P

B = 256
CHUNKS = 4
MESH = pl.DeviceIdType.MESH
ANY = pl.BlockSpec(memory_space=pl.ANY)
NT = (((1,), (1,)), ((), ()))
TN = (((0,), (0,)), ((), ()))


class Plan:
    def __init__(self, dp, mp, local_blocks):
        self.dp, self.mp, self.nb = dp, mp, local_blocks
        self.low = mp // 4
        g = max(1, dp // 2)
        while local_blocks % (4 * g):
            g //= 2
        self.g, self.groups = g, dp // g
        self.nq = local_blocks // (4 * g)

    def here(self):
        d, m = lax.axis_index("dp"), lax.axis_index("mp")
        return d, d // self.g, d % self.g, m // self.low, m % self.low


def greet(plan, d, h, lo):
    barrier = pltpu.get_barrier_semaphore()
    others = 4 * plan.dp
    me = d * 4 + h
    for k in range(1, others):
        t = (me + k) % others
        pl.semaphore_signal(
            barrier, inc=1, device_id=(t // 4, (t % 4) * plan.low + lo), device_id_type=MESH
        )
    pl.semaphore_wait(barrier, others - 1)


def sweep(first, last, body):
    lax.fori_loop(first, last, lambda k, _: (body(k), None)[1], None)


def whole(plan, scale, order, x, c, w1, w2, igo, gfo, gso, xb, cb, w1b, w2b, ig, gf, gs, w1p, w2p, act, pre,
          ts, tr, ws, wr, ls, os, orr, gsem, gr, ol):
    d, gi, r, h, lo = plan.here()
    tok, rows, nq = x.shape[0], w1.shape[2], plan.nq
    n_t, n_w = 4 * plan.g, 4 * plan.dp
    me_o, me_w = r * 4 + h, d * 4 + h
    greet(plan, d, h, lo)

    def peer_of_group(t):
        return (gi * plan.g + t // 4, (t % 4) * plan.low + lo)

    def peer_of_all(t):
        return (t // 4, (t % 4) * plan.low + lo)

    def tokens_in(i, a, k):
        t = (me_o + 5 * k) % n_t
        src, dst = ((x, xb), (c, cb))[a]
        s = src.at[:, pl.ds(pl.multiple_of((t * nq + i) * B, B), B)]
        e = dst.at[i, h, pl.ds(pl.multiple_of(r * tok, tok), tok)]
        if isinstance(k, int) and k == 0:
            return pltpu.make_async_copy(s, e, ls.at[i, a])
        return pltpu.make_async_remote_copy(
            s, e, ts.at[i, a, k], tr.at[i, a, k], device_id=peer_of_group(t), device_id_type=MESH
        )

    def weights_in(i, a, k):
        t = (me_w + 11 * k) % n_w
        src, dst = ((w1, w1b), (w2, w2b))[a]
        o = ((t // 4) % plan.g) * 4 + t % 4
        s = src.at[o * nq + i]
        e = dst.at[i, h, :, pl.ds(pl.multiple_of(d * rows, rows), rows)]
        if isinstance(k, int) and k == 0:
            return pltpu.make_async_copy(s, e, ls.at[i, 2 + a])
        return pltpu.make_async_remote_copy(
            s, e, ws.at[i, a, k], wr.at[i, a, k], device_id=peer_of_all(t), device_id_type=MESH
        )

    def tokens_out(i, k):
        t = (me_o + 5 * k) % n_t
        s = ig.at[i, t % 4, pl.ds(pl.multiple_of((t // 4) * tok, tok), tok)]
        e = igo.at[:, pl.ds(pl.multiple_of((me_o * nq + i) * B, B), B)]
        if isinstance(k, int) and k == 0:
            return pltpu.make_async_copy(s, e, ol.at[i, 0])
        return pltpu.make_async_remote_copy(
            s, e, os.at[i, k], orr.at[i, k], device_id=peer_of_group(t), device_id_type=MESH
        )

    def grads_out(i, a, k):
        t = (me_w + 11 * k) % n_w
        src, dst = ((gf, gfo), (gs, gso))[a]
        s = src.at[i, t % 4, :, pl.ds(pl.multiple_of((t // 4) * rows, rows), rows)]
        e = dst.at[gi, me_o * nq + i]
        if isinstance(k, int) and k == 0:
            return pltpu.make_async_copy(s, e, ol.at[i, 1 + a])
        return pltpu.make_async_remote_copy(
            s, e, gsem.at[i, a, k], gr.at[i, a, k], device_id=peer_of_all(t), device_id_type=MESH
        )

    def all_in(i, act_on):
        def some_weights(k, first):
            for j in range(first, plan.groups):
                for a in (0, 1):
                    act_on(weights_in(i, a, plan.groups * k + j))

        def both(k):
            act_on(tokens_in(i, 0, k))
            some_weights(k, 0)
            act_on(tokens_in(i, 1, k))

        some_weights(0, 1)
        sweep(1, n_t, both)

    def all_out(i, act_on):
        def some_grads(k, first):
            for j in range(first, plan.groups):
                for a in (0, 1):
                    act_on(grads_out(i, a, plan.groups * k + j))

        def both(k):
            act_on(tokens_out(i, k))
            some_grads(k, 0)

        some_grads(0, 1)
        sweep(1, n_t, both)

    def own_in(i):
        return [f(i, a, 0) for f in (tokens_in, weights_in) for a in (0, 1)]

    def own_out(i):
        return [tokens_out(i, 0), grads_out(i, 0, 0), grads_out(i, 1, 0)]

    for i in range(nq):
        all_in(i, lambda copy: copy.start())
        for copy in own_in(i):
            copy.start()
    for i in range(nq):
        for copy in own_in(i):
            copy.wait()
        all_in(i, lambda copy: copy.wait_recv())
        factors(scale, order, xb.at[i], cb.at[i], w1b.at[i], w2b.at[i], ig.at[i], gf.at[i], gs.at[i], w1p, w2p, act, pre)
        all_out(i, lambda copy: copy.start())
        for copy in own_out(i):
            copy.start()
    for i in range(nq):
        all_in(i, lambda copy: copy.wait_send())
        for copy in own_out(i):
            copy.wait()
        all_out(i, lambda copy: copy.wait())


class Lanes:
    def __init__(self, dp, mp, local_blocks):
        self.nc = nc = dp // 4
        self.low = mp // 4
        self.ng = local_blocks // (4 * nc) if nc else 0
        self.fits = dp % 4 == 0 and mp % 4 == 0 and self.ng > 0 and local_blocks % (4 * nc) == 0


def lanes(plan, scale, orders, x, c, w1, w2, igo, gfo, gso, order, ordered, xb, cb, w1b, w2b, ig, gf, gs, gif, gis, w1p, w2p, act, pre,
          tin, win, wout, wrel, gin, done, st, sw, sr, si, sg, sf):
    nc, low, ng = plan.nc, plan.low, plan.ng
    tok, rows = x.shape[0], w1.shape[2]
    d, m = lax.axis_index("dp"), lax.axis_index("mp")
    h, lo = m // low, m % low
    quarter, side, core, slot = d // nc, d // (2 * nc), d % nc, d % (2 * nc)
    inner = jnp.logical_or(quarter == 1, quarter == 2)
    outer = jnp.logical_not(inner)
    base, other, far = nc + side * nc, 2 * nc - side * nc, 3 * nc * side
    first, me, us = 2 * nc * side, core * 4 + h, slot * 4 + h
    n_s, n_o = 4 * nc, 8 * nc
    X, W, G, GI, GO = (x, c), (w1, w2), (gf, gs), (gif, gis), (gfo, gso)
    XB, WB = (xb, cb), (w1b, w2b)

    def mp_of(hh):
        return hh * low + lo

    def span(start, size):
        return pl.ds(pl.multiple_of(start * size, size), size)

    def put(src, dst, ssem, rsem, dev):
        return pltpu.make_async_remote_copy(src, dst, ssem, rsem, device_id=dev, device_id_type=MESH)

    def arrived(ref, sem):
        pltpu.make_async_copy(ref, ref, sem).wait()

    barrier = pltpu.get_barrier_semaphore()

    def hello(dev):
        pl.semaphore_signal(barrier, inc=1, device_id=dev, device_id_type=MESH)

    @pl.when(inner)
    def _():
        for cs in range(nc):
            hello((other + cs, m))
        for k in range(1, n_s):
            t = (me + k) % n_s
            hello((base + t // 4, mp_of(t % 4)))
        for cs in range(nc):
            hello((far + cs, m))
        pl.semaphore_wait(barrier, n_s - 1 + nc)

    @pl.when(outer)
    def _():
        for kh in range(1, 4):
            hello((d, mp_of((h + kh) % 4)))
        pl.semaphore_wait(barrier, nc + 3)

    def block_of(a, t, i):
        return W[a].at[t * ng + i]

    def columns_of(a, t, i):
        return X[a].at[:, span(t * ng + i, B)]

    def own_w(i, a, k):
        t = (me + k) % n_s
        e = WB[a].at[i, h, :, span(d, rows)]
        if isinstance(k, int) and k == 0:
            return pltpu.make_async_copy(block_of(a, t, i), e, win.at[i, a, h])
        return put(block_of(a, t, i), e, sw.at[0, a], win.at[i, a, h], (base + t // 4, mp_of(t % 4)))

    def cross_w(i, a, cs):
        e = WB[a].at[i, h, :, span(d, rows)]
        return put(block_of(a, cs * 4 + h, i), e, sw.at[1, a], wrel.at[i, a], (other + cs, m))

    def own_t(i, a, k):
        t = (me + k) % n_s
        e = XB[a].at[i, h, span(slot, tok)]
        if isinstance(k, int) and k == 0:
            return pltpu.make_async_copy(columns_of(a, t, i), e, tin.at[i, a])
        return put(columns_of(a, t, i), e, st.at[0, a], tin.at[i, a], (base + t // 4, mp_of(t % 4)))

    def plane_w(i, a, cs, kh):
        hh = (h + kh) % 4
        s, e = block_of(a, cs * 4 + hh, i), WB[a].at[i, h, :, span(cs, rows)]
        if kh == 0:
            return pltpu.make_async_copy(s, e, wout.at[i, a])
        return put(s, e, sw.at[0, a], wout.at[i, a], (d, mp_of(hh)))

    def plane_t(i, a, cs, kh):
        hh = (h + kh) % 4
        s, e = columns_of(a, cs * 4 + hh, i), XB[a].at[i, h, span(cs, tok)]
        if kh == 0:
            return pltpu.make_async_copy(s, e, tin.at[i, a])
        return put(s, e, st.at[0, a], tin.at[i, a], (d, mp_of(hh)))

    def up_w(i, a, cs):
        s, e = WB[a].at[i, :, :, span(cs, rows)], WB[a].at[i, :, :, span(d, rows)]
        return put(s, e, sw.at[1, a], wout.at[i, a], (base + cs, m))

    def up_t(i, a, cs):
        s, e = XB[a].at[i, :, span(cs, tok)], XB[a].at[i, :, span(slot, tok)]
        return put(s, e, st.at[1, a], tin.at[i, a], (base + cs, m))

    def relay_in(i, a, kh):
        s = WB[a].at[i, (h + kh) % 4, :, span(base // nc, nc * rows)]
        return put(s, s, sr.at[0, a], wrel.at[i, a], (other + core, m))

    def relay_out(i, a):
        s = WB[a].at[i, :, :, span(far // nc, nc * rows)]
        return put(s, s, sr.at[1, a], wrel.at[i, a], (other + core, m))

    def tokens_out(i, k, more=0):
        u = (us + k) % n_o
        s, e = ig.at[i, u % 4, span(u // 4, tok)], igo.at[:, span(me * ng + i, B)]
        if isinstance(k, int) and k == 0:
            return pltpu.make_async_copy(s, e, done.at[0])
        return put(s, e, si.at[more], done.at[0], (first + u // 4, mp_of(u % 4)))

    def partial(i, a, kh, near):
        hh, theirs = (h + kh) % 4, other // nc if near else 3 - far // nc
        s = G[a].at[i, hh, :, span(theirs, nc * rows)]
        return put(s, GI[a].at[i, hh, near], sg.at[a], gin.at[i, a, kh, near], (other + core, m))

    def grads_out(i, a, kh, near, k):
        hh, cs = (h + kh) % 4, (core + k) % nc
        s, e = GI[a].at[i, hh, near, :, span(cs, rows)], GO[a].at[me * ng + i]
        if near and kh == 0 and k == 0:
            return pltpu.make_async_copy(s, e, done.at[1 + a])
        return put(s, e, sf.at[near, a], done.at[1 + a], ((base if near else far) + cs, mp_of(hh)))

    parts = [(a, kh, near) for near in (0, 1) for kh in (1, 2, 3, 0) for a in (0, 1)]

    def both(f, *at):
        return [f(at[0], a, *at[1:]) for a in (0, 1)]

    def begin(copies):
        for copy in copies:
            copy.start()

    def combine(i):
        for a, kh, near in parts:
            hh = (h + kh) % 4
            arrived(GI[a].at[i, hh, near], gin.at[i, a, kh, near])
            ours = base // nc if near else far // nc
            mine = G[a][i, hh, :, span(ours, nc * rows)].astype(jnp.float32)
            GI[a][i, hh, near] = (mine + GI[a][i, hh, near].astype(jnp.float32)).astype(jnp.bfloat16)
            begin([grads_out(i, a, kh, near, k) for k in range(nc)])

    @pl.when(inner)
    def _():
        for i in range(ng):
            for cs in range(nc):
                begin(both(cross_w, i, cs))
        pltpu.make_async_copy(orders, order, ordered).start()
        for i in range(ng):
            sweep(1, n_s, lambda k: begin(both(own_w, i, k)))
            begin(both(own_w, i, 0))
        for i in range(ng):
            sweep(1, n_s, lambda k: begin(both(own_t, i, k)))
            begin(both(own_t, i, 0))
        for i in range(ng):
            for kh in range(4):
                for a in (0, 1):
                    hh = (h + kh) % 4
                    arrived(WB[a].at[i, hh, :, span(base // nc, nc * rows)], win.at[i, a, hh])
                    if kh:
                        relay_in(i, a, kh).start()
        for i in range(ng):
            for a in (0, 1):
                arrived(WB[a].at[i, :, :, span(far // nc, nc * rows)], wout.at[i, a])
                relay_out(i, a).start()
        arrived(order, ordered)
        for i in range(ng):
            for a in (0, 1):
                arrived(WB[a].at[i, :, :, span(1 - side, 2 * nc * rows)], wrel.at[i, a])
                arrived(XB[a].at[i], tin.at[i, a])
            factors(scale, order, xb.at[i], cb.at[i], w1b.at[i], w2b.at[i], ig.at[i], gf.at[i], gs.at[i], w1p, w2p, act, pre)
            begin([partial(i, *at) for at in parts])
            sweep(1, n_s, lambda k: tokens_out(i, k).start())
            sweep(n_s, n_o, lambda k: tokens_out(i, k, 1).start())
            tokens_out(i, 0).start()
            if i >= 1:
                combine(i - 1)
        combine(ng - 1)
        some = ng * (n_s - 1)
        arrived(igo.at[:, pl.ds(0, some * B)], si.at[0])
        arrived(igo, si.at[1])
        for a in (0, 1):
            arrived(X[a].at[:, pl.ds(0, some * B)], st.at[0, a])
            arrived(W[a].at[pl.ds(0, some)], sw.at[0, a])
            arrived(W[a].at[pl.ds(0, ng * nc)], sw.at[1, a])
            arrived(WB[a].at[:, pl.ds(0, 3), :, pl.ds(0, nc * rows)], sr.at[0, a])
            arrived(WB[a].at[:, :, :, pl.ds(0, nc * rows)], sr.at[1, a])
            arrived(GI[a], sg.at[a])
            arrived(GO[a], sf.at[0, a])
            arrived(GO[a].at[pl.ds(0, some)], sf.at[1, a])

    @pl.when(outer)
    def _():
        for i in range(ng):
            for kh in (1, 2, 3, 0):
                for cs in range(nc):
                    begin(both(plane_w, i, cs, kh))
        for i in range(ng):
            for kh in (1, 2, 3, 0):
                for cs in range(nc):
                    begin(both(plane_t, i, cs, kh))
        for i in range(ng):
            for a in (0, 1):
                arrived(WB[a].at[i, :, :, span(0, nc * rows)], wout.at[i, a])
                begin([up_w(i, a, cs) for cs in range(nc)])
        for i in range(ng):
            for a in (0, 1):
                arrived(XB[a].at[i, :, span(0, nc * tok)], tin.at[i, a])
                begin([up_t(i, a, cs) for cs in range(nc)])
        for a in (0, 1):
            arrived(W[a].at[pl.ds(0, 3 * ng * nc)], sw.at[0, a])
            arrived(X[a].at[:, pl.ds(0, 3 * ng * nc * B)], st.at[0, a])
            arrived(W[a], sw.at[1, a])
            arrived(X[a], st.at[1, a])

    arrived(igo, done.at[0])
    arrived(gfo, done.at[1])
    arrived(gso, done.at[2])


def by_lanes(plan, inputs, cotangent, first_weight, second_weight, orders):
    tok, width = inputs.shape
    rows = first_weight.shape[2]
    nc, ng, bf = plan.nc, plan.ng, jnp.bfloat16
    scale = 1.0 / math.sqrt(tok * 4 * nc)
    dma = pltpu.SemaphoreType.DMA
    toks = pltpu.VMEM((ng, 4, 2 * nc * tok, B), bf)
    mats = pltpu.VMEM((ng, 4, 2, B, B), bf)
    half = pltpu.VMEM((ng, 4, 2, 2, nc * rows, B), bf)
    part = pltpu.VMEM(first_weight.shape, bf)
    input_grad, first, second = pl.pallas_call(
        functools.partial(lanes, plan, scale),
        out_shape=(pltpu.VMEM((tok, width), bf), part, part),
        in_specs=[ANY] * 5,
        out_specs=(ANY,) * 3,
        scratch_shapes=[pltpu.VMEM(orders.shape, orders.dtype), dma]
        + [toks, toks, mats, mats, toks, mats, mats, half, half]
        + [pltpu.VMEM((4, B, B), bf)] * 2
        + [pltpu.VMEM((4, 2 * nc * tok, B), bf)] * 2
        + [dma((ng, 2)), dma((ng, 2, 4)), dma((ng, 2)), dma((ng, 2)), dma((ng, 2, 4, 2)), dma((3,))]
        + [dma((2, 2))] * 3 + [dma((2,))] * 2 + [dma((2, 2))],
        compiler_params=pltpu.CompilerParams(
            collective_id=0, has_side_effects=True, vmem_limit_bytes=58 * 2**20
        ),
        name="lanes",
    )(orders, inputs, cotangent, first_weight, second_weight)
    return finish(input_grad, first, second)


def store(ig, first, second, igo, fo, so, fw, sw, sems):
    copies = [pltpu.make_async_copy(ig, igo, sems.at[0, 0])]
    copies[0].start()
    size = max(1, first.shape[0] // CHUNKS)
    for n, at in enumerate(range(0, first.shape[0], size)):
        for a, (src, wide, dst) in enumerate(((first, fw, fo), (second, sw, so))):
            rows = pl.ds(at, size)
            wide[rows] = src[rows].astype(jnp.float32)
            copies.append(pltpu.make_async_copy(wide.at[rows], dst.at[rows], sems.at[1 + a, n]))
            copies[-1].start()
    for copy in copies:
        copy.wait()


def finish(input_grad, first, second):
    wide = jax.ShapeDtypeStruct(first.shape, jnp.float32)
    return pl.pallas_call(
        store,
        out_shape=(jax.ShapeDtypeStruct(input_grad.shape, input_grad.dtype), wide, wide),
        in_specs=[pl.BlockSpec(memory_space=pltpu.VMEM)] * 3,
        out_specs=(ANY,) * 3,
        scratch_shapes=[pltpu.VMEM(first.shape, jnp.float32)] * 2 + [pltpu.SemaphoreType.DMA((3, CHUNKS))],
        compiler_params=pltpu.CompilerParams(vmem_limit_bytes=48 * 2**20),
        name="store",
    )(input_grad, first, second)


def dot(left, right, dims=(((1,), (0,)), ((), ()))):
    return lax.dot_general(left, right, dims, preferred_element_type=jnp.float32)


def factors(scale, order, x, c, w1, w2, ig, gf, gs, w1p, w2p, act, pre):
    bf = jnp.bfloat16
    place = lax.broadcasted_iota(jnp.int32, (B, B), 0)
    spread_one = (place == order[0:1, :]).astype(jnp.float32).astype(bf)
    spread_two = (place == order[1:2, :]).astype(jnp.float32).astype(bf)
    root = math.sqrt(2.0 / math.pi)
    for h in range(4):
        w1p[h] = dot(spread_one, w1[h, 1]).astype(bf)
        w2p[h] = dot(spread_two, w2[h, 1]).astype(bf)
    for h in range(4):
        p, q = h ^ 2, h ^ 1
        v = dot(x[h], w1[h, 0]) + dot(x[p], w1p[h])
        up = dot(c[h], w2[h, 0], NT) + dot(c[q], w2p[q], NT)
        v2 = v * v
        t = jnp.tanh(root * v * (1.0 + 0.044715 * v2))
        half = 0.5 + 0.5 * t
        act[h] = (v * half).astype(bf)
        slope = half + (0.5 * root) * v * (1.0 - t * t) * (1.0 + (3 * 0.044715) * v2)
        pre[h] = (up * slope).astype(bf)
    for h in range(4):
        p, q = h ^ 2, h ^ 1
        ig[h] = (dot(pre[h], w1[h, 0], NT) + dot(pre[p], w1p[p], NT)).astype(bf)
        gf[h, 0] = (dot(x[h], pre[h], TN) * scale).astype(bf)
        cross = (dot(x[p], pre[h], TN) * scale).astype(bf)
        gf[h, 1] = dot(spread_one, cross, TN).astype(bf)
        gs[h, 0] = (dot(act[h], c[h], TN) * scale).astype(bf)
        cross = (dot(act[q], c[h], TN) * scale).astype(bf)
        gs[h, 1] = dot(spread_two, cross, TN).astype(bf)


def shards(plan, inputs, cotangent, first_weight, second_weight, orders):
    tok, width = inputs.shape
    rows = first_weight.shape[2]
    bf = jnp.bfloat16
    all_tok = plan.g * tok
    nq = plan.nq
    scale = 1.0 / math.sqrt(tok * plan.dp)
    dma = pltpu.SemaphoreType.DMA
    n_t, n_w = 4 * plan.g, 4 * plan.dp
    toks = pltpu.VMEM((nq, 4, all_tok, B), bf)
    mats = pltpu.VMEM((nq, 4, 2, B, B), bf)
    part = jax.ShapeDtypeStruct((plan.groups, plan.nb, 2, rows, B), bf)
    input_grad, first, second = pl.pallas_call(
        functools.partial(whole, plan, scale),
        out_shape=(jax.ShapeDtypeStruct((tok, width), bf), part, part),
        in_specs=[pl.BlockSpec(memory_space=pltpu.VMEM)] + [ANY] * 4,
        out_specs=(ANY,) * 3,
        scratch_shapes=[toks, toks, mats, mats, toks, mats, mats]
        + [pltpu.VMEM((4, B, B), bf)] * 2
        + [pltpu.VMEM((4, all_tok, B), bf)] * 2
        + [dma((nq, 2, n_t)), dma((nq, 2, n_t)), dma((nq, 2, n_w)), dma((nq, 2, n_w)), dma((nq, 4))]
        + [dma((nq, n_t)), dma((nq, n_t)), dma((nq, 2, n_w)), dma((nq, 2, n_w)), dma((nq, 3))],
        compiler_params=pltpu.CompilerParams(
            collective_id=0, has_side_effects=True, vmem_limit_bytes=56 * 2**20
        ),
        name="whole",
    )(orders, inputs, cotangent, first_weight, second_weight)
    total = lambda parts: jnp.sum(parts.astype(jnp.float32), axis=0)
    return input_grad, total(first), total(second)


def solution(mesh):
    in_specs = (
        P("dp", "mp"),
        P("dp", "mp"),
        P("mp", None, "dp", None),
        P("mp", None, "dp", None),
        P(),
    )
    out_specs = (P("dp", "mp"), P("mp", None, "dp", None), P("mp", None, "dp", None))

    def body(inputs, *rest):
        sizes = mesh.shape["dp"], mesh.shape["mp"], inputs.shape[1] // B
        plan = Lanes(*sizes)
        if plan.fits:
            return by_lanes(plan, inputs, *rest)
        plan = Plan(*sizes)
        return shards(plan, inputs, *rest)

    return jax.shard_map(body, mesh=mesh, in_specs=in_specs, out_specs=out_specs, check_vma=False)
```

```python
import functools
import math

import jax
import jax.numpy as jnp
from jax import lax
from jax.experimental import pallas as pl
from jax.experimental.pallas import tpu as pltpu
from jax.sharding import PartitionSpec as P

B = 256
CHUNKS = 4
MESH = pl.DeviceIdType.MESH
ANY = pl.BlockSpec(memory_space=pl.ANY)
NT = (((1,), (1,)), ((), ()))
TN = (((0,), (0,)), ((), ()))


class Plan:
    def __init__(self, dp, mp, local_blocks):
        self.dp, self.mp, self.nb = dp, mp, local_blocks
        self.low = mp // 4
        g = max(1, dp // 2)
        while local_blocks % (4 * g):
            g //= 2
        self.g, self.groups = g, dp // g
        self.nq = local_blocks // (4 * g)

    def here(self):
        d, m = lax.axis_index("dp"), lax.axis_index("mp")
        return d, d // self.g, d % self.g, m // self.low, m % self.low


def greet(plan, d, h, lo):
    barrier = pltpu.get_barrier_semaphore()
    others = 4 * plan.dp
    me = d * 4 + h
    for k in range(1, others):
        t = (me + k) % others
        pl.semaphore_signal(
            barrier, inc=1, device_id=(t // 4, (t % 4) * plan.low + lo), device_id_type=MESH
        )
    pl.semaphore_wait(barrier, others - 1)


def sweep(first, last, body):
    lax.fori_loop(first, last, lambda k, _: (body(k), None)[1], None)


def whole(plan, scale, order, x, c, w1, w2, igo, gfo, gso, xb, cb, w1b, w2b, ig, gf, gs, w1p, w2p, act, pre,
          ts, tr, ws, wr, ls, os, orr, gsem, gr, ol):
    d, gi, r, h, lo = plan.here()
    tok, rows, nq = x.shape[0], w1.shape[2], plan.nq
    n_t, n_w = 4 * plan.g, 4 * plan.dp
    me_o, me_w = r * 4 + h, d * 4 + h
    greet(plan, d, h, lo)

    def peer_of_group(t):
        return (gi * plan.g + t // 4, (t % 4) * plan.low + lo)

    def peer_of_all(t):
        return (t // 4, (t % 4) * plan.low + lo)

    def tokens_in(i, a, k):
        t = (me_o + 5 * k) % n_t
        src, dst = ((x, xb), (c, cb))[a]
        s = src.at[:, pl.ds(pl.multiple_of((t * nq + i) * B, B), B)]
        e = dst.at[i, h, pl.ds(pl.multiple_of(r * tok, tok), tok)]
        if isinstance(k, int) and k == 0:
            return pltpu.make_async_copy(s, e, ls.at[i, a])
        return pltpu.make_async_remote_copy(
            s, e, ts.at[i, a, k], tr.at[i, a, k], device_id=peer_of_group(t), device_id_type=MESH
        )

    def weights_in(i, a, k):
        t = (me_w + 11 * k) % n_w
        src, dst = ((w1, w1b), (w2, w2b))[a]
        o = ((t // 4) % plan.g) * 4 + t % 4
        s = src.at[o * nq + i]
        e = dst.at[i, h, :, pl.ds(pl.multiple_of(d * rows, rows), rows)]
        if isinstance(k, int) and k == 0:
            return pltpu.make_async_copy(s, e, ls.at[i, 2 + a])
        return pltpu.make_async_remote_copy(
            s, e, ws.at[i, a, k], wr.at[i, a, k], device_id=peer_of_all(t), device_id_type=MESH
        )

    def tokens_out(i, k):
        t = (me_o + 5 * k) % n_t
        s = ig.at[i, t % 4, pl.ds(pl.multiple_of((t // 4) * tok, tok), tok)]
        e = igo.at[:, pl.ds(pl.multiple_of((me_o * nq + i) * B, B), B)]
        if isinstance(k, int) and k == 0:
            return pltpu.make_async_copy(s, e, ol.at[i, 0])
        return pltpu.make_async_remote_copy(
            s, e, os.at[i, k], orr.at[i, k], device_id=peer_of_group(t), device_id_type=MESH
        )

    def grads_out(i, a, k):
        t = (me_w + 11 * k) % n_w
        src, dst = ((gf, gfo), (gs, gso))[a]
        s = src.at[i, t % 4, :, pl.ds(pl.multiple_of((t // 4) * rows, rows), rows)]
        e = dst.at[gi, me_o * nq + i]
        if isinstance(k, int) and k == 0:
            return pltpu.make_async_copy(s, e, ol.at[i, 1 + a])
        return pltpu.make_async_remote_copy(
            s, e, gsem.at[i, a, k], gr.at[i, a, k], device_id=peer_of_all(t), device_id_type=MESH
        )

    def all_in(i, act_on):
        def some_weights(k, first):
            for j in range(first, plan.groups):
                for a in (0, 1):
                    act_on(weights_in(i, a, plan.groups * k + j))

        def both(k):
            act_on(tokens_in(i, 0, k))
            some_weights(k, 0)
            act_on(tokens_in(i, 1, k))

        some_weights(0, 1)
        sweep(1, n_t, both)

    def all_out(i, act_on):
        def some_grads(k, first):
            for j in range(first, plan.groups):
                for a in (0, 1):
                    act_on(grads_out(i, a, plan.groups * k + j))

        def both(k):
            act_on(tokens_out(i, k))
            some_grads(k, 0)

        some_grads(0, 1)
        sweep(1, n_t, both)

    def own_in(i):
        return [f(i, a, 0) for f in (tokens_in, weights_in) for a in (0, 1)]

    def own_out(i):
        return [tokens_out(i, 0), grads_out(i, 0, 0), grads_out(i, 1, 0)]

    for i in range(nq):
        all_in(i, lambda copy: copy.start())
        for copy in own_in(i):
            copy.start()
    for i in range(nq):
        for copy in own_in(i):
            copy.wait()
        all_in(i, lambda copy: copy.wait_recv())
        factors(scale, order, xb.at[i], cb.at[i], w1b.at[i], w2b.at[i], ig.at[i], gf.at[i], gs.at[i], w1p, w2p, act, pre)
        all_out(i, lambda copy: copy.start())
        for copy in own_out(i):
            copy.start()
    for i in range(nq):
        all_in(i, lambda copy: copy.wait_send())
        for copy in own_out(i):
            copy.wait()
        all_out(i, lambda copy: copy.wait())


class Lanes:
    def __init__(self, dp, mp, local_blocks):
        self.nc = nc = dp // 4
        self.low = mp // 4
        self.ng = local_blocks // (4 * nc) if nc else 0
        self.fits = dp % 4 == 0 and mp % 4 == 0 and self.ng > 0 and local_blocks % (4 * nc) == 0


def lanes(plan, scale, orders, x, c, w1, w2, igo, go, order, ordered, xc, wb, ig, g, gi, w1p, w2p, act, pre,
          tin, win, wout, wrel, gin, done, st, sw, sr, si, sg, sf):
    nc, low, ng = plan.nc, plan.low, plan.ng
    tok, rows = x.shape[0], w1.shape[2]
    d, m = lax.axis_index("dp"), lax.axis_index("mp")
    h, lo = m // low, m % low
    quarter, side, core, slot = d // nc, d // (2 * nc), d % nc, d % (2 * nc)
    inner = jnp.logical_or(quarter == 1, quarter == 2)
    outer = jnp.logical_not(inner)
    base, other, far = nc + side * nc, 2 * nc - side * nc, 3 * nc * side
    first, me, us = 2 * nc * side, core * 4 + h, slot * 4 + h
    n_s, n_o = 4 * nc, 8 * nc
    X, W = (x, c), (w1, w2)

    def mp_of(hh):
        return hh * low + lo

    def span(start, size):
        return pl.ds(pl.multiple_of(start * size, size), size)

    def put(src, dst, ssem, rsem, dev):
        return pltpu.make_async_remote_copy(src, dst, ssem, rsem, device_id=dev, device_id_type=MESH)

    def arrived(ref, sem):
        pltpu.make_async_copy(ref, ref, sem).wait()

    barrier = pltpu.get_barrier_semaphore()

    def hello(dev):
        pl.semaphore_signal(barrier, inc=1, device_id=dev, device_id_type=MESH)

    @pl.when(inner)
    def _():
        for cs in range(nc):
            hello((other + cs, m))
        for k in range(1, n_s):
            t = (me + k) % n_s
            hello((base + t // 4, mp_of(t % 4)))
        for cs in range(nc):
            hello((far + cs, m))
        pl.semaphore_wait(barrier, n_s - 1 + nc)

    @pl.when(outer)
    def _():
        for kh in range(1, 4):
            hello((d, mp_of((h + kh) % 4)))
        pl.semaphore_wait(barrier, nc + 3)

    def block_of(a, t, i):
        return W[a].at[t * ng + i]

    def columns_of(a, t, i):
        return X[a].at[:, span(t * ng + i, B)]

    def own_w(i, a, k):
        t = (me + k) % n_s
        e, arrival = wb.at[i, h, pl.ds(2 * a, 2), span(d, rows)], win.at[3 + i if i else h]
        if isinstance(k, int) and k == 0:
            return pltpu.make_async_copy(block_of(a, t, i), e, arrival)
        return put(block_of(a, t, i), e, sw.at[0, a], arrival, (base + t // 4, mp_of(t % 4)))

    def cross_w(i, a, cs):
        e = wb.at[i, h, pl.ds(2 * a, 2), span(d, rows)]
        return put(block_of(a, cs * 4 + h, i), e, sw.at[1, a], wrel.at[i], (other + cs, m))

    def own_t(i, a, k):
        t = (me + k) % n_s
        e = xc.at[i, a, h, span(slot, tok)]
        if isinstance(k, int) and k == 0:
            return pltpu.make_async_copy(columns_of(a, t, i), e, tin.at[i])
        return put(columns_of(a, t, i), e, st.at[a], tin.at[i], (base + t // 4, mp_of(t % 4)))

    def plane_w(i, a, cs, kh):
        hh = (h + kh) % 4
        s, e = block_of(a, cs * 4 + hh, i), wb.at[i, h, pl.ds(2 * a, 2), span(cs, rows)]
        if kh == 0:
            return pltpu.make_async_copy(s, e, wout.at[i])
        return put(s, e, sw.at[0, a], wout.at[i], (d, mp_of(hh)))

    def plane_t(i, a, cs, kh):
        hh = (h + kh) % 4
        s, e = columns_of(a, cs * 4 + hh, i), xc.at[i, a, h, span(cs, tok)]
        if kh == 0:
            return pltpu.make_async_copy(s, e, tin.at[i])
        return put(s, e, st.at[a], tin.at[i], (d, mp_of(hh)))

    def up_w(i, cs):
        s, e = wb.at[i, :, :, span(cs, rows)], wb.at[i, :, :, span(d, rows)]
        return put(s, e, sr.at[0], wout.at[i], (base + cs, m))

    def up_t(i, cs):
        s, e = xc.at[i, :, :, span(cs, tok)], xc.at[i, :, :, span(slot, tok)]
        return put(s, e, sr.at[1], tin.at[i], (base + cs, m))

    def relay_in(i, kh):
        s = wb.at[i, (h + kh) % 4, :, span(base // nc, nc * rows)]
        return put(s, s, sr.at[0], wrel.at[i], (other + core, m))

    def relay_out(i):
        s = wb.at[i, :, :, span(far // nc, nc * rows)]
        return put(s, s, sr.at[1], wrel.at[i], (other + core, m))

    def tokens_out(i, k, more=0):
        u = (us + k) % n_o
        s, e = ig.at[i, u % 4, span(u // 4, tok)], igo.at[:, span(me * ng + i, B)]
        if isinstance(k, int) and k == 0:
            return pltpu.make_async_copy(s, e, done.at[0])
        return put(s, e, si.at[more], done.at[0], (first + u // 4, mp_of(u % 4)))

    def sums(i, kh, near):
        return gin.at[2 * i + near if i < ng - 1 else 2 * i + 4 * near + kh]

    def partial(i, kh, near):
        hh, theirs = (h + kh) % 4, other // nc if near else 3 - far // nc
        s = g.at[i, hh, :, span(theirs, nc * rows)]
        return put(s, gi.at[i, near, hh], sg, sums(i, kh, near), (other + core, m))

    def grads_out(i, kh, near, k):
        hh, cs = (h + kh) % 4, (core + k) % nc
        s, e = gi.at[i, near, hh, :, span(cs, rows)], go.at[me * ng + i]
        if near and kh == 0 and k == 0:
            return pltpu.make_async_copy(s, e, done.at[1])
        return put(s, e, sf.at[near], done.at[1], ((base if near else far) + cs, mp_of(hh)))

    lasts = (1, 2, 3, 0)

    def both(f, *at):
        return [f(at[0], a, *at[1:]) for a in (0, 1)]

    def begin(copies):
        for copy in copies:
            copy.start()

    def combine(i):
        for near in (0, 1):
            if i < ng - 1:
                arrived(gi.at[i, near], sums(i, 0, near))
            for kh in lasts:
                hh = (h + kh) % 4
                if i == ng - 1:
                    arrived(gi.at[i, near, hh], sums(i, kh, near))
                ours = base // nc if near else far // nc
                mine = g[i, hh, :, span(ours, nc * rows)].astype(jnp.float32)
                gi[i, near, hh] = (mine + gi[i, near, hh].astype(jnp.float32)).astype(jnp.bfloat16)
                begin([grads_out(i, kh, near, k) for k in range(nc)])

    @pl.when(inner)
    def _():
        for i in range(ng):
            for cs in range(nc):
                begin(both(cross_w, i, cs))
        pltpu.make_async_copy(orders, order, ordered).start()
        for i in range(ng):
            sweep(1, n_s, lambda k: begin(both(own_w, i, k)))
            begin(both(own_w, i, 0))
        for i in range(ng):
            sweep(1, n_s, lambda k: begin(both(own_t, i, k)))
            begin(both(own_t, i, 0))
        for i in range(ng):
            rest = span(base // nc, nc * rows)
            if i:
                arrived(wb.at[i, :, :, rest], win.at[3 + i])
            for kh in range(4):
                if i == 0:
                    arrived(wb.at[i, (h + kh) % 4, :, rest], win.at[(h + kh) % 4])
                if kh:
                    relay_in(i, kh).start()
        for i in range(ng):
            arrived(wb.at[i, :, :, span(far // nc, nc * rows)], wout.at[i])
            relay_out(i).start()
        arrived(order, ordered)
        for i in range(ng):
            arrived(wb.at[i, :, :, span(1 - side, 2 * nc * rows)], wrel.at[i])
            arrived(xc.at[i], tin.at[i])
            w1b, w2b = wb.at[i, :, pl.ds(0, 2)], wb.at[i, :, pl.ds(2, 2)]
            gf, gs = g.at[i, :, pl.ds(0, 2)], g.at[i, :, pl.ds(2, 2)]
            factors(scale, order, xc.at[i, 0], xc.at[i, 1], w1b, w2b, ig.at[i], gf, gs, w1p, w2p, act, pre)
            begin([partial(i, kh, near) for near in (0, 1) for kh in lasts])
            sweep(1, n_s, lambda k: tokens_out(i, k).start())
            sweep(n_s, n_o, lambda k: tokens_out(i, k, 1).start())
            tokens_out(i, 0).start()
            if i >= 1:
                combine(i - 1)
        combine(ng - 1)
        some = ng * (n_s - 1)
        arrived(igo.at[:, pl.ds(0, some * B)], si.at[0])
        arrived(igo, si.at[1])
        for a in (0, 1):
            arrived(X[a].at[:, pl.ds(0, some * B)], st.at[a])
            arrived(W[a].at[pl.ds(0, some)], sw.at[0, a])
            arrived(W[a].at[pl.ds(0, ng * nc)], sw.at[1, a])
        arrived(wb.at[:, pl.ds(0, 3), :, pl.ds(0, nc * rows)], sr.at[0])
        arrived(wb.at[:, :, :, pl.ds(0, nc * rows)], sr.at[1])
        arrived(gi, sg)
        arrived(go, sf.at[0])
        arrived(go.at[pl.ds(0, some)], sf.at[1])

    @pl.when(outer)
    def _():
        for i in range(ng):
            for kh in (1, 2, 3, 0):
                for cs in range(nc):
                    begin(both(plane_w, i, cs, kh))
        for i in range(ng):
            for kh in (1, 2, 3, 0):
                for cs in range(nc):
                    begin(both(plane_t, i, cs, kh))
        for i in range(ng):
            arrived(wb.at[i, :, :, span(0, nc * rows)], wout.at[i])
            begin([up_w(i, cs) for cs in range(nc)])
        for i in range(ng):
            arrived(xc.at[i, :, :, span(0, nc * tok)], tin.at[i])
            begin([up_t(i, cs) for cs in range(nc)])
        for a in (0, 1):
            arrived(W[a].at[pl.ds(0, 3 * ng * nc)], sw.at[0, a])
            arrived(X[a].at[:, pl.ds(0, 3 * ng * nc * B)], st.at[a])
        arrived(go, sr.at[0])
        arrived(xc.at[:, :, :, pl.ds(0, nc * tok)], sr.at[1])

    arrived(igo, done.at[0])
    arrived(go, done.at[1])


def by_lanes(plan, inputs, cotangent, first_weight, second_weight, orders):
    tok, width = inputs.shape
    rows = first_weight.shape[2]
    nc, ng, bf = plan.nc, plan.ng, jnp.bfloat16
    scale = 1.0 / math.sqrt(tok * 4 * nc)
    dma = pltpu.SemaphoreType.DMA
    all_tok = 2 * nc * tok
    mats = pltpu.VMEM((ng, 4, 4, B, B), bf)
    input_grad, sums = pl.pallas_call(
        functools.partial(lanes, plan, scale),
        out_shape=(pltpu.VMEM((tok, width), bf), pltpu.VMEM((4 * nc * ng, 4, rows, B), bf)),
        in_specs=[ANY] * 5,
        out_specs=(ANY,) * 2,
        scratch_shapes=[pltpu.VMEM(orders.shape, orders.dtype), dma]
        + [pltpu.VMEM((ng, 2, 4, all_tok, B), bf), mats]
        + [pltpu.VMEM((ng, 4, all_tok, B), bf), mats, pltpu.VMEM((ng, 2, 4, 4, nc * rows, B), bf)]
        + [pltpu.VMEM((4, B, B), bf)] * 2
        + [pltpu.VMEM((4, all_tok, B), bf)] * 2
        + [dma((ng,)), dma((ng + 3,)), dma((ng,)), dma((ng,)), dma((2 * ng + 6,)), dma((2,))]
        + [dma((2,)), dma((2, 2)), dma((2,)), dma((2,)), dma, dma((2,))],
        compiler_params=pltpu.CompilerParams(
            collective_id=0, has_side_effects=True, vmem_limit_bytes=58 * 2**20
        ),
        name="lanes",
    )(orders, inputs, cotangent, first_weight, second_weight)
    return finish(input_grad, sums)


def store(ig, sums, igo, fo, so, fw, sw, sems):
    copies = [pltpu.make_async_copy(ig, igo, sems.at[0, 0])]
    copies[0].start()
    size = max(1, sums.shape[0] // CHUNKS)
    for n, at in enumerate(range(0, sums.shape[0], size)):
        for a, (wide, dst) in enumerate(((fw, fo), (sw, so))):
            rows = pl.ds(at, size)
            wide[rows] = sums[rows, pl.ds(2 * a, 2)].astype(jnp.float32)
            copies.append(pltpu.make_async_copy(wide.at[rows], dst.at[rows], sems.at[1 + a, n]))
            copies[-1].start()
    for copy in copies:
        copy.wait()


def finish(input_grad, sums):
    nb, _, rows, width = sums.shape
    wide = (nb, 2, rows, width)
    out = jax.ShapeDtypeStruct(wide, jnp.float32)
    return pl.pallas_call(
        store,
        out_shape=(jax.ShapeDtypeStruct(input_grad.shape, input_grad.dtype), out, out),
        in_specs=[pl.BlockSpec(memory_space=pltpu.VMEM)] * 2,
        out_specs=(ANY,) * 3,
        scratch_shapes=[pltpu.VMEM(wide, jnp.float32)] * 2 + [pltpu.SemaphoreType.DMA((3, CHUNKS))],
        compiler_params=pltpu.CompilerParams(vmem_limit_bytes=48 * 2**20),
        name="store",
    )(input_grad, sums)


def dot(left, right, dims=(((1,), (0,)), ((), ()))):
    return lax.dot_general(left, right, dims, preferred_element_type=jnp.float32)


def factors(scale, order, x, c, w1, w2, ig, gf, gs, w1p, w2p, act, pre):
    bf = jnp.bfloat16
    place = lax.broadcasted_iota(jnp.int32, (B, B), 0)
    spread_one = (place == order[0:1, :]).astype(jnp.float32).astype(bf)
    spread_two = (place == order[1:2, :]).astype(jnp.float32).astype(bf)
    root = math.sqrt(2.0 / math.pi)
    for h in range(4):
        w1p[h] = dot(spread_one, w1[h, 1]).astype(bf)
        w2p[h] = dot(spread_two, w2[h, 1]).astype(bf)
    for h in range(4):
        p, q = h ^ 2, h ^ 1
        v = dot(x[h], w1[h, 0]) + dot(x[p], w1p[h])
        up = dot(c[h], w2[h, 0], NT) + dot(c[q], w2p[q], NT)
        v2 = v * v
        t = jnp.tanh(root * v * (1.0 + 0.044715 * v2))
        half = 0.5 + 0.5 * t
        act[h] = (v * half).astype(bf)
        slope = half + (0.5 * root) * v * (1.0 - t * t) * (1.0 + (3 * 0.044715) * v2)
        pre[h] = (up * slope).astype(bf)
    for h in range(4):
        p, q = h ^ 2, h ^ 1
        ig[h] = (dot(pre[h], w1[h, 0], NT) + dot(pre[p], w1p[p], NT)).astype(bf)
        gf[h, 0] = (dot(x[h], pre[h], TN) * scale).astype(bf)
        cross = (dot(x[p], pre[h], TN) * scale).astype(bf)
        gf[h, 1] = dot(spread_one, cross, TN).astype(bf)
        gs[h, 0] = (dot(act[h], c[h], TN) * scale).astype(bf)
        cross = (dot(act[q], c[h], TN) * scale).astype(bf)
        gs[h, 1] = dot(spread_two, cross, TN).astype(bf)


def shards(plan, inputs, cotangent, first_weight, second_weight, orders):
    tok, width = inputs.shape
    rows = first_weight.shape[2]
    bf = jnp.bfloat16
    all_tok = plan.g * tok
    nq = plan.nq
    scale = 1.0 / math.sqrt(tok * plan.dp)
    dma = pltpu.SemaphoreType.DMA
    n_t, n_w = 4 * plan.g, 4 * plan.dp
    toks = pltpu.VMEM((nq, 4, all_tok, B), bf)
    mats = pltpu.VMEM((nq, 4, 2, B, B), bf)
    part = jax.ShapeDtypeStruct((plan.groups, plan.nb, 2, rows, B), bf)
    input_grad, first, second = pl.pallas_call(
        functools.partial(whole, plan, scale),
        out_shape=(jax.ShapeDtypeStruct((tok, width), bf), part, part),
        in_specs=[pl.BlockSpec(memory_space=pltpu.VMEM)] + [ANY] * 4,
        out_specs=(ANY,) * 3,
        scratch_shapes=[toks, toks, mats, mats, toks, mats, mats]
        + [pltpu.VMEM((4, B, B), bf)] * 2
        + [pltpu.VMEM((4, all_tok, B), bf)] * 2
        + [dma((nq, 2, n_t)), dma((nq, 2, n_t)), dma((nq, 2, n_w)), dma((nq, 2, n_w)), dma((nq, 4))]
        + [dma((nq, n_t)), dma((nq, n_t)), dma((nq, 2, n_w)), dma((nq, 2, n_w)), dma((nq, 3))],
        compiler_params=pltpu.CompilerParams(
            collective_id=0, has_side_effects=True, vmem_limit_bytes=56 * 2**20
        ),
        name="whole",
    )(orders, inputs, cotangent, first_weight, second_weight)
    total = lambda parts: jnp.sum(parts.astype(jnp.float32), axis=0)
    return input_grad, total(first), total(second)


def solution(mesh):
    in_specs = (
        P("dp", "mp"),
        P("dp", "mp"),
        P("mp", None, "dp", None),
        P("mp", None, "dp", None),
        P(),
    )
    out_specs = (P("dp", "mp"), P("mp", None, "dp", None), P("mp", None, "dp", None))

    def body(inputs, *rest):
        sizes = mesh.shape["dp"], mesh.shape["mp"], inputs.shape[1] // B
        plan = Lanes(*sizes)
        if plan.fits:
            return by_lanes(plan, inputs, *rest)
        plan = Plan(*sizes)
        return shards(plan, inputs, *rest)

    return jax.shard_map(body, mesh=mesh, in_specs=in_specs, out_specs=out_specs, check_vma=False)
```

```python
import functools
import math

import jax
import jax.numpy as jnp
from jax import lax
from jax.experimental import pallas as pl
from jax.experimental.pallas import tpu as pltpu
from jax.sharding import PartitionSpec as P

B = 256
CHUNKS = 4
MESH = pl.DeviceIdType.MESH
ANY = pl.BlockSpec(memory_space=pl.ANY)
NT = (((1,), (1,)), ((), ()))
TN = (((0,), (0,)), ((), ()))


class Plan:
    def __init__(self, dp, mp, local_blocks):
        self.dp, self.mp, self.nb = dp, mp, local_blocks
        self.low = mp // 4
        g = max(1, dp // 2)
        while local_blocks % (4 * g):
            g //= 2
        self.g, self.groups = g, dp // g
        self.nq = local_blocks // (4 * g)

    def here(self):
        d, m = lax.axis_index("dp"), lax.axis_index("mp")
        return d, d // self.g, d % self.g, m // self.low, m % self.low


def greet(plan, d, h, lo):
    barrier = pltpu.get_barrier_semaphore()
    others = 4 * plan.dp
    me = d * 4 + h
    for k in range(1, others):
        t = (me + k) % others
        pl.semaphore_signal(
            barrier, inc=1, device_id=(t // 4, (t % 4) * plan.low + lo), device_id_type=MESH
        )
    pl.semaphore_wait(barrier, others - 1)


def sweep(first, last, body):
    lax.fori_loop(first, last, lambda k, _: (body(k), None)[1], None)


def whole(plan, scale, order, x, c, w1, w2, igo, gfo, gso, xb, cb, w1b, w2b, ig, gf, gs, w1p, w2p, act, pre,
          ts, tr, ws, wr, ls, os, orr, gsem, gr, ol):
    d, gi, r, h, lo = plan.here()
    tok, rows, nq = x.shape[0], w1.shape[2], plan.nq
    n_t, n_w = 4 * plan.g, 4 * plan.dp
    me_o, me_w = r * 4 + h, d * 4 + h
    greet(plan, d, h, lo)

    def peer_of_group(t):
        return (gi * plan.g + t // 4, (t % 4) * plan.low + lo)

    def peer_of_all(t):
        return (t // 4, (t % 4) * plan.low + lo)

    def tokens_in(i, a, k):
        t = (me_o + 5 * k) % n_t
        src, dst = ((x, xb), (c, cb))[a]
        s = src.at[:, pl.ds(pl.multiple_of((t * nq + i) * B, B), B)]
        e = dst.at[i, h, pl.ds(pl.multiple_of(r * tok, tok), tok)]
        if isinstance(k, int) and k == 0:
            return pltpu.make_async_copy(s, e, ls.at[i, a])
        return pltpu.make_async_remote_copy(
            s, e, ts.at[i, a, k], tr.at[i, a, k], device_id=peer_of_group(t), device_id_type=MESH
        )

    def weights_in(i, a, k):
        t = (me_w + 11 * k) % n_w
        src, dst = ((w1, w1b), (w2, w2b))[a]
        o = ((t // 4) % plan.g) * 4 + t % 4
        s = src.at[o * nq + i]
        e = dst.at[i, h, :, pl.ds(pl.multiple_of(d * rows, rows), rows)]
        if isinstance(k, int) and k == 0:
            return pltpu.make_async_copy(s, e, ls.at[i, 2 + a])
        return pltpu.make_async_remote_copy(
            s, e, ws.at[i, a, k], wr.at[i, a, k], device_id=peer_of_all(t), device_id_type=MESH
        )

    def tokens_out(i, k):
        t = (me_o + 5 * k) % n_t
        s = ig.at[i, t % 4, pl.ds(pl.multiple_of((t // 4) * tok, tok), tok)]
        e = igo.at[:, pl.ds(pl.multiple_of((me_o * nq + i) * B, B), B)]
        if isinstance(k, int) and k == 0:
            return pltpu.make_async_copy(s, e, ol.at[i, 0])
        return pltpu.make_async_remote_copy(
            s, e, os.at[i, k], orr.at[i, k], device_id=peer_of_group(t), device_id_type=MESH
        )

    def grads_out(i, a, k):
        t = (me_w + 11 * k) % n_w
        src, dst = ((gf, gfo), (gs, gso))[a]
        s = src.at[i, t % 4, :, pl.ds(pl.multiple_of((t // 4) * rows, rows), rows)]
        e = dst.at[gi, me_o * nq + i]
        if isinstance(k, int) and k == 0:
            return pltpu.make_async_copy(s, e, ol.at[i, 1 + a])
        return pltpu.make_async_remote_copy(
            s, e, gsem.at[i, a, k], gr.at[i, a, k], device_id=peer_of_all(t), device_id_type=MESH
        )

    def all_in(i, act_on):
        def some_weights(k, first):
            for j in range(first, plan.groups):
                for a in (0, 1):
                    act_on(weights_in(i, a, plan.groups * k + j))

        def both(k):
            act_on(tokens_in(i, 0, k))
            some_weights(k, 0)
            act_on(tokens_in(i, 1, k))

        some_weights(0, 1)
        sweep(1, n_t, both)

    def all_out(i, act_on):
        def some_grads(k, first):
            for j in range(first, plan.groups):
                for a in (0, 1):
                    act_on(grads_out(i, a, plan.groups * k + j))

        def both(k):
            act_on(tokens_out(i, k))
            some_grads(k, 0)

        some_grads(0, 1)
        sweep(1, n_t, both)

    def own_in(i):
        return [f(i, a, 0) for f in (tokens_in, weights_in) for a in (0, 1)]

    def own_out(i):
        return [tokens_out(i, 0), grads_out(i, 0, 0), grads_out(i, 1, 0)]

    for i in range(nq):
        all_in(i, lambda copy: copy.start())
        for copy in own_in(i):
            copy.start()
    for i in range(nq):
        for copy in own_in(i):
            copy.wait()
        all_in(i, lambda copy: copy.wait_recv())
        factors(scale, order, xb.at[i], cb.at[i], w1b.at[i], w2b.at[i], ig.at[i], gf.at[i], gs.at[i], w1p, w2p, act, pre)
        all_out(i, lambda copy: copy.start())
        for copy in own_out(i):
            copy.start()
    for i in range(nq):
        all_in(i, lambda copy: copy.wait_send())
        for copy in own_out(i):
            copy.wait()
        all_out(i, lambda copy: copy.wait())


class Lanes:
    def __init__(self, dp, mp, local_blocks):
        self.nc = nc = dp // 4
        self.low = mp // 4
        self.ng = local_blocks // (4 * nc) if nc else 0
        self.fits = dp % 4 == 0 and mp % 4 == 0 and self.ng > 0 and local_blocks % (4 * nc) == 0


def lanes(plan, scale, orders, x, c, w1, w2, igo, go, order, ordered, xc, wb, ig, g, gi, w1p, w2p, act, pre,
          tin, win, wout, wrel, gin, done, st, sw, sr, si, sg, sf):
    nc, low, ng = plan.nc, plan.low, plan.ng
    tok, rows = x.shape[0], w1.shape[2]
    d, m = lax.axis_index("dp"), lax.axis_index("mp")
    h, lo = m // low, m % low
    quarter, side, core, slot = d // nc, d // (2 * nc), d % nc, d % (2 * nc)
    inner = jnp.logical_or(quarter == 1, quarter == 2)
    outer = jnp.logical_not(inner)
    base, other, far = nc + side * nc, 2 * nc - side * nc, 3 * nc * side
    first, me, us = 2 * nc * side, core * 4 + h, slot * 4 + h
    n_s, n_o = 4 * nc, 8 * nc
    X, W = (x, c), (w1, w2)

    def column(kh):
        return (h, h + 1 - 2 * (h % 2), (h + 2) % 4, 3 - h)[kh]

    def mp_of(hh):
        return hh * low + lo

    def span(start, size):
        return pl.ds(pl.multiple_of(start * size, size), size)

    def put(src, dst, ssem, rsem, dev):
        return pltpu.make_async_remote_copy(src, dst, ssem, rsem, device_id=dev, device_id_type=MESH)

    def arrived(ref, sem):
        pltpu.make_async_copy(ref, ref, sem).wait()

    barrier = pltpu.get_barrier_semaphore()

    def hello(dev):
        pl.semaphore_signal(barrier, inc=1, device_id=dev, device_id_type=MESH)

    @pl.when(inner)
    def _():
        for cs in range(nc):
            hello((other + cs, m))
        for k in range(1, n_s):
            t = (me + k) % n_s
            hello((base + t // 4, mp_of(t % 4)))
        for cs in range(nc):
            hello((far + cs, m))
        pl.semaphore_wait(barrier, n_s - 1 + nc)

    @pl.when(outer)
    def _():
        for kh in range(1, 4):
            hello((d, mp_of(column(kh))))
        pl.semaphore_wait(barrier, nc + 3)

    def block_of(a, t, i):
        return W[a].at[t * ng + i]

    def columns_of(a, t, i):
        return X[a].at[:, span(t * ng + i, B)]

    def own_w(i, a, k):
        t = (me + k) % n_s
        e, arrival = wb.at[i, h, pl.ds(2 * a, 2), span(d, rows)], win.at[3 + i if i else h]
        if isinstance(k, int) and k == 0:
            return pltpu.make_async_copy(block_of(a, t, i), e, arrival)
        return put(block_of(a, t, i), e, sw.at[0, a], arrival, (base + t // 4, mp_of(t % 4)))

    def cross_w(i, a, cs):
        e = wb.at[i, h, pl.ds(2 * a, 2), span(d, rows)]
        return put(block_of(a, cs * 4 + h, i), e, sw.at[1, a], wrel.at[i], (other + cs, m))

    def own_t(i, a, k):
        t = (me + k) % n_s
        e = xc.at[i, a, h, span(slot, tok)]
        if isinstance(k, int) and k == 0:
            return pltpu.make_async_copy(columns_of(a, t, i), e, tin.at[i])
        return put(columns_of(a, t, i), e, st.at[a], tin.at[i], (base + t // 4, mp_of(t % 4)))

    def plane_w(i, a, cs, kh):
        hh = column(kh)
        s, e = block_of(a, cs * 4 + hh, i), wb.at[i, h, pl.ds(2 * a, 2), span(cs, rows)]
        return put(s, e, sw.at[0, a], wout.at[i], (d, mp_of(hh)))

    def straight_w(i, a, cs):
        e = wb.at[i, h, pl.ds(2 * a, 2), span(d, rows)]
        return put(block_of(a, cs * 4 + h, i), e, sw.at[1, a], wout.at[i], (base + cs, m))

    def plane_t(i, a, cs, kh):
        hh = column(kh)
        s, e = columns_of(a, cs * 4 + hh, i), xc.at[i, a, h, span(cs, tok)]
        if kh == 0:
            return pltpu.make_async_copy(s, e, tin.at[i])
        return put(s, e, st.at[a], tin.at[i], (d, mp_of(hh)))

    def up_w(i, cs, kh):
        hh = column(kh)
        s, e = wb.at[i, hh, :, span(cs, rows)], wb.at[i, hh, :, span(d, rows)]
        return put(s, e, sr.at[0], wout.at[i], (base + cs, m))

    def up_t(i, cs):
        s, e = xc.at[i, :, :, span(cs, tok)], xc.at[i, :, :, span(slot, tok)]
        return put(s, e, sr.at[1], tin.at[i], (base + cs, m))

    def relay_in(i, kh):
        s = wb.at[i, column(kh), :, span(base // nc, nc * rows)]
        return put(s, s, sr.at[0], wrel.at[i], (other + core, m))

    def relay_out(i):
        s = wb.at[i, :, :, span(far // nc, nc * rows)]
        return put(s, s, sr.at[1], wrel.at[i], (other + core, m))

    def tokens_out(i, k, more=0):
        u = (us + k) % n_o
        s, e = ig.at[i, u % 4, span(u // 4, tok)], igo.at[:, span(me * ng + i, B)]
        if isinstance(k, int) and k == 0:
            return pltpu.make_async_copy(s, e, done.at[0])
        return put(s, e, si.at[more], done.at[0], (first + u // 4, mp_of(u % 4)))

    def sums(i, kh, near):
        return gin.at[2 * i + near]

    def partial(i, kh, near):
        hh, theirs = column(kh), other // nc if near else 3 - far // nc
        s = g.at[i, hh, :, span(theirs, nc * rows)]
        return put(s, gi.at[i, near, hh], sg, sums(i, kh, near), (other + core, m))

    def partial_half(kh, near, half):
        hh, theirs, two = column(kh), other // nc if near else 3 - far // nc, pl.ds(2 * half, 2)
        s, e = g.at[ng - 1, hh, two, span(theirs, nc * rows)], gi.at[ng - 1, near, hh, two]
        return put(s, e, sg, gin.at[2 * ng - 2 + 8 * near + 2 * kh + half], (other + core, m))

    def own_rows(k):
        cs = (core + 1 + k) % nc
        s, e = g.at[ng - 1, h, :, span(other + cs, rows)], gi.at[ng - 1, 1, h, :, span(cs, rows)]
        return put(s, e, sg, gin.at[2 * ng + 14 + k], (other + core, m))

    def grads_out(i, kh, near, k, mats=slice(None)):
        hh, cs = column(kh), (core + k) % nc
        s, e = gi.at[i, near, hh, mats, span(cs, rows)], go.at[me * ng + i, mats]
        if near and kh == 0 and k == 0:
            return pltpu.make_async_copy(s, e, done.at[1])
        return put(s, e, sf.at[near], done.at[1], ((base if near else far) + cs, mp_of(hh)))

    lasts = (3, 1, 2, 0)
    order_at_end = ((3, 0), (1, 0), (2, 0), (3, 1), (1, 1), (0, 0), (2, 1))
    farthest_first = [(kh, near, half) for kh, near in order_at_end for half in (0, 1)]

    def both(f, *at):
        return [f(at[0], a, *at[1:]) for a in (0, 1)]

    def begin(copies):
        for copy in copies:
            copy.start()

    def add(i, kh, near, mats=slice(None)):
        hh = column(kh)
        ours = base // nc if near else far // nc
        mine = g[i, hh, mats, span(ours, nc * rows)].astype(jnp.float32)
        gi[i, near, hh, mats] = (mine + gi[i, near, hh, mats].astype(jnp.float32)).astype(jnp.bfloat16)
        begin([grads_out(i, kh, near, k, mats) for k in range(nc)])

    def combine(i):
        for near in (0, 1):
            arrived(gi.at[i, near], sums(i, 0, near))
            for kh in lasts:
                add(i, kh, near)

    def combine_last():
        i = ng - 1
        for kh, near, half in farthest_first:
            two = pl.ds(2 * half, 2)
            arrived(gi.at[i, near, column(kh), two], gin.at[2 * ng - 2 + 8 * near + 2 * kh + half])
            add(i, kh, near, two)
        for k in range(nc):
            cs = (core + 1 + k) % nc
            arrived(gi.at[i, 1, h, :, span(cs, rows)], gin.at[2 * ng + 14 + k])
            mine = g[i, h, :, span(base + cs, rows)].astype(jnp.float32)
            total = (mine + gi[i, 1, h, :, span(cs, rows)].astype(jnp.float32)).astype(jnp.bfloat16)
            if k < nc - 1:
                gi[i, 1, h, :, span(cs, rows)] = total
                grads_out(i, 0, 1, 1 + k).start()
            else:
                go[me * ng + i] = total

    @pl.when(inner)
    def _():
        for i in range(ng):
            for cs in range(nc):
                begin(both(cross_w, i, cs))
        pltpu.make_async_copy(orders, order, ordered).start()
        for i in range(ng):
            sweep(1, n_s, lambda k: begin(both(own_w, i, k)))
            begin(both(own_w, i, 0))
        for i in range(ng):
            sweep(1, n_s, lambda k: begin(both(own_t, i, k)))
            begin(both(own_t, i, 0))
        for i in range(ng):
            rest = span(base // nc, nc * rows)
            if i:
                arrived(wb.at[i, :, :, rest], win.at[3 + i])
            for kh in range(4):
                if i == 0:
                    arrived(wb.at[i, column(kh), :, rest], win.at[column(kh)])
                if kh:
                    relay_in(i, kh).start()
        for i in range(ng):
            arrived(wb.at[i, :, :, span(far // nc, nc * rows)], wout.at[i])
            relay_out(i).start()
        arrived(order, ordered)
        for i in range(ng):
            arrived(wb.at[i, :, :, span(1 - side, 2 * nc * rows)], wrel.at[i])
            arrived(xc.at[i], tin.at[i])
            w1b, w2b = wb.at[i, :, pl.ds(0, 2)], wb.at[i, :, pl.ds(2, 2)]
            gf, gs = g.at[i, :, pl.ds(0, 2)], g.at[i, :, pl.ds(2, 2)]
            factors(scale, order, xc.at[i, 0], xc.at[i, 1], w1b, w2b, ig.at[i], gf, gs, w1p, w2p, act, pre)
            if i < ng - 1:
                begin([partial(i, kh, near) for near in (0, 1) for kh in lasts])
            else:
                begin([partial_half(*at) for at in farthest_first] + [own_rows(k) for k in range(nc)])
            sweep(1, n_s, lambda k: tokens_out(i, k).start())
            sweep(n_s, n_o, lambda k: tokens_out(i, k, 1).start())
            tokens_out(i, 0).start()
            if i >= 1:
                combine(i - 1)
        combine_last()
        some = ng * (n_s - 1)
        arrived(igo.at[:, pl.ds(0, some * B)], si.at[0])
        arrived(igo, si.at[1])
        for a in (0, 1):
            arrived(X[a].at[:, pl.ds(0, some * B)], st.at[a])
            arrived(W[a].at[pl.ds(0, some)], sw.at[0, a])
            arrived(W[a].at[pl.ds(0, ng * nc)], sw.at[1, a])
        arrived(wb.at[:, pl.ds(0, 3), :, pl.ds(0, nc * rows)], sr.at[0])
        arrived(wb.at[:, :, :, pl.ds(0, nc * rows)], sr.at[1])
        arrived(gi, sg)
        arrived(go, sf.at[0])
        arrived(go.at[pl.ds(0, some)], sf.at[1])
        arrived(go.at[pl.ds(0, 4 * nc * ng - 1)], done.at[1])

    @pl.when(outer)
    def _():
        for i in range(ng):
            for cs in range(nc):
                begin(both(straight_w, i, cs))
        for i in range(ng):
            for kh in (1, 2, 3):
                for cs in range(nc):
                    begin(both(plane_w, i, cs, kh))
        for i in range(ng):
            for kh in (1, 2, 3, 0):
                for cs in range(nc):
                    begin(both(plane_t, i, cs, kh))
        for i in range(ng):
            arrived(wb.at[i, pl.ds(0, 3), :, span(0, nc * rows)], wout.at[i])
            begin([up_w(i, cs, kh) for kh in (1, 2, 3) for cs in range(nc)])
        for i in range(ng):
            arrived(xc.at[i, :, :, span(0, nc * tok)], tin.at[i])
            begin([up_t(i, cs) for cs in range(nc)])
        for a in (0, 1):
            arrived(W[a].at[pl.ds(0, 3 * ng * nc)], sw.at[0, a])
            arrived(W[a].at[pl.ds(0, ng * nc)], sw.at[1, a])
            arrived(X[a].at[:, pl.ds(0, 3 * ng * nc * B)], st.at[a])
        arrived(go.at[pl.ds(0, 3 * ng * nc)], sr.at[0])
        arrived(xc.at[:, :, :, pl.ds(0, nc * tok)], sr.at[1])
        arrived(go, done.at[1])

    arrived(igo, done.at[0])


def by_lanes(plan, inputs, cotangent, first_weight, second_weight, orders):
    tok, width = inputs.shape
    rows = first_weight.shape[2]
    nc, ng, bf = plan.nc, plan.ng, jnp.bfloat16
    scale = 1.0 / math.sqrt(tok * 4 * nc)
    dma = pltpu.SemaphoreType.DMA
    all_tok = 2 * nc * tok
    mats = pltpu.VMEM((ng, 4, 4, B, B), bf)
    input_grad, sums = pl.pallas_call(
        functools.partial(lanes, plan, scale),
        out_shape=(pltpu.VMEM((tok, width), bf), pltpu.VMEM((4 * nc * ng, 4, rows, B), bf)),
        in_specs=[ANY] * 5,
        out_specs=(pl.BlockSpec(memory_space=pltpu.VMEM),) * 2,
        scratch_shapes=[pltpu.VMEM(orders.shape, orders.dtype), dma]
        + [pltpu.VMEM((ng, 2, 4, all_tok, B), bf), mats]
        + [pltpu.VMEM((ng, 4, all_tok, B), bf), mats, pltpu.VMEM((ng, 2, 4, 4, nc * rows, B), bf)]
        + [pltpu.VMEM((4, B, B), bf)] * 2
        + [pltpu.VMEM((4, all_tok, B), bf)] * 2
        + [dma((ng,)), dma((ng + 3,)), dma((ng,)), dma((ng,)), dma((2 * ng + 14 + nc,)), dma((2,))]
        + [dma((2,)), dma((2, 2)), dma((2,)), dma((2,)), dma, dma((2,))],
        compiler_params=pltpu.CompilerParams(
            collective_id=0, has_side_effects=True, vmem_limit_bytes=58 * 2**20
        ),
        name="lanes",
    )(orders, inputs, cotangent, first_weight, second_weight)
    return finish(input_grad, sums)


def store(ig, sums, igo, fo, so, fw, sw, sems):
    copies = [pltpu.make_async_copy(ig, igo, sems.at[0, 0])]
    copies[0].start()
    size = max(1, sums.shape[0] // CHUNKS)
    for n, at in enumerate(range(0, sums.shape[0], size)):
        for a, (wide, dst) in enumerate(((fw, fo), (sw, so))):
            rows = pl.ds(at, size)
            wide[rows] = sums[rows, pl.ds(2 * a, 2)].astype(jnp.float32)
            copies.append(pltpu.make_async_copy(wide.at[rows], dst.at[rows], sems.at[1 + a, n]))
            copies[-1].start()
    for copy in copies:
        copy.wait()


def finish(input_grad, sums):
    nb, _, rows, width = sums.shape
    wide = (nb, 2, rows, width)
    out = jax.ShapeDtypeStruct(wide, jnp.float32)
    return pl.pallas_call(
        store,
        out_shape=(jax.ShapeDtypeStruct(input_grad.shape, input_grad.dtype), out, out),
        in_specs=[pl.BlockSpec(memory_space=pltpu.VMEM)] * 2,
        out_specs=(ANY,) * 3,
        scratch_shapes=[pltpu.VMEM(wide, jnp.float32)] * 2 + [pltpu.SemaphoreType.DMA((3, CHUNKS))],
        compiler_params=pltpu.CompilerParams(vmem_limit_bytes=48 * 2**20),
        name="store",
    )(input_grad, sums)


def dot(left, right, dims=(((1,), (0,)), ((), ()))):
    return lax.dot_general(left, right, dims, preferred_element_type=jnp.float32)


def factors(scale, order, x, c, w1, w2, ig, gf, gs, w1p, w2p, act, pre):
    bf = jnp.bfloat16
    place = lax.broadcasted_iota(jnp.int32, (B, B), 0)
    spread_one = (place == order[0:1, :]).astype(jnp.float32).astype(bf)
    spread_two = (place == order[1:2, :]).astype(jnp.float32).astype(bf)
    root = math.sqrt(2.0 / math.pi)
    for h in range(4):
        w1p[h] = dot(spread_one, w1[h, 1]).astype(bf)
        w2p[h] = dot(spread_two, w2[h, 1]).astype(bf)
    for h in range(4):
        p, q = h ^ 2, h ^ 1
        v = dot(x[h], w1[h, 0]) + dot(x[p], w1p[h])
        up = dot(c[h], w2[h, 0], NT) + dot(c[q], w2p[q], NT)
        v2 = v * v
        t = jnp.tanh(root * v * (1.0 + 0.044715 * v2))
        half = 0.5 + 0.5 * t
        act[h] = (v * half).astype(bf)
        slope = half + (0.5 * root) * v * (1.0 - t * t) * (1.0 + (3 * 0.044715) * v2)
        pre[h] = (up * slope).astype(bf)
    for h in range(4):
        p, q = h ^ 2, h ^ 1
        ig[h] = (dot(pre[h], w1[h, 0], NT) + dot(pre[p], w1p[p], NT)).astype(bf)
        gf[h, 0] = (dot(x[h], pre[h], TN) * scale).astype(bf)
        cross = (dot(x[p], pre[h], TN) * scale).astype(bf)
        gf[h, 1] = dot(spread_one, cross, TN).astype(bf)
        gs[h, 0] = (dot(act[h], c[h], TN) * scale).astype(bf)
        cross = (dot(act[q], c[h], TN) * scale).astype(bf)
        gs[h, 1] = dot(spread_two, cross, TN).astype(bf)


def shards(plan, inputs, cotangent, first_weight, second_weight, orders):
    tok, width = inputs.shape
    rows = first_weight.shape[2]
    bf = jnp.bfloat16
    all_tok = plan.g * tok
    nq = plan.nq
    scale = 1.0 / math.sqrt(tok * plan.dp)
    dma = pltpu.SemaphoreType.DMA
    n_t, n_w = 4 * plan.g, 4 * plan.dp
    toks = pltpu.VMEM((nq, 4, all_tok, B), bf)
    mats = pltpu.VMEM((nq, 4, 2, B, B), bf)
    part = jax.ShapeDtypeStruct((plan.groups, plan.nb, 2, rows, B), bf)
    input_grad, first, second = pl.pallas_call(
        functools.partial(whole, plan, scale),
        out_shape=(jax.ShapeDtypeStruct((tok, width), bf), part, part),
        in_specs=[pl.BlockSpec(memory_space=pltpu.VMEM)] + [ANY] * 4,
        out_specs=(ANY,) * 3,
        scratch_shapes=[toks, toks, mats, mats, toks, mats, mats]
        + [pltpu.VMEM((4, B, B), bf)] * 2
        + [pltpu.VMEM((4, all_tok, B), bf)] * 2
        + [dma((nq, 2, n_t)), dma((nq, 2, n_t)), dma((nq, 2, n_w)), dma((nq, 2, n_w)), dma((nq, 4))]
        + [dma((nq, n_t)), dma((nq, n_t)), dma((nq, 2, n_w)), dma((nq, 2, n_w)), dma((nq, 3))],
        compiler_params=pltpu.CompilerParams(
            collective_id=0, has_side_effects=True, vmem_limit_bytes=56 * 2**20
        ),
        name="whole",
    )(orders, inputs, cotangent, first_weight, second_weight)
    total = lambda parts: jnp.sum(parts.astype(jnp.float32), axis=0)
    return input_grad, total(first), total(second)


def solution(mesh):
    in_specs = (
        P("dp", "mp"),
        P("dp", "mp"),
        P("mp", None, "dp", None),
        P("mp", None, "dp", None),
        P(),
    )
    out_specs = (P("dp", "mp"), P("mp", None, "dp", None), P("mp", None, "dp", None))

    def body(inputs, *rest):
        sizes = mesh.shape["dp"], mesh.shape["mp"], inputs.shape[1] // B
        plan = Lanes(*sizes)
        if plan.fits:
            return by_lanes(plan, inputs, *rest)
        plan = Plan(*sizes)
        return shards(plan, inputs, *rest)

    return jax.shard_map(body, mesh=mesh, in_specs=in_specs, out_specs=out_specs, check_vma=False)
```

```python
import functools
import math

import jax
import jax.numpy as jnp
from jax import lax
from jax.experimental import pallas as pl
from jax.experimental.pallas import tpu as pltpu
from jax.sharding import PartitionSpec as P

B = 256
CHUNKS = 4
MESH = pl.DeviceIdType.MESH
ANY = pl.BlockSpec(memory_space=pl.ANY)
NT = (((1,), (1,)), ((), ()))
TN = (((0,), (0,)), ((), ()))


class Plan:
    def __init__(self, dp, mp, local_blocks):
        self.dp, self.mp, self.nb = dp, mp, local_blocks
        self.low = mp // 4
        g = max(1, dp // 2)
        while local_blocks % (4 * g):
            g //= 2
        self.g, self.groups = g, dp // g
        self.nq = local_blocks // (4 * g)

    def here(self):
        d, m = lax.axis_index("dp"), lax.axis_index("mp")
        return d, d // self.g, d % self.g, m // self.low, m % self.low


def greet(plan, d, h, lo):
    barrier = pltpu.get_barrier_semaphore()
    others = 4 * plan.dp
    me = d * 4 + h
    for k in range(1, others):
        t = (me + k) % others
        pl.semaphore_signal(
            barrier, inc=1, device_id=(t // 4, (t % 4) * plan.low + lo), device_id_type=MESH
        )
    pl.semaphore_wait(barrier, others - 1)


def sweep(first, last, body):
    lax.fori_loop(first, last, lambda k, _: (body(k), None)[1], None)


def whole(plan, scale, order, x, c, w1, w2, igo, gfo, gso, xb, cb, w1b, w2b, ig, gf, gs, w1p, w2p, act, pre,
          ts, tr, ws, wr, ls, os, orr, gsem, gr, ol):
    d, gi, r, h, lo = plan.here()
    tok, rows, nq = x.shape[0], w1.shape[2], plan.nq
    n_t, n_w = 4 * plan.g, 4 * plan.dp
    me_o, me_w = r * 4 + h, d * 4 + h
    greet(plan, d, h, lo)

    def peer_of_group(t):
        return (gi * plan.g + t // 4, (t % 4) * plan.low + lo)

    def peer_of_all(t):
        return (t // 4, (t % 4) * plan.low + lo)

    def tokens_in(i, a, k):
        t = (me_o + 5 * k) % n_t
        src, dst = ((x, xb), (c, cb))[a]
        s = src.at[:, pl.ds(pl.multiple_of((t * nq + i) * B, B), B)]
        e = dst.at[i, h, pl.ds(pl.multiple_of(r * tok, tok), tok)]
        if isinstance(k, int) and k == 0:
            return pltpu.make_async_copy(s, e, ls.at[i, a])
        return pltpu.make_async_remote_copy(
            s, e, ts.at[i, a, k], tr.at[i, a, k], device_id=peer_of_group(t), device_id_type=MESH
        )

    def weights_in(i, a, k):
        t = (me_w + 11 * k) % n_w
        src, dst = ((w1, w1b), (w2, w2b))[a]
        o = ((t // 4) % plan.g) * 4 + t % 4
        s = src.at[o * nq + i]
        e = dst.at[i, h, :, pl.ds(pl.multiple_of(d * rows, rows), rows)]
        if isinstance(k, int) and k == 0:
            return pltpu.make_async_copy(s, e, ls.at[i, 2 + a])
        return pltpu.make_async_remote_copy(
            s, e, ws.at[i, a, k], wr.at[i, a, k], device_id=peer_of_all(t), device_id_type=MESH
        )

    def tokens_out(i, k):
        t = (me_o + 5 * k) % n_t
        s = ig.at[i, t % 4, pl.ds(pl.multiple_of((t // 4) * tok, tok), tok)]
        e = igo.at[:, pl.ds(pl.multiple_of((me_o * nq + i) * B, B), B)]
        if isinstance(k, int) and k == 0:
            return pltpu.make_async_copy(s, e, ol.at[i, 0])
        return pltpu.make_async_remote_copy(
            s, e, os.at[i, k], orr.at[i, k], device_id=peer_of_group(t), device_id_type=MESH
        )

    def grads_out(i, a, k):
        t = (me_w + 11 * k) % n_w
        src, dst = ((gf, gfo), (gs, gso))[a]
        s = src.at[i, t % 4, :, pl.ds(pl.multiple_of((t // 4) * rows, rows), rows)]
        e = dst.at[gi, me_o * nq + i]
        if isinstance(k, int) and k == 0:
            return pltpu.make_async_copy(s, e, ol.at[i, 1 + a])
        return pltpu.make_async_remote_copy(
            s, e, gsem.at[i, a, k], gr.at[i, a, k], device_id=peer_of_all(t), device_id_type=MESH
        )

    def all_in(i, act_on):
        def some_weights(k, first):
            for j in range(first, plan.groups):
                for a in (0, 1):
                    act_on(weights_in(i, a, plan.groups * k + j))

        def both(k):
            act_on(tokens_in(i, 0, k))
            some_weights(k, 0)
            act_on(tokens_in(i, 1, k))

        some_weights(0, 1)
        sweep(1, n_t, both)

    def all_out(i, act_on):
        def some_grads(k, first):
            for j in range(first, plan.groups):
                for a in (0, 1):
                    act_on(grads_out(i, a, plan.groups * k + j))

        def both(k):
            act_on(tokens_out(i, k))
            some_grads(k, 0)

        some_grads(0, 1)
        sweep(1, n_t, both)

    def own_in(i):
        return [f(i, a, 0) for f in (tokens_in, weights_in) for a in (0, 1)]

    def own_out(i):
        return [tokens_out(i, 0), grads_out(i, 0, 0), grads_out(i, 1, 0)]

    for i in range(nq):
        all_in(i, lambda copy: copy.start())
        for copy in own_in(i):
            copy.start()
    for i in range(nq):
        for copy in own_in(i):
            copy.wait()
        all_in(i, lambda copy: copy.wait_recv())
        factors(scale, order, xb.at[i], cb.at[i], w1b.at[i], w2b.at[i], ig.at[i], gf.at[i], gs.at[i], w1p, w2p, act, pre)
        all_out(i, lambda copy: copy.start())
        for copy in own_out(i):
            copy.start()
    for i in range(nq):
        all_in(i, lambda copy: copy.wait_send())
        for copy in own_out(i):
            copy.wait()
        all_out(i, lambda copy: copy.wait())


class Lanes:
    def __init__(self, dp, mp, local_blocks):
        self.nc = nc = dp // 4
        self.low = mp // 4
        self.ng = local_blocks // (4 * nc) if nc else 0
        self.fits = dp % 4 == 0 and mp % 4 == 0 and self.ng > 0 and local_blocks % (4 * nc) == 0


def lanes(plan, scale, orders, x, c, w1, w2, igo, go, order, ordered, xc, wb, ig, g, gi, w1p, w2p, act, pre,
          tin, win, wout, wrel, gin, done, st, sw, sr, si, sg, sf):
    nc, low, ng = plan.nc, plan.low, plan.ng
    tok, rows = x.shape[0], w1.shape[2]
    d, m = lax.axis_index("dp"), lax.axis_index("mp")
    h, lo = m // low, m % low
    quarter, side, core, slot = d // nc, d // (2 * nc), d % nc, d % (2 * nc)
    inner = jnp.logical_or(quarter == 1, quarter == 2)
    outer = jnp.logical_not(inner)
    base, other, far = nc + side * nc, 2 * nc - side * nc, 3 * nc * side
    first, me, us = 2 * nc * side, core * 4 + h, slot * 4 + h
    n_s, n_o = 4 * nc, 8 * nc
    X, W = (x, c), (w1, w2)

    def column(kh):
        return (h, h + 1 - 2 * (h % 2), (h + 2) % 4, 3 - h)[kh]

    def mp_of(hh):
        return hh * low + lo

    def span(start, size):
        return pl.ds(pl.multiple_of(start * size, size), size)

    def put(src, dst, ssem, rsem, dev):
        return pltpu.make_async_remote_copy(src, dst, ssem, rsem, device_id=dev, device_id_type=MESH)

    def arrived(ref, sem):
        pltpu.make_async_copy(ref, ref, sem).wait()

    barrier = pltpu.get_barrier_semaphore()

    def hello(dev):
        pl.semaphore_signal(barrier, inc=1, device_id=dev, device_id_type=MESH)

    @pl.when(inner)
    def _():
        for cs in range(nc):
            hello((other + cs, m))
        for kh in (1, 2):
            for cs in range(nc):
                hello((base + cs, mp_of(column(kh))))
        for k in range(1, nc):
            hello((base + (core + k) % nc, m))
        for cs in range(nc):
            hello((far + cs, m))
        pl.semaphore_wait(barrier, 4 * nc - 1)

    @pl.when(outer)
    def _():
        for kh in range(1, 4):
            hello((d, mp_of(column(kh))))
        pl.semaphore_wait(barrier, nc + 3)

    def block_of(a, t, i):
        return W[a].at[t * ng + i]

    def columns_of(a, t, i):
        return X[a].at[:, span(t * ng + i, B)]

    def own_w(i, a, kh, k):
        cs, hh = (core + k) % nc, column(kh)
        s, e = block_of(a, cs * 4 + hh, i), wb.at[i, h, pl.ds(2 * a, 2), span(d, rows)]
        if kh == 0 and k == 0:
            return pltpu.make_async_copy(s, e, win.at[i, h])
        return put(s, e, sw.at[0, a], win.at[i, h], (base + cs, mp_of(hh)))

    def cross_w(i, a, cs):
        e = wb.at[i, h, pl.ds(2 * a, 2), span(d, rows)]
        return put(block_of(a, cs * 4 + h, i), e, sw.at[1, a], wrel.at[i], (other + cs, m))

    def own_t(i, a, kh, k):
        cs, hh = (core + k) % nc, column(kh)
        s, e = columns_of(a, cs * 4 + hh, i), xc.at[i, a, h, span(slot, tok)]
        if kh == 0 and k == 0:
            return pltpu.make_async_copy(s, e, tin.at[i])
        return put(s, e, st.at[a], tin.at[i], (base + cs, mp_of(hh)))

    def plane_w(i, a, cs, kh):
        hh = column(kh)
        s, e = block_of(a, cs * 4 + hh, i), wb.at[i, h, pl.ds(2 * a, 2), span(cs, rows)]
        return put(s, e, sw.at[0, a], wout.at[i], (d, mp_of(hh)))

    def straight_w(i, a, cs):
        e = wb.at[i, h, pl.ds(2 * a, 2), span(d, rows)]
        return put(block_of(a, cs * 4 + h, i), e, sw.at[1, a], wout.at[i], (base + cs, m))

    def plane_t(i, a, cs, kh):
        hh = column(kh)
        s, e = columns_of(a, cs * 4 + hh, i), xc.at[i, a, h, span(cs, tok)]
        if kh == 0:
            return pltpu.make_async_copy(s, e, tin.at[i])
        return put(s, e, st.at[a], tin.at[i], (d, mp_of(hh)))

    def up_w(i, cs, kh):
        hh = column(kh)
        s, e = wb.at[i, hh, :, span(cs, rows)], wb.at[i, hh, :, span(d, rows)]
        return put(s, e, sr.at[0], wout.at[i], (base + cs, m))

    def up_t(i, cs):
        s, e = xc.at[i, :, :, span(cs, tok)], xc.at[i, :, :, span(slot, tok)]
        return put(s, e, sr.at[1], tin.at[i], (base + cs, m))

    def relay_in(i, kh):
        s = wb.at[i, column(kh), :, span(base // nc, nc * rows)]
        return put(s, s, sr.at[0], wrel.at[i], (other + core, m))

    def relay_out(i):
        s = wb.at[i, :, :, span(far // nc, nc * rows)]
        return put(s, s, sr.at[1], wrel.at[i], (other + core, m))

    def tokens_out(i, k, more=0):
        u = (us + k) % n_o
        s, e = ig.at[i, u % 4, span(u // 4, tok)], igo.at[:, span(me * ng + i, B)]
        if isinstance(k, int) and k == 0:
            return pltpu.make_async_copy(s, e, done.at[0])
        return put(s, e, si.at[more], done.at[0], (first + u // 4, mp_of(u % 4)))

    def sums(i, kh, near):
        return gin.at[2 * i + near]

    def partial(i, kh, near):
        hh, theirs = column(kh), other // nc if near else 3 - far // nc
        s = g.at[i, hh, :, span(theirs, nc * rows)]
        return put(s, gi.at[i, near, hh], sg, sums(i, kh, near), (other + core, m))

    def partial_half(kh, near, half):
        hh, theirs, two = column(kh), other // nc if near else 3 - far // nc, pl.ds(2 * half, 2)
        s, e = g.at[ng - 1, hh, two, span(theirs, nc * rows)], gi.at[ng - 1, near, hh, two]
        return put(s, e, sg, gin.at[2 * ng - 2 + 8 * near + 2 * kh + half], (other + core, m))

    def own_rows(k):
        cs = (core + 1 + k) % nc
        s, e = g.at[ng - 1, h, :, span(other + cs, rows)], gi.at[ng - 1, 1, h, :, span(cs, rows)]
        return put(s, e, sg, gin.at[2 * ng + 14 + k], (other + core, m))

    def grads_out(i, kh, near, k, mats=slice(None)):
        hh, cs = column(kh), (core + k) % nc
        s, e = gi.at[i, near, hh, mats, span(cs, rows)], go.at[me * ng + i, mats]
        if near and kh == 0 and k == 0:
            return pltpu.make_async_copy(s, e, done.at[1])
        return put(s, e, sf.at[near], done.at[1], ((base if near else far) + cs, mp_of(hh)))

    lasts = (3, 1, 2, 0)
    order_at_end = ((3, 0), (1, 0), (2, 0), (3, 1), (1, 1), (0, 0), (2, 1))
    farthest_first = [(kh, near, half) for kh, near in order_at_end for half in (0, 1)]

    def both(f, *at):
        return [f(at[0], a, *at[1:]) for a in (0, 1)]

    def begin(copies):
        for copy in copies:
            copy.start()

    def add(i, kh, near, mats=slice(None)):
        hh = column(kh)
        ours = base // nc if near else far // nc
        mine = g[i, hh, mats, span(ours, nc * rows)].astype(jnp.float32)
        gi[i, near, hh, mats] = (mine + gi[i, near, hh, mats].astype(jnp.float32)).astype(jnp.bfloat16)
        begin([grads_out(i, kh, near, k, mats) for k in range(nc)])

    def combine(i):
        for near in (0, 1):
            arrived(gi.at[i, near], sums(i, 0, near))
            for kh in lasts:
                add(i, kh, near)

    def combine_last():
        i = ng - 1
        for kh, near, half in farthest_first:
            two = pl.ds(2 * half, 2)
            arrived(gi.at[i, near, column(kh), two], gin.at[2 * ng - 2 + 8 * near + 2 * kh + half])
            add(i, kh, near, two)
        for k in range(nc):
            cs = (core + 1 + k) % nc
            arrived(gi.at[i, 1, h, :, span(cs, rows)], gin.at[2 * ng + 14 + k])
            mine = g[i, h, :, span(base + cs, rows)].astype(jnp.float32)
            total = (mine + gi[i, 1, h, :, span(cs, rows)].astype(jnp.float32)).astype(jnp.bfloat16)
            if k < nc - 1:
                gi[i, 1, h, :, span(cs, rows)] = total
                grads_out(i, 0, 1, 1 + k).start()
            else:
                go[me * ng + i] = total

    @pl.when(inner)
    def _():
        for i in range(ng):
            for cs in range(nc):
                begin(both(cross_w, i, cs))
        pltpu.make_async_copy(orders, order, ordered).start()
        rest = span(base // nc, nc * rows)
        for i in range(ng):
            for kh in (1, 2, 0):
                for k in range(nc):
                    begin(both(own_w, i, kh, k))
        arrived(wb.at[0, column(1), :, rest], win.at[0, column(1)])
        relay_in(0, 1).start()
        for i in range(ng):
            for k in range(nc):
                begin(both(own_w, i, 3, k))
        for i in range(ng):
            for kh in (3, 1, 2, 0):
                for k in range(nc):
                    begin(both(own_t, i, kh, k))
        for kh in (1, 2, 3, 0):
            for i in range(ng):
                if i or kh != 1:
                    arrived(wb.at[i, column(kh), :, rest], win.at[i, column(kh)])
                    if kh:
                        relay_in(i, kh).start()
        for i in range(ng):
            arrived(wb.at[i, :, :, span(far // nc, nc * rows)], wout.at[i])
            relay_out(i).start()
        arrived(order, ordered)
        for i in range(ng):
            arrived(wb.at[i, :, :, span(1 - side, 2 * nc * rows)], wrel.at[i])
            arrived(xc.at[i], tin.at[i])
            w1b, w2b = wb.at[i, :, pl.ds(0, 2)], wb.at[i, :, pl.ds(2, 2)]
            gf, gs = g.at[i, :, pl.ds(0, 2)], g.at[i, :, pl.ds(2, 2)]
            factors(scale, order, xc.at[i, 0], xc.at[i, 1], w1b, w2b, ig.at[i], gf, gs, w1p, w2p, act, pre)
            if i < ng - 1:
                begin([partial(i, kh, near) for near in (0, 1) for kh in lasts])
            else:
                begin([partial_half(*at) for at in farthest_first] + [own_rows(k) for k in range(nc)])
            sweep(1, n_s, lambda k: tokens_out(i, k).start())
            sweep(n_s, n_o, lambda k: tokens_out(i, k, 1).start())
            tokens_out(i, 0).start()
            if i >= 1:
                combine(i - 1)
        combine_last()
        some = ng * (n_s - 1)
        arrived(igo.at[:, pl.ds(0, some * B)], si.at[0])
        arrived(igo, si.at[1])
        for a in (0, 1):
            arrived(X[a].at[:, pl.ds(0, some * B)], st.at[a])
            arrived(W[a].at[pl.ds(0, some)], sw.at[0, a])
            arrived(W[a].at[pl.ds(0, ng * nc)], sw.at[1, a])
        arrived(wb.at[:, pl.ds(0, 3), :, pl.ds(0, nc * rows)], sr.at[0])
        arrived(wb.at[:, :, :, pl.ds(0, nc * rows)], sr.at[1])
        arrived(gi, sg)
        arrived(go, sf.at[0])
        arrived(go.at[pl.ds(0, some)], sf.at[1])
        arrived(go.at[pl.ds(0, 4 * nc * ng - 1)], done.at[1])

    @pl.when(outer)
    def _():
        for i in range(ng):
            for cs in range(nc):
                begin(both(straight_w, i, cs))
        for i in range(ng):
            for kh in (1, 2, 3):
                for cs in range(nc):
                    begin(both(plane_w, i, cs, kh))
        for i in range(ng):
            for kh in (1, 2, 3, 0):
                for cs in range(nc):
                    begin(both(plane_t, i, cs, kh))
        for i in range(ng):
            arrived(wb.at[i, pl.ds(0, 3), :, span(0, nc * rows)], wout.at[i])
            begin([up_w(i, cs, kh) for kh in (1, 2, 3) for cs in range(nc)])
        for i in range(ng):
            arrived(xc.at[i, :, :, span(0, nc * tok)], tin.at[i])
            begin([up_t(i, cs) for cs in range(nc)])
        for a in (0, 1):
            arrived(W[a].at[pl.ds(0, 3 * ng * nc)], sw.at[0, a])
            arrived(W[a].at[pl.ds(0, ng * nc)], sw.at[1, a])
            arrived(X[a].at[:, pl.ds(0, 3 * ng * nc * B)], st.at[a])
        arrived(go.at[pl.ds(0, 3 * ng * nc)], sr.at[0])
        arrived(xc.at[:, :, :, pl.ds(0, nc * tok)], sr.at[1])
        arrived(go, done.at[1])

    arrived(igo, done.at[0])


def by_lanes(plan, inputs, cotangent, first_weight, second_weight, orders):
    tok, width = inputs.shape
    rows = first_weight.shape[2]
    nc, ng, bf = plan.nc, plan.ng, jnp.bfloat16
    scale = 1.0 / math.sqrt(tok * 4 * nc)
    dma = pltpu.SemaphoreType.DMA
    all_tok = 2 * nc * tok
    mats = pltpu.VMEM((ng, 4, 4, B, B), bf)
    input_grad, sums = pl.pallas_call(
        functools.partial(lanes, plan, scale),
        out_shape=(pltpu.VMEM((tok, width), bf), pltpu.VMEM((4 * nc * ng, 4, rows, B), bf)),
        in_specs=[ANY] * 5,
        out_specs=(pl.BlockSpec(memory_space=pltpu.VMEM),) * 2,
        scratch_shapes=[pltpu.VMEM(orders.shape, orders.dtype), dma]
        + [pltpu.VMEM((ng, 2, 4, all_tok, B), bf), mats]
        + [pltpu.VMEM((ng, 4, all_tok, B), bf), mats, pltpu.VMEM((ng, 2, 4, 4, nc * rows, B), bf)]
        + [pltpu.VMEM((4, B, B), bf)] * 2
        + [pltpu.VMEM((4, all_tok, B), bf)] * 2
        + [dma((ng,)), dma((ng, 4)), dma((ng,)), dma((ng,)), dma((2 * ng + 14 + nc,)), dma((2,))]
        + [dma((2,)), dma((2, 2)), dma((2,)), dma((2,)), dma, dma((2,))],
        compiler_params=pltpu.CompilerParams(
            collective_id=0, has_side_effects=True, vmem_limit_bytes=58 * 2**20
        ),
        name="lanes",
    )(orders, inputs, cotangent, first_weight, second_weight)
    return finish(input_grad, sums)


def store(ig, sums, igo, fo, so, fw, sw, sems):
    copies = [pltpu.make_async_copy(ig, igo, sems.at[0, 0])]
    copies[0].start()
    size = max(1, sums.shape[0] // CHUNKS)
    for n, at in enumerate(range(0, sums.shape[0], size)):
        for a, (wide, dst) in enumerate(((fw, fo), (sw, so))):
            rows = pl.ds(at, size)
            wide[rows] = sums[rows, pl.ds(2 * a, 2)].astype(jnp.float32)
            copies.append(pltpu.make_async_copy(wide.at[rows], dst.at[rows], sems.at[1 + a, n]))
            copies[-1].start()
    for copy in copies:
        copy.wait()


def finish(input_grad, sums):
    nb, _, rows, width = sums.shape
    wide = (nb, 2, rows, width)
    out = jax.ShapeDtypeStruct(wide, jnp.float32)
    return pl.pallas_call(
        store,
        out_shape=(jax.ShapeDtypeStruct(input_grad.shape, input_grad.dtype), out, out),
        in_specs=[pl.BlockSpec(memory_space=pltpu.VMEM)] * 2,
        out_specs=(ANY,) * 3,
        scratch_shapes=[pltpu.VMEM(wide, jnp.float32)] * 2 + [pltpu.SemaphoreType.DMA((3, CHUNKS))],
        compiler_params=pltpu.CompilerParams(vmem_limit_bytes=48 * 2**20),
        name="store",
    )(input_grad, sums)


def dot(left, right, dims=(((1,), (0,)), ((), ()))):
    return lax.dot_general(left, right, dims, preferred_element_type=jnp.float32)


def factors(scale, order, x, c, w1, w2, ig, gf, gs, w1p, w2p, act, pre):
    bf = jnp.bfloat16
    place = lax.broadcasted_iota(jnp.int32, (B, B), 0)
    spread_one = (place == order[0:1, :]).astype(jnp.float32).astype(bf)
    spread_two = (place == order[1:2, :]).astype(jnp.float32).astype(bf)
    root = math.sqrt(2.0 / math.pi)
    for h in range(4):
        w1p[h] = dot(spread_one, w1[h, 1]).astype(bf)
        w2p[h] = dot(spread_two, w2[h, 1]).astype(bf)
    for h in range(4):
        p, q = h ^ 2, h ^ 1
        v = dot(x[h], w1[h, 0]) + dot(x[p], w1p[h])
        up = dot(c[h], w2[h, 0], NT) + dot(c[q], w2p[q], NT)
        v2 = v * v
        t = jnp.tanh(root * v * (1.0 + 0.044715 * v2))
        half = 0.5 + 0.5 * t
        act[h] = (v * half).astype(bf)
        slope = half + (0.5 * root) * v * (1.0 - t * t) * (1.0 + (3 * 0.044715) * v2)
        pre[h] = (up * slope).astype(bf)
    for h in range(4):
        p, q = h ^ 2, h ^ 1
        ig[h] = (dot(pre[h], w1[h, 0], NT) + dot(pre[p], w1p[p], NT)).astype(bf)
        gf[h, 0] = (dot(x[h], pre[h], TN) * scale).astype(bf)
        cross = (dot(x[p], pre[h], TN) * scale).astype(bf)
        gf[h, 1] = dot(spread_one, cross, TN).astype(bf)
        gs[h, 0] = (dot(act[h], c[h], TN) * scale).astype(bf)
        cross = (dot(act[q], c[h], TN) * scale).astype(bf)
        gs[h, 1] = dot(spread_two, cross, TN).astype(bf)


def shards(plan, inputs, cotangent, first_weight, second_weight, orders):
    tok, width = inputs.shape
    rows = first_weight.shape[2]
    bf = jnp.bfloat16
    all_tok = plan.g * tok
    nq = plan.nq
    scale = 1.0 / math.sqrt(tok * plan.dp)
    dma = pltpu.SemaphoreType.DMA
    n_t, n_w = 4 * plan.g, 4 * plan.dp
    toks = pltpu.VMEM((nq, 4, all_tok, B), bf)
    mats = pltpu.VMEM((nq, 4, 2, B, B), bf)
    part = jax.ShapeDtypeStruct((plan.groups, plan.nb, 2, rows, B), bf)
    input_grad, first, second = pl.pallas_call(
        functools.partial(whole, plan, scale),
        out_shape=(jax.ShapeDtypeStruct((tok, width), bf), part, part),
        in_specs=[pl.BlockSpec(memory_space=pltpu.VMEM)] + [ANY] * 4,
        out_specs=(ANY,) * 3,
        scratch_shapes=[toks, toks, mats, mats, toks, mats, mats]
        + [pltpu.VMEM((4, B, B), bf)] * 2
        + [pltpu.VMEM((4, all_tok, B), bf)] * 2
        + [dma((nq, 2, n_t)), dma((nq, 2, n_t)), dma((nq, 2, n_w)), dma((nq, 2, n_w)), dma((nq, 4))]
        + [dma((nq, n_t)), dma((nq, n_t)), dma((nq, 2, n_w)), dma((nq, 2, n_w)), dma((nq, 3))],
        compiler_params=pltpu.CompilerParams(
            collective_id=0, has_side_effects=True, vmem_limit_bytes=56 * 2**20
        ),
        name="whole",
    )(orders, inputs, cotangent, first_weight, second_weight)
    total = lambda parts: jnp.sum(parts.astype(jnp.float32), axis=0)
    return input_grad, total(first), total(second)


def solution(mesh):
    in_specs = (
        P("dp", "mp"),
        P("dp", "mp"),
        P("mp", None, "dp", None),
        P("mp", None, "dp", None),
        P(),
    )
    out_specs = (P("dp", "mp"), P("mp", None, "dp", None), P("mp", None, "dp", None))

    def body(inputs, *rest):
        sizes = mesh.shape["dp"], mesh.shape["mp"], inputs.shape[1] // B
        plan = Lanes(*sizes)
        if plan.fits:
            return by_lanes(plan, inputs, *rest)
        plan = Plan(*sizes)
        return shards(plan, inputs, *rest)

    return jax.shard_map(body, mesh=mesh, in_specs=in_specs, out_specs=out_specs, check_vma=False)
```
